32 devices in a mesh: leaf: 8 (over z, y), sub: 4 (over x, core).
Axes of the slice: x: 2, y: 2, z: 4, core: 2. Of those that a mesh axis runs over, the one named last changes fastest.
Arguments:
- points: float32 [3, 131072], P(None, ('leaf', 'sub')), may hold values from 0 to 256, as said below
- vectors: float32 [32, 131072], P(None, ('leaf', 'sub')), may hold values from -6 to 6
- counts: int32 [256, 8], P(('leaf', 'sub')), may hold values from 1 to 64, 384 in all within a row
Outputs:
- product: float32 [32, 131072], P(None, ('leaf', 'sub'))
The draws below stay inside these ranges and needn't reach their ends.
Inputs may be any that keep to these rules, and one draw needn't show every extreme that they name: `points`: rows 0, 1, 2 are x, y, z. The slots of leaf l = 8 s + 4 cz + 2 cy + cx lie in its cell: x in [cx / 2, (cx + 1) / 2], y in [cy / 2, (cy + 1) / 2], z in [s + cz / 2, s + (cz + 1) / 2]. Leaf 8 s + c holds its points in its first counts[s, c] slots; later slots are empty. Each row sums to 384 and holds 64 at least once.
All inputs are finite; a program needn't handle non-finite values.
Results may differ from the reference program's by a relative error of at most 0.0003.
Values sent between devices are 32-bit elements; how exact they have to be, the bound alone decides.
A program may use at most 128 MiB of HBM per device.

```python
import math
import jax
import jax.numpy as jnp
import numpy as np
from jax import lax

LEAF_PTS = 64
ORDER = 4
RANK = 64
VECS = 32
NSLAB = 256
LEVELS = 7
NPTS = 131072


def draw_points(key, part):
    leaf_count = NPTS // LEAF_PTS
    samples = jax.random.uniform(key, (3, leaf_count, LEAF_PTS), jnp.float32)
    leaves = jnp.arange(leaf_count)
    slab_index = (leaves // 8).astype(jnp.float32)
    depth_index = (leaves // 4 % 2).astype(jnp.float32)
    row_index = (leaves // 2 % 2).astype(jnp.float32)
    column_index = (leaves % 2).astype(jnp.float32)
    abscissa = (column_index[:, None] + samples[0]) * 0.5
    ordinate = (row_index[:, None] + samples[1]) * 0.5
    altitude = slab_index[:, None] + (depth_index[:, None] + samples[2]) * 0.5
    return jnp.stack([abscissa, ordinate, altitude]).reshape(3, NPTS)


def levels(stream_key, shape, pieces, low, largest):
    level = 1.0
    for dim, blocks in pieces:
        steps = jax.random.uniform(jax.random.fold_in(jax.random.fold_in(stream_key, 6), dim), (blocks,), jnp.float32, low / len(pieces), largest / len(pieces))
        level = level * jnp.repeat(jnp.exp(steps), shape[dim] // blocks).reshape((-1,) + (1,) * (len(shape) - 1 - dim))
    return level


def split_up(amount, total, bound, slope):
    loads = [(1 << 20) // math.isqrt(rank ** slope) + 1 for rank in range(2, amount + 1)]
    surplus, given = total - bound - (amount - 1), [1] * (amount - 1)
    while surplus > 0:
        candidates = [i for i in range(amount - 1) if given[i] < bound]
        mass, left = sum([loads[i] for i in candidates]), surplus
        for i in candidates:
            more = min(bound - given[i], max(1, left * loads[i] // mass), surplus)
            given[i] = given[i] + more
            surplus = surplus - more
    return np.array([bound] + given)


def ragged_sizes(stream_key, amount, total, bound, lean):
    if amount == 2:
        one = jax.random.randint(stream_key, (), max(1, total - bound), min(bound, total - 1) + 1)
        return jnp.stack([one, total - one])
    tallies = jnp.asarray(split_up(amount, total, bound, lean), jnp.int32)
    couples = (amount - 1) // 2
    source_of, receiver = tallies[1:1 + 2 * couples:2], tallies[2:2 + 2 * couples:2]
    room = jnp.minimum(source_of - 1, bound - receiver)
    passed = jax.random.randint(jax.random.fold_in(stream_key, 1), (couples,), 0, 1 << 20) % (room + 1)
    tallies = tallies.at[1:1 + 2 * couples:2].set(source_of - passed).at[2:2 + 2 * couples:2].set(receiver + passed)
    return tallies[jax.random.permutation(jax.random.fold_in(stream_key, 2), amount)]


def gaussian(rng, dims, width, bound, pieces=(), kind=jnp.bfloat16):
    gain = levels(rng, dims, pieces, -0.22, 0.18) if pieces else 1.0
    entries = jax.random.normal(rng, dims, jnp.float32) * width * gain
    return jnp.minimum(jnp.maximum(entries, -bound), bound).astype(kind)


def setup_inputs(seed: int = 0) -> dict:
    key_list = jax.random.split(jax.random.key(seed), 4)
    points = draw_points(jax.random.fold_in(key_list[3], 71), 0)
    vectors = gaussian(key_list[1], (VECS, NPTS), 1.0, 6.0, ((1, 32),), jnp.float32)
    counts = jax.vmap(lambda own: ragged_sizes(own, 8, 6 * LEAF_PTS, LEAF_PTS, 2))(jax.random.split(key_list[2], NSLAB)).reshape((NSLAB, 8)).astype(jnp.int32)
    return dict(points=points, vectors=vectors, counts=counts)


TERM_SCALE = 1.0 / 32.0
ROOT_THREE = math.sqrt(3.0)
far_offsets = (-3, -2, 2, 3)
far_sources = ((0, (0, 4, 5)), (1, (0, 1, 5)))
slab_group = 16

def term_lengths(slab_count):
    term_count = (slab_count.bit_length() - 1) // 3 + 1
    return [slab_count / 4.0 / 8.0 ** term_index for term_index in range(term_count)]

def chebyshev(order):
    return np.cos((2.0 * np.arange(order) + 1.0) * np.pi / (2.0 * order))

def lagrange_table(values, node_values):
    columns = []
    for anchor in range(len(node_values)):
        product = values * 0.0 + 1.0
        for against in range(len(node_values)):
            if against != anchor:
                product = product * (values - node_values[against]) / (node_values[anchor] - node_values[against])
        columns.append(product)
    return np.stack(columns, -1)

def lagrange_values(values, node_values):
    columns = []
    for anchor in range(len(node_values)):
        product = jnp.ones_like(values)
        for against in range(len(node_values)):
            if against != anchor:
                factor = 1.0 / float(node_values[anchor] - node_values[against])
                product = product * ((values - float(node_values[against])) * factor)
        columns.append(product)
    return jnp.stack(columns, -1)

def grid_nodes(node_values):
    number = len(node_values)
    along_z, along_y, along_x = np.meshgrid(np.arange(number), np.arange(number), np.arange(number), indexing='ij')
    return np.stack([node_values[along_x.ravel()], node_values[along_y.ravel()], node_values[along_z.ravel()]], -1)

def kernel_table(targets, sources, lengths):
    offsets_xyz = targets[:, None, :] - sources[None, :, :]
    distance = np.sqrt(np.sum(offsets_xyz * offsets_xyz, -1))
    summed_terms = distance * 0.0
    for length in lengths:
        scaled = distance * (ROOT_THREE / length)
        summed_terms = summed_terms + TERM_SCALE / math.sqrt(length) * (1.0 + scaled) * np.exp(-scaled)
    return summed_terms

def kernel_values(squared, lengths):
    distance = jnp.sqrt(squared)
    summed_terms = jnp.zeros_like(distance)
    for length in lengths:
        scaled = distance * (ROOT_THREE / length)
        summed_terms = summed_terms + TERM_SCALE / math.sqrt(length) * (1.0 + scaled) * jnp.exp(-scaled)
    return summed_terms

def child_tables(node_values):
    halves = [lagrange_table(side_offset + 0.5 * node_values, node_values) for side_offset in (-0.5, 0.5)]
    identity = np.eye(len(node_values))
    octant_rows = []
    for depth_index in range(2):
        for row_index in range(2):
            for column_index in range(2):
                octant_rows.append(np.kron(np.kron(halves[depth_index], halves[row_index]), halves[column_index]))
    octant_array = np.stack(octant_rows).reshape((2, 2, 2) + octant_rows[0].shape)
    half_array = np.stack([np.kron(np.kron(halves[half_index], identity), identity) for half_index in range(2)])
    return (octant_array, half_array)

def leaf_coupling(node_values, depth_index, layer_index, lengths):
    scaled = grid_nodes(node_values) * 0.25
    targets = []
    sources = []
    for row_index in range(2):
        for column_index in range(2):
            targets.append(scaled + np.array([(column_index + 0.5) * 0.5, (row_index + 0.5) * 0.5, (depth_index + 0.5) * 0.5]))
            sources.append(scaled + np.array([(column_index + 0.5) * 0.5, (row_index + 0.5) * 0.5, (layer_index - 1.5) * 0.5]))
    return kernel_table(np.concatenate(targets), np.concatenate(sources), lengths)

def coarse_couplings(node_values, height, lengths):
    span = float(1 << height)
    targets = grid_nodes(node_values) * np.array([0.5, 0.5, 0.5 * span])
    return np.stack([kernel_table(targets, targets + np.array([0.0, 0.0, offset * span]), lengths) for offset in far_offsets])

def basis_of(coords, first_slab, node_values):
    layer_ids = jnp.arange(coords.shape[1])
    slab_of = (first_slab + layer_ids // 2).astype(coords.dtype)
    depth_centre = ((layer_ids % 2).astype(coords.dtype) + 0.5) * 0.5
    centre = (jnp.arange(2).astype(coords.dtype) + 0.5) * 0.5
    along_width = (coords[0] - centre[None, None, :, None]) * 4.0
    along_height = (coords[1] - centre[None, :, None, None]) * 4.0
    along_depth = (coords[2] - slab_of[:, None, None, None] - depth_centre[:, None, None, None]) * 4.0
    poly_width = lagrange_values(along_width, node_values)
    poly_height = lagrange_values(along_height, node_values)
    poly_depth = lagrange_values(along_depth, node_values)
    combined = poly_depth[..., :, None, None] * poly_height[..., None, :, None] * poly_width[..., None, None, :]
    return combined.reshape(combined.shape[:4] + (-1,))

def near_field(window, targets, lengths):
    layer_count = targets.shape[1]
    padded = jnp.pad(window, ((0, 0), (0, 0), (1, 1), (1, 1), (0, 0)))
    summed = jnp.zeros((window.shape[0] - 3,) + targets.shape[1:], window.dtype)
    for step_depth in (-1, 0, 1):
        for step_height in (-1, 0, 1):
            for step_width in (-1, 0, 1):
                source = padded[:, 1 + step_depth:1 + step_depth + layer_count, 1 + step_height:3 + step_height, 1 + step_width:3 + step_width]
                squared = (targets[0][..., :, None] - source[0][..., None, :]) ** 2 + (targets[1][..., :, None] - source[1][..., None, :]) ** 2 + (targets[2][..., :, None] - source[2][..., None, :]) ** 2
                weights = kernel_values(squared, lengths)
                summed = summed + jnp.einsum('zyxij,vzyxj->vzyxi', weights, source[3:], precision=lax.Precision.HIGHEST)
    return summed

def leaf_far(window, node_values, lengths):
    pair_count = (window.shape[0] - 4) // 2
    rank_count = window.shape[3]
    vector_count = window.shape[4]
    stacked = []
    for depth_index, layer_list in far_sources:
        summed = jnp.zeros((pair_count, 4 * rank_count, vector_count), window.dtype)
        for layer_index in layer_list:
            coupling = jnp.asarray(leaf_coupling(node_values, depth_index, layer_index, lengths), jnp.float32)
            source = window[layer_index:layer_index + 2 * pair_count:2].reshape(pair_count, 4 * rank_count, vector_count)
            summed = summed + jnp.einsum('mn,jnv->jmv', coupling, source, precision=lax.Precision.HIGHEST)
        stacked.append(summed.reshape(pair_count, 2, 2, rank_count, vector_count))
    return jnp.stack(stacked, 1).reshape(2 * pair_count, 2, 2, rank_count, vector_count)

def reference(points, vectors, counts):
    lengths = term_lengths(NSLAB)
    node_values = chebyshev(ORDER)
    octant_array, half_array = child_tables(node_values)
    octants = jnp.asarray(octant_array, jnp.float32)
    half_tables = jnp.asarray(half_array, jnp.float32)
    layers = 2 * NSLAB
    coords = points.reshape(3, layers, 2, 2, LEAF_PTS)
    occupied = (jnp.arange(LEAF_PTS)[None, :] < counts.reshape(-1, 1)).astype(jnp.float32).reshape(layers, 2, 2, LEAF_PTS)
    masked = vectors.reshape(VECS, layers, 2, 2, LEAF_PTS) * occupied
    record = jnp.concatenate([coords, masked], 0)
    leaf_bases = basis_of(coords, 0, node_values)
    leaf_coeffs = jnp.einsum('zyxpr,vzyxp->zyxrv', leaf_bases, masked, precision=lax.Precision.HIGHEST)
    box_table = jnp.einsum('abcmn,sabcmv->snv', octants, leaf_coeffs.reshape(NSLAB, 2, 2, 2, RANK, VECS), precision=lax.Precision.HIGHEST)
    far_terms = []
    for height in range(LEVELS):
        box_count = box_table.shape[0]
        padded = jnp.pad(box_table, ((3, 3), (0, 0), (0, 0)))
        parity = (jnp.arange(box_count) % 2 == 0)[:, None, None]
        couplings = jnp.asarray(coarse_couplings(node_values, height, lengths), jnp.float32)
        summed = jnp.zeros_like(box_table)
        for position, offset in enumerate(far_offsets):
            source = padded[3 + offset:3 + offset + box_count]
            contribution = jnp.einsum('mn,inv->imv', couplings[position], source, precision=lax.Precision.HIGHEST)
            if offset == 3:
                contribution = jnp.where(parity, contribution, 0.0)
            if offset == -3:
                contribution = jnp.where(parity, 0.0, contribution)
            summed = summed + contribution
        far_terms.append(summed)
        if height + 1 < LEVELS:
            paired = box_table.reshape(box_count // 2, 2, RANK, VECS)
            box_table = jnp.einsum('cmn,icmv->inv', half_tables, paired, precision=lax.Precision.HIGHEST)
    local_exp = far_terms[LEVELS - 1]
    for height in range(LEVELS - 2, -1, -1):
        children = jnp.einsum('cmn,inv->icmv', half_tables, local_exp, precision=lax.Precision.HIGHEST)
        local_exp = far_terms[height] + children.reshape(-1, RANK, VECS)
    inherited = jnp.einsum('abcmn,snv->sabcmv', octants, local_exp, precision=lax.Precision.HIGHEST).reshape(layers, 2, 2, RANK, VECS)
    coeff_padded = jnp.pad(leaf_coeffs, ((2, 2), (0, 0), (0, 0), (0, 0), (0, 0)))
    record_padded = jnp.pad(record, ((0, 0), (1, 1), (0, 0), (0, 0), (0, 0)))

    def per_group(group_index):
        first_layer = (2 * slab_group * group_index).astype(jnp.int32)
        coeff_window = lax.dynamic_slice_in_dim(coeff_padded, first_layer, 2 * slab_group + 4, 0)
        near_window = lax.dynamic_slice_in_dim(record_padded, first_layer, 2 * slab_group + 2, 1)
        targets = lax.dynamic_slice_in_dim(coords, first_layer, 2 * slab_group, 1)
        return (leaf_far(coeff_window, node_values, lengths), near_field(near_window, targets, lengths))
    far_leaves, near_terms = lax.map(per_group, jnp.arange(NSLAB // slab_group).astype(jnp.int32))
    leaf_local = inherited + far_leaves.reshape(layers, 2, 2, RANK, VECS)
    near_term = jnp.transpose(near_terms, (1, 0, 2, 3, 4, 5)).reshape(VECS, layers, 2, 2, LEAF_PTS)
    result = jnp.einsum('zyxpr,zyxrv->vzyxp', leaf_bases, leaf_local, precision=lax.Precision.HIGHEST) + near_term
    return (result * occupied).reshape(VECS, -1)
```

```python
import functools
import math

import jax
import jax.numpy as jnp
import numpy as np
from jax import lax
from jax.experimental import pallas as pl
from jax.experimental.pallas import tpu as pltpu
from jax.sharding import PartitionSpec as P

ORDER = 4


TERM_SCALE = 1.0 / 32.0
ROOT_THREE = math.sqrt(3.0)
far_offsets = (-3, -2, 2, 3)
far_sources = ((0, (0, 4, 5)), (1, (0, 1, 5)))


def term_lengths(slab_count):
    term_count = (slab_count.bit_length() - 1) // 3 + 1
    return [slab_count / 4.0 / 8.0**term_index for term_index in range(term_count)]


def chebyshev(order):
    return np.cos((2.0 * np.arange(order) + 1.0) * np.pi / (2.0 * order))


def lagrange_table(values, node_values):
    columns = []
    for anchor in range(len(node_values)):
        product = values * 0.0 + 1.0
        for against in range(len(node_values)):
            if against != anchor:
                product = (
                    product
                    * (values - node_values[against])
                    / (node_values[anchor] - node_values[against])
                )
        columns.append(product)
    return np.stack(columns, -1)


def grid_nodes(node_values):
    number = len(node_values)
    along_z, along_y, along_x = np.meshgrid(
        np.arange(number), np.arange(number), np.arange(number), indexing="ij"
    )
    return np.stack(
        [node_values[along_x.ravel()], node_values[along_y.ravel()], node_values[along_z.ravel()]],
        -1,
    )


def kernel_table(targets, sources, lengths):
    offsets_xyz = targets[:, None, :] - sources[None, :, :]
    distance = np.sqrt(np.sum(offsets_xyz * offsets_xyz, -1))
    summed_terms = distance * 0.0
    for length in lengths:
        scaled = distance * (ROOT_THREE / length)
        summed_terms = summed_terms + TERM_SCALE / math.sqrt(length) * (1.0 + scaled) * np.exp(
            -scaled
        )
    return summed_terms


def child_tables(node_values):
    halves = [
        lagrange_table(side_offset + 0.5 * node_values, node_values) for side_offset in (-0.5, 0.5)
    ]
    identity = np.eye(len(node_values))
    octant_rows = []
    for depth_index in range(2):
        for row_index in range(2):
            for column_index in range(2):
                octant_rows.append(
                    np.kron(np.kron(halves[depth_index], halves[row_index]), halves[column_index])
                )
    octant_array = np.stack(octant_rows).reshape((2, 2, 2) + octant_rows[0].shape)
    half_array = np.stack(
        [np.kron(np.kron(halves[half_index], identity), identity) for half_index in range(2)]
    )
    return (octant_array, half_array)


def leaf_coupling(node_values, depth_index, layer_index, lengths):
    scaled = grid_nodes(node_values) * 0.25
    targets = []
    sources = []
    for row_index in range(2):
        for column_index in range(2):
            targets.append(
                scaled
                + np.array(
                    [(column_index + 0.5) * 0.5, (row_index + 0.5) * 0.5, (depth_index + 0.5) * 0.5]
                )
            )
            sources.append(
                scaled
                + np.array(
                    [(column_index + 0.5) * 0.5, (row_index + 0.5) * 0.5, (layer_index - 1.5) * 0.5]
                )
            )
    return kernel_table(np.concatenate(targets), np.concatenate(sources), lengths)


def coarse_couplings(node_values, height, lengths):
    span = float(1 << height)
    targets = grid_nodes(node_values) * np.array([0.5, 0.5, 0.5 * span])
    return np.stack(
        [
            kernel_table(targets, targets + np.array([0.0, 0.0, offset * span]), lengths)
            for offset in far_offsets
        ]
    )


def halves_bf16(value):
    high = value.astype(jnp.bfloat16)
    low = (value - high.astype(jnp.float32)).astype(jnp.bfloat16)
    return high, low


def np_halves(table):
    table = np.asarray(table, np.float32)
    high = table.astype(jnp.bfloat16)
    low = (table - high.astype(np.float32)).astype(jnp.bfloat16)
    return np.stack([high, low])


def dot_split(first, second, high, low):
    return jnp.dot(
        jnp.concatenate([first, second, first], 1), jnp.concatenate([high, high, low], 0),
        preferred_element_type=jnp.float32,
    )


def dot3(value, high, low):
    return dot_split(*halves_bf16(value), high, low)


def smooth_split(lengths):
    r = np.linspace(0.0, math.sqrt(3.0) * 1.0005, 2001)
    s = r * r

    def term(length):
        a = r * (ROOT_THREE / length)
        return TERM_SCALE / math.sqrt(length) * (1.0 + a) * np.exp(-a)

    smooth = sum(term(length) for length in lengths[:-1])
    basis = np.stack([np.ones_like(r), s, s * r, s * s], 1)
    weight = np.ones_like(r)
    for _ in range(100):
        root = np.sqrt(weight)
        fitted = np.linalg.lstsq(basis * root[:, None], smooth * root, rcond=None)[0]
        error = np.abs(smooth - basis @ fitted)
        weight = weight * (error / error.max() + 1e-3)
        weight = weight / weight.mean()
    full = smooth + term(lengths[-1])
    low = basis[:, :2]
    c0, c1 = np.linalg.lstsq(low / full[:, None], np.ones_like(r), rcond=None)[0]
    return (float(c0), float(c1)), [float(v) for v in fitted - np.array([c0, c1, 0.0, 0.0])]


def moment_tables(node_values, c0, c1):
    nodes = grid_nodes(node_values) * 0.25
    layer_nodes = []
    for row_index in range(2):
        for column_index in range(2):
            layer_nodes.append(nodes + np.array([0.5 * column_index - 0.25, 0.5 * row_index - 0.25, 0.0]))
    x, y, d = np.concatenate(layer_nodes).T
    norm = x * x + y * y + d * d
    one = np.ones_like(x)
    gather = np.zeros((len(x), 128))
    spread = np.zeros((128, len(x)))
    for group, step in enumerate((-1.0, 0.0, 1.0)):
        source = (
            c0 + c1 * (norm + step * step / 4.0 + step * d), -2.0 * c1 * x, -2.0 * c1 * y,
            -c1 * (2.0 * d + step), c1 * one,
        )
        for index, (column, row) in enumerate(zip(source, (one, x, y, d, norm))):
            gather[:, 8 * group + index] = column
            spread[8 * group + index] = row
    return gather, spread


def poly_table(node_values):
    number = len(node_values)
    rows = number * number
    table = np.zeros((2, number, 2, rows, 128), np.float32)
    for row in range(rows):
        for which, anchor in enumerate((row % number, row // number)):
            for against in range(number):
                if against == anchor:
                    table[which, against, 1, row] = 1.0
                else:
                    factor = 1.0 / (node_values[anchor] - node_values[against])
                    table[which, against, 0, row] = factor
                    table[which, against, 1, row] = -node_values[against] * factor
    return table


def make_tables(node_values, level_count, lengths):
    octants, halves = child_tables(node_values)
    rank = ORDER**3
    eight = octants.reshape(8, rank, rank)
    leaf_up = np.zeros((2, 8, rank, 2, rank))
    for parity in range(2):
        leaf_up[parity, :, :, parity, :] = eight
    leaf_up = leaf_up.reshape(16 * rank, 2 * rank)
    leaf_down = leaf_up.T
    box_up = np.zeros((2, 2, rank, 2, rank))
    for parity in range(2):
        box_up[parity, :, :, parity, :] = halves
    box_up = box_up.reshape(2, 2 * rank, 2 * rank)
    box_down = np.swapaxes(box_up, 1, 2)
    far = np.zeros((level_count, 2, 2, rank, 2, rank))
    for height in range(level_count):
        m3, m2, p2, p3 = [c.T for c in coarse_couplings(node_values, height, lengths)]
        far[height, 0, 0, :, 0] = m2
        far[height, 0, 0, :, 1] = m3
        far[height, 0, 1, :, 1] = m2
        far[height, 1, 0, :, 0] = p2
        far[height, 1, 1, :, 0] = p3
        far[height, 1, 1, :, 1] = p2
    far = far.reshape(level_count, 2, 2 * rank, 2 * rank)
    leaf_far = np.stack(
        [
            np.concatenate(
                [leaf_coupling(node_values, depth, layer, lengths).T for layer in layers]
            )
            for depth, layers in far_sources
        ]
    )
    return leaf_up, leaf_down, box_up, box_down, far, leaf_far


def kernel_body(
    dims, lengths, pieces, pts, vec, cnt, poly, leaf_up, box_up, down_hbm, box_down, far_hbm,
    leaf_far_hbm, moment_in, moment_out,
    out, mw, pw, bd, lc, lh, ls, r2s, kn, acc, send, recv, gsend, gath, low_pairs, ups, locs, ll,
    leaf_down, far, leaf_far, send_sems, recv_sems, gsend_sems, grecv_sems, table_sems,
):
    nleaf, nsub, cubes, levels = dims
    n = nleaf * nsub
    layers = 2 * cubes
    cube_levels = cubes.bit_length() - 1
    nodes = chebyshev(ORDER)
    me = lax.axis_index("leaf") * nsub + lax.axis_index("sub")
    mesh_id = pl.DeviceIdType.MESH

    def place(d):
        return (d // nsub, lax.rem(d, nsub))

    barrier = pltpu.get_barrier_semaphore()

    def greet(k, carry):
        pl.semaphore_signal(
            barrier, inc=1, device_id=place(lax.rem(me + k, n)), device_id_type=mesh_id
        )
        return carry

    lax.fori_loop(1, n, greet, 0)
    table_copies = [
        pltpu.make_async_copy(down_hbm, leaf_down, table_sems.at[0]),
        pltpu.make_async_copy(far_hbm, far, table_sems.at[1]),
        pltpu.make_async_copy(leaf_far_hbm, leaf_far, table_sems.at[2]),
    ]
    for copy in table_copies:
        copy.start()

    first_slab = (me * cubes).astype(jnp.float32)
    lane = lax.broadcasted_iota(jnp.int32, (1, 256), 1)
    quarter = lane // 64
    slot = lane - quarter * 64
    centre_x = ((quarter % 2).astype(jnp.float32) + 0.5) * 0.5
    centre_y = ((quarter // 2).astype(jnp.float32) + 0.5) * 0.5
    row8 = lax.broadcasted_iota(jnp.int32, (8, 512), 0)

    def span(z, width=256):
        return pl.ds(pl.multiple_of(z * 256, 256), width)

    def occupancy(z):
        cube, base = z // 2, lax.rem(z, 2) * 4
        limit = jnp.where(
            quarter < 2,
            jnp.where(quarter == 0, cnt[cube, base], cnt[cube, base + 1]),
            jnp.where(quarter == 2, cnt[cube, base + 2], cnt[cube, base + 3]),
        )
        return jnp.where(slot < limit, 1.0, 0.0)

    def poly_of(u, which, rows):
        product = None
        for against in range(ORDER):
            a = poly[which, against, 0, :rows]
            b = poly[which, against, 1, :rows]
            a = jnp.concatenate([a, a], 1)
            b = jnp.concatenate([b, b], 1)
            factor = u * a + b
            product = factor if product is None else product * factor
        return product

    nt = (((1,), (1,)), ((), ()))
    nothing = jnp.zeros((64, 128), jnp.bfloat16)

    def up_layer(z, carry):
        masked = vec[:, span(z)] * occupancy(z)
        mh, ml = halves_bf16(masked)
        mw[:, span(z + 1)] = mh
        coords = pts[:, span(z)]
        pw[0:3, span(z + 1)] = coords
        depth = (lax.rem(z, 2).astype(jnp.float32) + 0.5) * 0.5
        slab = first_slab + (z // 2).astype(jnp.float32)
        ux = (coords[0:1] - centre_x) * 4.0
        uy = (coords[1:2] - centre_y) * 4.0
        uz = ((coords[2:3] - slab) - depth) * 4.0
        plane = poly_of(ux, 0, 16) * poly_of(uy, 1, 16)
        height = poly_of(uz, 0, 8)
        basis = jnp.concatenate([plane * height[a : a + 1] for a in range(ORDER)], 0)
        high = basis.astype(jnp.bfloat16).astype(jnp.float32)
        low = basis - high
        for leaf in range(4):
            start = leaf // 2 * 128
            mine = (quarter == leaf)[:, start : start + 128]
            for which, part in ((0, high), (1, low)):
                own = jnp.where(mine, part[:, start : start + 128], 0.0).astype(jnp.bfloat16)
                both = [own, nothing] if leaf < 2 else [nothing, own]
                bd[which, z, leaf * 64 : leaf * 64 + 64] = jnp.concatenate(both, 1)
        both = lax.dot_general(
            jnp.concatenate([mh, ml], 0), bd[0, z], nt, preferred_element_type=jnp.float32
        )
        rest = lax.dot_general(mh, bd[1, z], nt, preferred_element_type=jnp.float32)
        coeffs = both[0:32] + both[32:64] + rest
        lc[z + 2] = coeffs
        lh[z + 2], ls[z + 2] = halves_bf16(coeffs)
        return carry

    lax.fori_loop(0, layers, up_layer, 0, unroll=2)

    pairs = cubes // 2
    lane128 = lax.broadcasted_iota(jnp.int32, (16, 128), 1)
    offsets = []
    base = 128 + 32 * cube_levels

    def rise():
        flat = []
        for part in (lh, ls):
            own = part[2 : 2 + layers].reshape(pairs, 4, 32, 256)
            flat.append(jnp.concatenate([own[:, i].reshape(pairs * 32, 256) for i in range(4)], 1))
        level = dot_split(*flat, leaf_up[0], leaf_up[1]).reshape(pairs, 32, 128)
        yield
        offset = 0
        for height in range(cube_levels):
            offsets.append(offset)
            count = pairs >> height
            low_pairs[offset + 1 : offset + 1 + count] = level
            send[0, 128 + 32 * height : 160 + 32 * height] = level[0]
            send[1, 128 + 32 * height : 160 + 32 * height] = level[count - 1]
            offset += count + 2
            if count > 1:
                two = level.reshape(count // 2, 2, 32, 128)
                level = dot3(
                    two[:, 0].reshape(count * 16, 128), box_up[0, 0], box_up[1, 0]
                ) + dot3(two[:, 1].reshape(count * 16, 128), box_up[0, 1], box_up[1, 1])
                level = level.reshape(count // 2, 32, 128)
                yield
        box = dot3(level[0], box_up[0, 0], box_up[1, 0])
        folded = jnp.where(lane128 < 64, box[0:16], pltpu.roll(box[16:32], 64, 1))
        gsend[...] = folded
        gath[me] = folded
        yield
        for side, edge in ((0, 0), (1, layers - 1)):
            masked = vec[:, edge * 256 : edge * 256 + 256] * occupancy(jnp.int32(edge))
            coords = pts[:, edge * 256 : edge * 256 + 256]
            for half in range(2):
                cols = slice(half * 128, half * 128 + 128)
                send[side, base + 32 * half : base + 32 + 32 * half] = masked[:, cols]
                send[side, base + 64 + 8 * half : base + 67 + 8 * half] = coords[:, cols]
                for i in range(2):
                    source = lc[2 + i] if side == 0 else lc[layers + i]
                    start = (2 * i + half) * 32
                    send[side, start : start + 32] = source[:, cols]
        pad = jnp.zeros((5, 128), jnp.float32)
        for side in range(2):
            for half in range(2):
                send[side, base + 67 + 8 * half : base + 72 + 8 * half] = pad

    def near_squared(z, p, with_self=True):
        boundary = first_slab + (z + 1).astype(jnp.float32) * 0.5
        block = pw[:, span(z + 1, 512)]
        x = block[0:1] - 0.5
        y = block[1:2] - 0.5
        d = block[2:3] - boundary
        norm = x * x + y * y + d * d
        one = jnp.where(row8 == 4, 1.0, 0.0)
        right = jnp.where(row8 == 0, x, jnp.where(row8 == 1, y, jnp.where(row8 == 2, d,
            jnp.where(row8 == 3, norm, one))))
        swap = jnp.where(row8 == 3, 1.0, jnp.where(row8 == 4, norm, 0.0))
        left = jnp.where(row8 < 3, -2.0 * right, swap)[:, 0:256]

        def thirds(v):
            h = v.astype(jnp.bfloat16).astype(jnp.float32)
            m = (v - h).astype(jnp.bfloat16).astype(jnp.float32)
            return h, m, v - h - m

        rh, rm, rl = thirds(right)
        lh, lm, lo = thirds(left)
        if not with_self:
            rh, rm, rl = rh[:, 256:], rm[:, 256:], rl[:, 256:]
        rs = jnp.concatenate([rh, rm, rh, rl, rm, rh], 0).astype(jnp.bfloat16)
        ls = jnp.concatenate([lh, lh, lm, lh, lm, lo], 0).astype(jnp.bfloat16)
        r2s[p, :, (0 if with_self else 256) : 512] = lax.dot_general(
            ls, rs, (((0,), (0,)), ((), ())), preferred_element_type=jnp.float32
        )

    rate = ROOT_THREE / lengths[-1]
    weight = TERM_SCALE / math.sqrt(lengths[-1])
    d0, d1, q0, q1 = pieces

    def near_kernel(p, with_self=True, filler=None, every=4):
        for chunk in range(16):
            if filler is not None and chunk % every == 0:
                next(filler, None)
            rows = slice(chunk * 16, chunk * 16 + 16)
            c0 = (0 if chunk < 8 else 128) if with_self else 256
            sq = jnp.maximum(r2s[p, rows, c0:512], 1e-20)
            r = sq * lax.rsqrt(sq)
            decay = jnp.exp2(r * (-rate * math.log2(math.e)))
            rest = d0 + sq * (d1 + r * (q0 + r * q1))
            kn[p, rows, c0:512] = ((weight + (weight * rate) * r) * decay + rest).astype(jnp.bfloat16)

    first, second, whole = slice(0, 128), slice(128, 256), slice(0, 256)

    def plain(m, rows, cols, p):
        return jnp.dot(m, kn[p, rows, cols], preferred_element_type=jnp.float32)

    def turned(m, rows, cols, p):
        return lax.dot_general(m, kn[p, rows, cols], nt, preferred_element_type=jnp.float32)

    def near_apply(z, p):
        here = mw[:, span(z + 1)]
        there = mw[:, span(z + 2)]
        own = plain(here[:, first], first, whole, p)
        low = plain(here[:, second], second, second, p)
        high = turned(here[:, second], first, second, p)
        back = turned(there, whole, slice(256, 512), p)
        acc[:, span(z + 1)] += own + jnp.concatenate([high, low], 1) + back
        acc[:, span(z + 2)] = plain(here, whole, slice(256, 512), p)

    def near_step(z, p, filler=None, every=4):
        near_squared(z + 1, 1 - p)
        near_kernel(p, True, filler, every)
        near_apply(z - 1, 1 - p)

    def near_four(t, carry):
        for i in range(4):
            near_step(4 * t + (i + 1), (i + 1) % 2)
        return carry

    acc[:, 256:512] = jnp.zeros((32, 256), jnp.float32)
    late = layers // 4 - 1
    rising = rise()
    near_squared(jnp.int32(0), 0)
    next(rising)
    near_squared(jnp.int32(1), 1)
    near_kernel(0, True, rising, 5)
    for z in range(1, 5):
        near_step(jnp.int32(z), z % 2, rising, 5)
    for _ in rising:
        pass

    @pl.when(me == 0)
    def _():
        recv[0] = jnp.zeros(recv.shape[1:], jnp.float32)

    @pl.when(me == n - 1)
    def _():
        recv[1] = jnp.zeros(recv.shape[1:], jnp.float32)

    pl.semaphore_wait(barrier, n - 1)
    to_left = pltpu.make_async_remote_copy(
        send.at[0], recv.at[1], send_sems.at[0], recv_sems.at[1],
        device_id=place(lax.rem(me + n - 1, n)), device_id_type=mesh_id,
    )
    to_right = pltpu.make_async_remote_copy(
        send.at[1], recv.at[0], send_sems.at[1], recv_sems.at[0],
        device_id=place(lax.rem(me + 1, n)), device_id_type=mesh_id,
    )

    @pl.when(me > 0)
    def _():
        to_left.start()

    @pl.when(me < n - 1)
    def _():
        to_right.start()

    def spread(k, target):
        return pltpu.make_async_remote_copy(
            gsend, gath.at[me], gsend_sems.at[k], grecv_sems.at[me],
            device_id=place(target), device_id_type=mesh_id,
        )

    def spread_start(k, carry):
        spread(k, lax.rem(me + k, n)).start()
        return carry

    lax.fori_loop(1, n, spread_start, 0)

    lax.fori_loop(1, late, near_four, 0)

    @pl.when(me > 0)
    def _():
        to_right.wait_recv()

    @pl.when(me < n - 1)
    def _():
        to_left.wait_recv()

    for side, window in ((0, 0), (1, layers + 1)):
        for half in range(2):
            cols = slice(window * 256 + half * 128, window * 256 + half * 128 + 128)
            masked = recv[side, base + 32 * half : base + 32 + 32 * half]
            mw[:, cols] = masked.astype(jnp.bfloat16)
            pw[:, cols] = recv[side, base + 64 + 8 * half : base + 72 + 8 * half]
        for i in range(2):
            at = i if side == 0 else layers + 2 + i
            for half in range(2):
                start = (2 * i + half) * 32
                lanes = slice(half * 128, half * 128 + 128)
                lh[at, :, lanes], ls[at, :, lanes] = halves_bf16(recv[side, start : start + 32])
        for height in range(cube_levels):
            at = offsets[height] + (0 if side == 0 else (pairs >> height) + 1)
            low_pairs[at] = recv[side, 128 + 32 * height : 160 + 32 * height]
    low_far = []

    def leaves():
        spans = slice(1, layers + 3)
        rows = (layers + 2) * 32
        moments = dot_split(
            lh[spans].reshape(rows, 256), ls[spans].reshape(rows, 256), moment_in[0], moment_in[1]
        ).reshape(layers + 2, 32, 128)
        lane3 = lax.broadcasted_iota(jnp.int32, (layers, 32, 128), 2)
        joined = jnp.where(
            lane3 < 8, moments[0:layers],
            jnp.where(lane3 < 16, moments[1 : layers + 1], moments[2 : layers + 2]),
        )
        ll[...] = dot3(joined.reshape(layers * 32, 128), moment_out[0], moment_out[1]).reshape(
            layers, 32, 256
        )
        yield
        windows = [part[...].reshape(cubes + 2, 2, 32, 256) for part in (lh, ls)]
        for depth, sources in far_sources:
            gathered = [
                jnp.concatenate(
                    [w[s // 2 : s // 2 + cubes, s % 2].reshape(cubes * 32, 256) for s in sources], 1
                )
                for w in windows
            ]
            far_part = dot_split(*gathered, leaf_far[0, depth], leaf_far[1, depth])
            for j in range(cubes):
                ll[2 * j + depth] += far_part[32 * j : 32 * j + 32]
            yield
        for height in range(cube_levels):
            count = pairs >> height
            at = offsets[height]
            below = low_pairs[at : at + count].reshape(count * 32, 128)
            above = low_pairs[at + 2 : at + 2 + count].reshape(count * 32, 128)
            low_far.append(
                dot3(below, far[0, height, 0], far[1, height, 0])
                + dot3(above, far[0, height, 1], far[1, height, 1])
            )
            yield

    def descend():
        count = n // 2
        blank = jnp.zeros((32, 128), jnp.float32)
        offset = 0
        tops = []
        for height in range(cube_levels, levels):
            tops.append(offset)
            ups[offset] = blank
            ups[offset + count + 1] = blank
            if height == cube_levels:

                folds = gath[...].reshape(count, 2, 16, 128)
                even, odd = folds[:, 0], folds[:, 1]
                near_half = lax.broadcasted_iota(jnp.int32, even.shape, 2) < 64
                ups[1 : 1 + count, 0:16] = jnp.where(near_half, even, pltpu.roll(odd, 64, 2))
                ups[1 : 1 + count, 16:32] = jnp.where(near_half, pltpu.roll(even, 64, 2), odd)
            else:
                two = ups[tops[-2] + 1 : tops[-2] + 1 + 2 * count].reshape(count, 2, 32, 128)
                level = dot3(
                    two[:, 0].reshape(count * 32, 128), box_up[0, 0], box_up[1, 0]
                ) + dot3(two[:, 1].reshape(count * 32, 128), box_up[0, 1], box_up[1, 1])
                ups[offset + 1 : offset + 1 + count] = level.reshape(count, 32, 128)
            offset += count + 2
            count //= 2
            yield

        expansion = None
        for height in range(levels - 1, cube_levels - 1, -1):
            j = me >> (height - cube_levels + 1)
            at = tops[height - cube_levels]
            below, above = ups[at + j], ups[at + j + 2]
            here = dot3(below, far[0, height, 0], far[1, height, 0]) + dot3(
                above, far[0, height, 1], far[1, height, 1]
            )
            if expansion is not None:
                parity = lax.rem(j, 2)
                here = here + dot3(expansion, box_down[0, parity], box_down[1, parity])
            expansion = here
            yield
        for height in range(cube_levels - 1, -1, -1):
            count = pairs >> height
            here = low_far[height]
            if height == cube_levels - 1:
                parity = lax.rem(me, 2)
                expansion = here + dot3(expansion, box_down[0, parity], box_down[1, parity])
            else:
                lower = dot3(expansion, box_down[0, 0], box_down[1, 0]).reshape(count // 2, 1, 32, 128)
                upper = dot3(expansion, box_down[0, 1], box_down[1, 1]).reshape(count // 2, 1, 32, 128)
                expansion = here + jnp.concatenate([lower, upper], 1).reshape(count * 32, 128)
            yield
        yield
        inherited = dot3(expansion, leaf_down[0], leaf_down[1])
        for i in range(4):
            for j in range(pairs):
                ll[4 * j + i] += inherited[32 * j : 32 * j + 32, 256 * i : 256 * i + 256]

    for copy in table_copies:
        copy.wait()
    spreading = leaves()
    near_step(jnp.int32(layers - 3), 1, spreading, 4)
    for _ in spreading:
        pass

    def gather_wait(k, carry):
        source = lax.rem(me + n - k, n)
        pltpu.make_async_remote_copy(
            gsend, gath.at[source], gsend_sems.at[k], grecv_sems.at[source],
            device_id=place(source), device_id_type=mesh_id,
        ).wait_recv()
        return carry

    lax.fori_loop(1, n, gather_wait, 0)

    falling = descend()
    near_step(jnp.int32(layers - 2), 0, falling, 4)
    near_squared(jnp.int32(-1), 0, False)
    near_kernel(1, True, falling, 4)
    near_apply(jnp.int32(layers - 2), 0)
    near_kernel(0, False, falling, 4)
    near_apply(jnp.int32(layers - 1), 1)
    acc[:, 256:512] += plain(mw[:, 0:256], whole, slice(256, 512), 0)
    for _ in falling:
        pass

    def finish(z, carry):
        lh, lo = halves_bf16(ll[z])
        both = jnp.dot(
            jnp.concatenate([lh, lo], 0), bd[0, z], preferred_element_type=jnp.float32
        )
        rest = jnp.dot(lh, bd[1, z], preferred_element_type=jnp.float32)
        value = acc[:, span(z + 1)] + (both[0:32] + both[32:64] + rest)
        out[:, span(z)] = value * occupancy(z)
        return carry

    lax.fori_loop(0, layers, finish, 0, unroll=4)

    @pl.when(me > 0)
    def _():
        to_left.wait_send()

    @pl.when(me < n - 1)
    def _():
        to_right.wait_send()

    def send_wait(k, carry):
        spread(k, lax.rem(me + k, n)).wait_send()
        return carry

    lax.fori_loop(1, n, send_wait, 0)


def local(points, vectors, counts):
    cubes = counts.shape[0]
    nleaf, nsub = lax.axis_size("leaf"), lax.axis_size("sub")
    n = nleaf * nsub
    slab_count = cubes * n
    level_count = slab_count.bit_length() - 2
    cube_levels = cubes.bit_length() - 1
    lengths = term_lengths(slab_count)
    node_values = chebyshev(ORDER)
    leaf_up, leaf_down, box_up, box_down, far, leaf_far = [
        jnp.asarray(np_halves(t)) for t in make_tables(node_values, level_count, lengths)
    ]
    poly = jnp.asarray(poly_table(node_values))
    (c0, c1), pieces = smooth_split(lengths)
    moment_in, moment_out = [jnp.asarray(np_halves(t)) for t in moment_tables(node_values, c0, c1)]
    layers = 2 * cubes
    pairs = cubes // 2
    low_count = sum((pairs >> h) + 2 for h in range(cube_levels))
    top_count = sum((n // 2 >> h) + 2 for h in range(level_count - cube_levels))
    halo_rows = 128 + 32 * cube_levels + 80
    f32, bf16 = jnp.float32, jnp.bfloat16
    vmem = pl.BlockSpec(memory_space=pltpu.VMEM)
    anywhere = pl.BlockSpec(memory_space=pl.ANY)
    return pl.pallas_call(
        functools.partial(kernel_body, (nleaf, nsub, cubes, level_count), lengths, pieces),
        out_shape=jax.ShapeDtypeStruct(vectors.shape, f32),
        in_specs=[vmem, vmem, pl.BlockSpec(memory_space=pltpu.SMEM), vmem, vmem, vmem,
                  anywhere, vmem, anywhere, anywhere, vmem, vmem],
        out_specs=vmem,
        scratch_shapes=[
            pltpu.VMEM((32, (layers + 2) * 256), bf16),
            pltpu.VMEM((8, (layers + 2) * 256), f32),
            pltpu.VMEM((2, layers, 256, 256), bf16),
            pltpu.VMEM((layers + 4, 32, 256), f32),
            pltpu.VMEM((layers + 4, 32, 256), bf16),
            pltpu.VMEM((layers + 4, 32, 256), bf16),
            pltpu.VMEM((2, 256, 512), f32),
            pltpu.VMEM((2, 256, 512), bf16),
            pltpu.VMEM((32, (layers + 2) * 256), f32),
            pltpu.VMEM((2, halo_rows, 128), f32),
            pltpu.VMEM((2, halo_rows, 128), f32),
            pltpu.VMEM((16, 128), f32),
            pltpu.VMEM((n, 16, 128), f32),
            pltpu.VMEM((low_count, 32, 128), f32),
            pltpu.VMEM((top_count, 32, 128), f32),
            pltpu.VMEM((8, 128), f32),
            pltpu.VMEM((layers, 32, 256), f32),
            pltpu.VMEM(leaf_down.shape, bf16),
            pltpu.VMEM(far.shape, bf16),
            pltpu.VMEM(leaf_far.shape, bf16),
            pltpu.SemaphoreType.DMA((2,)),
            pltpu.SemaphoreType.DMA((2,)),
            pltpu.SemaphoreType.DMA((n,)),
            pltpu.SemaphoreType.DMA((n,)),
            pltpu.SemaphoreType.DMA((3,)),
        ],
        compiler_params=pltpu.CompilerParams(
            collective_id=0, has_side_effects=True, vmem_limit_bytes=60 * 1024 * 1024
        ),
    )(points, vectors, counts, poly, leaf_up, box_up, leaf_down, box_down, far, leaf_far,
      moment_in, moment_out)


def solution(mesh):
    in_specs = (P(None, ("leaf", "sub")), P(None, ("leaf", "sub")), P(("leaf", "sub"), None))
    out_specs = P(None, ("leaf", "sub"))
    return jax.shard_map(local, mesh=mesh, in_specs=in_specs, out_specs=out_specs, check_vma=False)
```

```python
import functools
import math

import jax
import jax.numpy as jnp
import numpy as np
from jax import lax
from jax.experimental import pallas as pl
from jax.experimental.pallas import tpu as pltpu
from jax.sharding import PartitionSpec as P

ORDER = 4
SOONER_HOPS = 1
VMEM_BYTES = 60 * 1024 * 1024


TERM_SCALE = 1.0 / 32.0
ROOT_THREE = math.sqrt(3.0)
far_offsets = (-3, -2, 2, 3)
far_sources = ((0, (0, 4, 5)), (1, (0, 1, 5)))


def term_lengths(slab_count):
    term_count = (slab_count.bit_length() - 1) // 3 + 1
    return [slab_count / 4.0 / 8.0**term_index for term_index in range(term_count)]


def chebyshev(order):
    return np.cos((2.0 * np.arange(order) + 1.0) * np.pi / (2.0 * order))


def lagrange_table(values, node_values):
    columns = []
    for anchor in range(len(node_values)):
        product = values * 0.0 + 1.0
        for against in range(len(node_values)):
            if against != anchor:
                product = (
                    product
                    * (values - node_values[against])
                    / (node_values[anchor] - node_values[against])
                )
        columns.append(product)
    return np.stack(columns, -1)


def grid_nodes(node_values):
    number = len(node_values)
    along_z, along_y, along_x = np.meshgrid(
        np.arange(number), np.arange(number), np.arange(number), indexing="ij"
    )
    return np.stack(
        [node_values[along_x.ravel()], node_values[along_y.ravel()], node_values[along_z.ravel()]],
        -1,
    )


def kernel_table(targets, sources, lengths):
    offsets_xyz = targets[:, None, :] - sources[None, :, :]
    distance = np.sqrt(np.sum(offsets_xyz * offsets_xyz, -1))
    summed_terms = distance * 0.0
    for length in lengths:
        scaled = distance * (ROOT_THREE / length)
        summed_terms = summed_terms + TERM_SCALE / math.sqrt(length) * (1.0 + scaled) * np.exp(
            -scaled
        )
    return summed_terms


def child_tables(node_values):
    halves = [
        lagrange_table(side_offset + 0.5 * node_values, node_values) for side_offset in (-0.5, 0.5)
    ]
    identity = np.eye(len(node_values))
    octant_rows = []
    for depth_index in range(2):
        for row_index in range(2):
            for column_index in range(2):
                octant_rows.append(
                    np.kron(np.kron(halves[depth_index], halves[row_index]), halves[column_index])
                )
    octant_array = np.stack(octant_rows).reshape((2, 2, 2) + octant_rows[0].shape)
    half_array = np.stack(
        [np.kron(np.kron(halves[half_index], identity), identity) for half_index in range(2)]
    )
    return (octant_array, half_array)


def leaf_coupling(node_values, depth_index, layer_index, lengths):
    scaled = grid_nodes(node_values) * 0.25
    targets = []
    sources = []
    for row_index in range(2):
        for column_index in range(2):
            targets.append(
                scaled
                + np.array(
                    [(column_index + 0.5) * 0.5, (row_index + 0.5) * 0.5, (depth_index + 0.5) * 0.5]
                )
            )
            sources.append(
                scaled
                + np.array(
                    [(column_index + 0.5) * 0.5, (row_index + 0.5) * 0.5, (layer_index - 1.5) * 0.5]
                )
            )
    return kernel_table(np.concatenate(targets), np.concatenate(sources), lengths)


def coarse_couplings(node_values, height, lengths):
    span = float(1 << height)
    targets = grid_nodes(node_values) * np.array([0.5, 0.5, 0.5 * span])
    return np.stack(
        [
            kernel_table(targets, targets + np.array([0.0, 0.0, offset * span]), lengths)
            for offset in far_offsets
        ]
    )


def halves_bf16(value):
    high = value.astype(jnp.bfloat16)
    low = (value - high.astype(jnp.float32)).astype(jnp.bfloat16)
    return high, low


def np_halves(table):
    table = np.asarray(table, np.float32)
    high = table.astype(jnp.bfloat16)
    low = (table - high.astype(np.float32)).astype(jnp.bfloat16)
    return np.stack([high, low])


def dot_split(first, second, high, low):
    return jnp.dot(
        jnp.concatenate([first, second, first], 1), jnp.concatenate([high, high, low], 0),
        preferred_element_type=jnp.float32,
    )


def dot3(value, high, low):
    return dot_split(*halves_bf16(value), high, low)


def smooth_split(lengths):
    r = np.linspace(0.0, math.sqrt(3.0) * 1.0005, 2001)
    s = r * r

    def term(length):
        a = r * (ROOT_THREE / length)
        return TERM_SCALE / math.sqrt(length) * (1.0 + a) * np.exp(-a)

    smooth = sum(term(length) for length in lengths[:-1])
    basis = np.stack([np.ones_like(r), s, s * r, s * s], 1)
    weight = np.ones_like(r)
    for _ in range(100):
        root = np.sqrt(weight)
        fitted = np.linalg.lstsq(basis * root[:, None], smooth * root, rcond=None)[0]
        error = np.abs(smooth - basis @ fitted)
        weight = weight * (error / error.max() + 1e-3)
        weight = weight / weight.mean()
    full = smooth + term(lengths[-1])
    low = basis[:, :2]
    c0, c1 = np.linalg.lstsq(low / full[:, None], np.ones_like(r), rcond=None)[0]
    return (float(c0), float(c1)), [float(v) for v in fitted - np.array([c0, c1, 0.0, 0.0])]


def moment_tables(node_values, c0, c1):
    nodes = grid_nodes(node_values) * 0.25
    layer_nodes = []
    for row_index in range(2):
        for column_index in range(2):
            layer_nodes.append(nodes + np.array([0.5 * column_index - 0.25, 0.5 * row_index - 0.25, 0.0]))
    x, y, d = np.concatenate(layer_nodes).T
    norm = x * x + y * y + d * d
    one = np.ones_like(x)
    gather = np.zeros((len(x), 128))
    spread = np.zeros((128, len(x)))
    for group, step in enumerate((-1.0, 0.0, 1.0)):
        source = (
            c0 + c1 * (norm + step * step / 4.0 + step * d), -2.0 * c1 * x, -2.0 * c1 * y,
            -c1 * (2.0 * d + step), c1 * one,
        )
        for index, (column, row) in enumerate(zip(source, (one, x, y, d, norm))):
            gather[:, 8 * group + index] = column
            spread[8 * group + index] = row
    return gather, spread


def lagrange_coefficients(node_values):
    rows = []
    for anchor in range(len(node_values)):
        others = np.delete(node_values, anchor)
        rows.append(np.poly(others)[::-1] / np.prod(node_values[anchor] - others))
    return np.stack(rows)


def make_tables(node_values, level_count, lengths):
    octants, halves = child_tables(node_values)
    rank = ORDER**3
    eight = octants.reshape(8, rank, rank)
    leaf_up = np.zeros((2, 8, rank, 2, rank))
    for parity in range(2):
        leaf_up[parity, :, :, parity, :] = eight
    leaf_up = leaf_up.reshape(16 * rank, 2 * rank)
    leaf_down = leaf_up.T
    box_up = np.zeros((2, 2, rank, 2, rank))
    for parity in range(2):
        box_up[parity, :, :, parity, :] = halves
    box_up = box_up.reshape(2, 2 * rank, 2 * rank)
    box_down = np.swapaxes(box_up, 1, 2)
    far = np.zeros((level_count, 2, 2, rank, 2, rank))
    for height in range(level_count):
        m3, m2, p2, p3 = [c.T for c in coarse_couplings(node_values, height, lengths)]
        far[height, 0, 0, :, 0] = m2
        far[height, 0, 0, :, 1] = m3
        far[height, 0, 1, :, 1] = m2
        far[height, 1, 0, :, 0] = p2
        far[height, 1, 1, :, 0] = p3
        far[height, 1, 1, :, 1] = p2
    far = far.reshape(level_count, 2, 2 * rank, 2 * rank)
    leaf_far = np.stack(
        [
            np.concatenate(
                [leaf_coupling(node_values, depth, layer, lengths).T for layer in layers]
            )
            for depth, layers in far_sources
        ]
    )
    return leaf_up, leaf_down, box_up, box_down, far, leaf_far


def kernel_body(
    dims, lengths, pieces, pts_hbm, vec_hbm, cnt, leaf_up_hbm, box_up_hbm, leaf_down_hbm,
    box_down_hbm, far_hbm, leaf_far_hbm, moment_in_hbm, moment_out_hbm,
    out, pts, vec, mw, pw, bd, b3, lh, ls, r2s, kn, acc, send, recv, send2, recv2, gsend, gath, crossed,
    low_pairs, ups, locs, ll, leaf_up, box_up, leaf_down, box_down, far, leaf_far, moment_in,
    moment_out, send_sems, recv_sems, gsend_sems, grecv_sems, swap_sems, table_sems,
):
    nleaf, nsub, cubes, levels = dims
    n = nleaf * nsub
    layers = 2 * cubes
    cube_levels = cubes.bit_length() - 1
    nodes = chebyshev(ORDER)
    me = lax.axis_index("leaf") * nsub + lax.axis_index("sub")
    mesh_id = pl.DeviceIdType.LOGICAL

    def place(d):
        return d

    copies = [
        pltpu.make_async_copy(source, target, table_sems.at[index])
        for index, (source, target) in enumerate((
            (pts_hbm, pts), (vec_hbm, vec), (leaf_up_hbm, leaf_up), (box_up_hbm, box_up),
            (moment_in_hbm, moment_in), (moment_out_hbm, moment_out), (leaf_far_hbm, leaf_far),
            (far_hbm, far), (box_down_hbm, box_down), (leaf_down_hbm, leaf_down),
        ))
    ]
    for copy in copies:
        copy.start()

    barrier = pltpu.get_barrier_semaphore()

    def greet(k, carry):
        pl.semaphore_signal(
            barrier, inc=1, device_id=place((me + k) & (n - 1)), device_id_type=mesh_id
        )
        return carry

    lax.fori_loop(1, n, greet, 0)

    first_slab = (me * cubes).astype(jnp.float32)
    lane = lax.broadcasted_iota(jnp.int32, (1, 256), 1)
    quarter = lane // 64
    slot = lane - quarter * 64
    centre_x = ((quarter % 2).astype(jnp.float32) + 0.5) * 0.5
    centre_y = ((quarter // 2).astype(jnp.float32) + 0.5) * 0.5
    row8 = lax.broadcasted_iota(jnp.int32, (8, 512), 0)

    def span(z, width=256):
        return pl.ds(pl.multiple_of(z * 256, 256), width)

    def occupancy(z):
        cube, base = z // 2, lax.rem(z, 2) * 4
        limit = jnp.where(
            quarter < 2,
            jnp.where(quarter == 0, cnt[cube, base], cnt[cube, base + 1]),
            jnp.where(quarter == 2, cnt[cube, base + 2], cnt[cube, base + 3]),
        )
        return jnp.where(slot < limit, 1.0, 0.0)

    table = lagrange_coefficients(nodes)
    row16 = lax.broadcasted_iota(jnp.int32, (16, 128), 0)

    def spread_rows(anchor):
        powers = []
        for power in range(ORDER):
            c = [float(v) for v in table[:, power]]
            one = jnp.where(
                anchor < 2, jnp.where(anchor == 0, c[0], c[1]), jnp.where(anchor == 2, c[2], c[3])
            )
            powers.append(jnp.concatenate([one, one], 1))
        return powers

    along_x = spread_rows(row16 % ORDER)
    along_y = spread_rows(row16 // ORDER)
    along_z = [c[0:8] for c in along_x]

    def poly_of(u, powers):
        p0, p1, p2, p3 = powers
        return ((p3 * u + p2) * u + p1) * u + p0

    def basis_of(ux, uy, uz):
        plane = poly_of(ux, along_x) * poly_of(uy, along_y)
        height = poly_of(uz, along_z)
        return halves_bf16(
            jnp.concatenate([plane * height[a : a + 1] for a in range(ORDER)], 0)
        )

    nt = (((1,), (1,)), ((), ()))
    left64 = lax.broadcasted_iota(jnp.int32, (64, 128), 1) < 64
    nothing = jnp.zeros((64, 128), jnp.bfloat16)

    def box_layer(z, carry):
        masked = vec[:, span(z)] * occupancy(z)
        mw[0:32, span(z + 1)], mw[32:64, span(z + 1)] = halves_bf16(masked)
        coords = pts[:, span(z)]
        pw[0:3, span(z + 1)] = coords
        b3[0:64, span(z)], b3[64:128, span(z)] = basis_of(
            coords[0:1] * 2.0 - 1.0, coords[1:2] * 2.0 - 1.0,
            (coords[2:3] - first_slab) * (2.0 / cubes) - 1.0,
        )
        return carry

    def leaf_layer(z, carry):
        coords = pts[:, span(z)]
        depth = (lax.rem(z, 2).astype(jnp.float32) + 0.5) * 0.5
        slab = first_slab + (z // 2).astype(jnp.float32)
        high, low = basis_of(
            (coords[0:1] - centre_x) * 4.0, (coords[1:2] - centre_y) * 4.0,
            ((coords[2:3] - slab) - depth) * 4.0,
        )
        for half in range(2):
            cols = slice(half * 128, half * 128 + 128)
            for which, part in ((0, high[:, cols]), (1, low[:, cols])):
                bd[which, z, half] = jnp.concatenate(
                    [jnp.where(left64, part, nothing), jnp.where(left64, nothing, part)], 0
                )
        return carry

    def couple():
        edge = [0, 1, layers - 2, layers - 1]
        for index, z in enumerate(edge + list(range(2, layers - 2))):
            for half in range(2):
                cols = slice(half * 128, half * 128 + 128)
                at = slice(256 * (z + 1) + half * 128, 256 * (z + 1) + half * 128 + 128)
                main = lax.dot_general(
                    mw[:, at], bd[0, z, half], nt, preferred_element_type=jnp.float32
                )
                rest = lax.dot_general(
                    mw[0:32, at], bd[1, z, half], nt, preferred_element_type=jnp.float32
                )
                coeffs = main[0:32] + main[32:64] + rest
                if z in edge:
                    side, i = (0, z) if z < 2 else (1, z - layers + 2)
                    start = (2 * i + half) * 32
                    send[side, start : start + 32] = coeffs
                lh[z + 2, :, cols], ls[z + 2, :, cols] = halves_bf16(coeffs)
            if index % 2:
                yield

    copies[0].wait()
    copies[1].wait()
    lax.fori_loop(0, layers, box_layer, 0, unroll=4)
    box = lax.dot_general(
        mw[:, 256 : 256 + layers * 256], b3[...], nt, preferred_element_type=jnp.float32
    )

    pairs = cubes // 2
    lane128 = lax.broadcasted_iota(jnp.int32, (16, 128), 1)
    offsets = []
    base = 128
    box = box[0:32] + box[32:64]
    box = box + pltpu.roll(box, 64, 1)
    core = lax.rem(me, 2)
    folded = [
        jnp.where(lane128[0:8] < 64, box[16 * k : 16 * k + 8], box[16 * k + 8 : 16 * k + 16])
        for k in range(2)
    ]
    gsend[0] = folded[0]
    gsend[1] = folded[1]
    gath[me] = jnp.where(core == 0, folded[0], folded[1])

    def rise():
        for copy in copies[2:4]:
            copy.wait()
        flat = []
        for part in (lh, ls):
            own = part[2 : 2 + layers].reshape(pairs, 4, 32, 256)
            flat.append(jnp.concatenate([own[:, i].reshape(pairs * 32, 256) for i in range(4)], 1))
        level = dot_split(*flat, leaf_up[0], leaf_up[1]).reshape(pairs, 32, 128)
        yield
        offset = 0
        for height in range(cube_levels):
            offsets.append(offset)
            count = pairs >> height
            low_pairs[offset + 1 : offset + 1 + count] = level
            send2[0, 32 * height : 32 * height + 32] = level[0]
            send2[1, 32 * height : 32 * height + 32] = level[count - 1]
            offset += count + 2
            if count > 1:
                two = level.reshape(count // 2, 2, 32, 128)
                level = dot3(
                    two[:, 0].reshape(count * 16, 128), box_up[0, 0], box_up[1, 0]
                ) + dot3(two[:, 1].reshape(count * 16, 128), box_up[0, 1], box_up[1, 1])
                level = level.reshape(count // 2, 32, 128)
                yield

    for side, edge in ((0, 0), (1, layers - 1)):
        masked = vec[:, edge * 256 : edge * 256 + 256] * occupancy(jnp.int32(edge))
        coords = pts[:, edge * 256 : edge * 256 + 256]
        for half in range(2):
            cols = slice(half * 128, half * 128 + 128)
            send[side, base + 32 * half : base + 32 + 32 * half] = masked[:, cols]
            send[side, base + 64 + 8 * half : base + 67 + 8 * half] = coords[:, cols]
    pad = jnp.zeros((5, 128), jnp.float32)
    for side in range(2):
        for half in range(2):
            send[side, base + 67 + 8 * half : base + 72 + 8 * half] = pad

    def near_squared(z, p, with_self=True):
        boundary = first_slab + (z + 1).astype(jnp.float32) * 0.5
        block = pw[:, span(z + 1, 512)]
        x = block[0:1] - 0.5
        y = block[1:2] - 0.5
        d = block[2:3] - boundary
        norm = x * x + y * y + d * d
        one = jnp.where(row8 == 4, 1.0, 0.0)
        right = jnp.where(row8 == 0, x, jnp.where(row8 == 1, y, jnp.where(row8 == 2, d,
            jnp.where(row8 == 3, norm, one))))
        swap = jnp.where(row8 == 3, 1.0, jnp.where(row8 == 4, norm, 0.0))
        left = jnp.where(row8 < 3, -2.0 * right, swap)[:, 0:256]

        def thirds(v):
            h = v.astype(jnp.bfloat16).astype(jnp.float32)
            m = (v - h).astype(jnp.bfloat16).astype(jnp.float32)
            return h, m, v - h - m

        rh, rm, rl = thirds(right)
        lh, lm, lo = thirds(left)
        if not with_self:
            rh, rm, rl = rh[:, 256:], rm[:, 256:], rl[:, 256:]
        rs = jnp.concatenate([rh, rm, rh, rl, rm, rh], 0).astype(jnp.bfloat16)
        ls = jnp.concatenate([lh, lh, lm, lh, lm, lo], 0).astype(jnp.bfloat16)
        r2s[p, :, (0 if with_self else 256) : 512] = lax.dot_general(
            ls, rs, (((0,), (0,)), ((), ())), preferred_element_type=jnp.float32
        )

    rate = ROOT_THREE / lengths[-1]
    weight = TERM_SCALE / math.sqrt(lengths[-1])
    d0, d1, q0, q1 = pieces

    def near_kernel(p, with_self=True, filler=None, every=4):
        for chunk in range(16):
            if filler is not None and chunk % every == 0:
                next(filler, None)
            rows = slice(chunk * 16, chunk * 16 + 16)
            c0 = (0 if chunk < 8 else 128) if with_self else 256
            sq = jnp.maximum(r2s[p, rows, c0:512], 1e-20)
            r = sq * lax.rsqrt(sq)
            decay = jnp.exp2(r * (-rate * math.log2(math.e)))
            rest = d0 + sq * (d1 + r * (q0 + r * q1))
            kn[p, rows, c0:512] = ((weight + (weight * rate) * r) * decay + rest).astype(jnp.bfloat16)

    first, second, whole = slice(0, 128), slice(128, 256), slice(0, 256)

    def plain(m, rows, cols, p):
        return jnp.dot(m, kn[p, rows, cols], preferred_element_type=jnp.float32)

    def turned(m, rows, cols, p):
        return lax.dot_general(m, kn[p, rows, cols], nt, preferred_element_type=jnp.float32)

    def near_apply(z, p):
        here = mw[0:32, span(z + 1)]
        there = mw[0:32, span(z + 2)]
        own = plain(here[:, first], first, whole, p)
        low = plain(here[:, second], second, second, p)
        high = turned(here[:, second], first, second, p)
        back = turned(there, whole, slice(256, 512), p)
        acc[:, span(z + 1)] += own + jnp.concatenate([high, low], 1) + back
        acc[:, span(z + 2)] = plain(here, whole, slice(256, 512), p)

    def near_step(z, p, filler=None, every=4):
        near_squared(z + 1, 1 - p)
        near_kernel(p, True, filler, every)
        near_apply(z - 1, 1 - p)

    def near_four(t, carry):
        for i in range(4):
            near_step(4 * t + (i + 1), (i + 1) % 2)
        return carry

    @pl.when(me == 0)
    def _():
        recv[0] = jnp.zeros(recv.shape[1:], jnp.float32)
        recv2[0] = jnp.zeros(recv2.shape[1:], jnp.float32)

    @pl.when(me == n - 1)
    def _():
        recv[1] = jnp.zeros(recv.shape[1:], jnp.float32)
        recv2[1] = jnp.zeros(recv2.shape[1:], jnp.float32)

    def sideways(source, target, rows, first_sem):
        to_left = pltpu.make_async_remote_copy(
            source.at[0, rows], target.at[1, rows],
            send_sems.at[first_sem], recv_sems.at[first_sem + 1],
            device_id=place((me + n - 1) & (n - 1)), device_id_type=mesh_id,
        )
        to_right = pltpu.make_async_remote_copy(
            source.at[1, rows], target.at[0, rows],
            send_sems.at[first_sem + 1], recv_sems.at[first_sem],
            device_id=place((me + 1) & (n - 1)), device_id_type=mesh_id,
        )
        return to_left, to_right

    point_edges = sideways(send, recv, pl.ds(base, 80), 0)
    leaf_edges = sideways(send, recv, pl.ds(0, base), 2)
    box_edges = sideways(send2, recv2, pl.ds(0, 32 * cube_levels), 4)

    def wait_edges(pair):
        edges(pair, lambda pair: pair[1].wait_recv(), lambda pair: pair[0].wait_recv())

    def edges(pair, left_action, right_action):
        @pl.when(me > 0)
        def _():
            left_action(pair)

        @pl.when(me < n - 1)
        def _():
            right_action(pair)

    def start_edges(pair):
        edges(pair, lambda pair: pair[0].start(), lambda pair: pair[1].start())

    def spread(k, target):
        return pltpu.make_async_remote_copy(
            gsend.at[target & 1], gath.at[me], gsend_sems.at[0], grecv_sems.at[0],
            device_id=place(target), device_id_type=mesh_id,
        )

    def spread_start(k, carry):
        spread(k, (me + k) & (n - 1)).start()
        return carry

    def first_sends():
        pl.semaphore_wait(barrier, n - 1)
        lax.fori_loop(1, n, spread_start, 0)
        start_edges(point_edges)

    hops = lax.rem(me // 2, 2) + lax.rem(me // 4, 2) + me // 8
    sooner = hops <= SOONER_HOPS

    @pl.when(jnp.logical_not(sooner))
    def _():
        first_sends()

    lax.fori_loop(0, layers, leaf_layer, 0, unroll=4)

    acc[:, 256:512] = jnp.zeros((32, 256), jnp.float32)
    late = layers // 4 - 1

    def climb():
        yield from couple()
        yield from rise()

    rising = climb()
    near_squared(jnp.int32(0), 0)
    near_squared(jnp.int32(1), 1)
    near_kernel(0, True, rising, 4)
    near_step(jnp.int32(1), 1, rising, 4)

    @pl.when(sooner)
    def _():
        first_sends()

    start_edges(leaf_edges)
    for z in range(2, 5):
        near_step(jnp.int32(z), z % 2, rising, 2)
    for _ in rising:
        pass
    start_edges(box_edges)
    lax.fori_loop(1, late, near_four, 0)

    def take_points():
        wait_edges(point_edges)
        for side, window in ((0, 0), (1, layers + 1)):
            for half in range(2):
                cols = slice(window * 256 + half * 128, window * 256 + half * 128 + 128)
                masked = recv[side, base + 32 * half : base + 32 + 32 * half]
                mw[0:32, cols] = masked.astype(jnp.bfloat16)
                pw[:, cols] = recv[side, base + 64 + 8 * half : base + 72 + 8 * half]

    def take_leaves():
        wait_edges(leaf_edges)
        for side in range(2):
            for i in range(2):
                at = i if side == 0 else layers + 2 + i
                for half in range(2):
                    start = (2 * i + half) * 32
                    lanes = slice(half * 128, half * 128 + 128)
                    lh[at, :, lanes], ls[at, :, lanes] = halves_bf16(recv[side, start : start + 32])

    def take_boxes():
        wait_edges(box_edges)
        for side in range(2):
            for height in range(cube_levels):
                at = offsets[height] + (0 if side == 0 else (pairs >> height) + 1)
                low_pairs[at] = recv2[side, 32 * height : 32 * height + 32]

    def leaves():
        spans = slice(1, layers + 3)
        rows = (layers + 2) * 32
        moments = dot_split(
            lh[spans].reshape(rows, 256), ls[spans].reshape(rows, 256), moment_in[0], moment_in[1]
        ).reshape(layers + 2, 32, 128)
        lane3 = lax.broadcasted_iota(jnp.int32, (layers, 32, 128), 2)
        joined = jnp.where(
            lane3 < 8, moments[0:layers],
            jnp.where(lane3 < 16, moments[1 : layers + 1], moments[2 : layers + 2]),
        )
        ll[...] = dot3(joined.reshape(layers * 32, 128), moment_out[0], moment_out[1]).reshape(
            layers, 32, 256
        )
        yield
        windows = [part[...].reshape(cubes + 2, 2, 32, 256) for part in (lh, ls)]
        for depth, sources in far_sources:
            gathered = [
                jnp.concatenate(
                    [w[s // 2 : s // 2 + cubes, s % 2].reshape(cubes * 32, 256) for s in sources], 1
                )
                for w in windows
            ]
            far_part = dot_split(*gathered, leaf_far[0, depth], leaf_far[1, depth])
            for j in range(cubes):
                ll[2 * j + depth] += far_part[32 * j : 32 * j + 32]
            yield

    def lower():
        expansion = None
        for height in reversed(range(cube_levels)):
            count = pairs >> height
            at = offsets[height]
            below = low_pairs[at : at + count].reshape(count * 32, 128)
            above = low_pairs[at + 2 : at + 2 + count].reshape(count * 32, 128)
            here = dot3(below, far[0, height, 0], far[1, height, 0]) + dot3(
                above, far[0, height, 1], far[1, height, 1]
            )
            if expansion is not None:
                below, above = [
                    dot3(expansion, box_down[0, side], box_down[1, side]).reshape(
                        count // 2, 1, 32, 128
                    )
                    for side in range(2)
                ]
                here = here + jnp.concatenate([below, above], 1).reshape(count * 32, 128)
            expansion = here
            yield
        inherited = dot3(expansion, leaf_down[0], leaf_down[1])
        yield
        for i in range(4):
            for j in range(pairs):
                ll[4 * j + i] += inherited[32 * j : 32 * j + 32, 256 * i : 256 * i + 256]
        yield

    partner = me + 1 - 2 * core
    swap = pltpu.make_async_remote_copy(
        crossed.at[core], crossed.at[core], swap_sems.at[0], swap_sems.at[1],
        device_id=place(partner), device_id_type=mesh_id,
    )

    def descend():
        count = n // 2
        blank = jnp.zeros((16, 128), jnp.float32)
        offset = 0
        tops = []
        for height in range(cube_levels, levels):
            tops.append(offset)
            ups[offset] = blank
            ups[offset + count + 1] = blank
            if height == cube_levels:

                folds = gath[...].reshape(count, 2, 8, 128)
                even, odd = folds[:, 0], folds[:, 1]
                near_half = lax.broadcasted_iota(jnp.int32, even.shape, 2) < 64
                ups[1 : 1 + count, 0:8] = jnp.where(near_half, even, pltpu.roll(odd, 64, 2))
                ups[1 : 1 + count, 8:16] = jnp.where(near_half, pltpu.roll(even, 64, 2), odd)
            else:
                two = ups[tops[-2] + 1 : tops[-2] + 1 + 2 * count].reshape(count, 2, 16, 128)
                level = dot3(
                    two[:, 0].reshape(count * 16, 128), box_up[0, 0], box_up[1, 0]
                ) + dot3(two[:, 1].reshape(count * 16, 128), box_up[0, 1], box_up[1, 1])
                ups[offset + 1 : offset + 1 + count] = level.reshape(count, 16, 128)
            offset += count + 2
            count //= 2
            yield

        expansion = None
        for height in range(levels - 1, cube_levels - 1, -1):
            j = me >> (height - cube_levels + 1)
            at = tops[height - cube_levels]
            below, above = ups[at + j], ups[at + j + 2]
            here = dot3(below, far[0, height, 0], far[1, height, 0]) + dot3(
                above, far[0, height, 1], far[1, height, 1]
            )
            if expansion is not None:
                parity = lax.rem(j, 2)
                here = here + dot3(expansion, box_down[0, parity], box_down[1, parity])
            expansion = here
            yield
        crossed[core] = expansion

    def join_halves():
        swap.wait_recv()
        both = jnp.concatenate([crossed[0], crossed[1]], 0)
        wide = lax.broadcasted_iota(jnp.int32, (32, 128), 1) < 64
        turned_round = pltpu.roll(both, 64, 1)
        own = jnp.where(wide == (core == 0), both, turned_round)
        high, low = halves_bf16(own)
        locs[...] = jnp.concatenate([high, low], 1)

    def settle():
        for z in range(layers):
            lhigh, llow = halves_bf16(ll[z])
            both = jnp.concatenate([lhigh, llow], 0)
            parts = []
            for half in range(2):
                cols = slice(half * 128, half * 128 + 128)
                main = jnp.dot(both[:, cols], bd[0, z, half], preferred_element_type=jnp.float32)
                rest = jnp.dot(lhigh[:, cols], bd[1, z, half], preferred_element_type=jnp.float32)
                parts.append(main[0:32] + main[32:64] + rest)
            acc[:, 256 * (z + 1) : 256 * (z + 2)] += jnp.concatenate(parts, 1)
            if z % 2:
                yield

    for copy in copies[4:]:
        copy.wait()
    take_leaves()
    spreading = leaves()
    near_step(jnp.int32(layers - 3), 1, spreading, 4)
    for _ in spreading:
        pass
    take_points()
    take_boxes()
    lowering = lower()
    near_step(jnp.int32(layers - 2), 0, lowering, 2)
    for _ in lowering:
        pass
    near_squared(jnp.int32(-1), 0, False)
    near_apply(jnp.int32(layers - 2), 0)

    everyone = pltpu.make_async_remote_copy(
        gath.at[pl.ds(0, n - 1)], gath.at[pl.ds(0, n - 1)], gsend_sems.at[0], grecv_sems.at[0],
        device_id=place(partner), device_id_type=mesh_id,
    )
    everyone.wait_recv()
    falling = descend()
    near_kernel(1, True, falling, 1)
    for _ in falling:
        pass
    swap.start()
    settling = settle()
    near_kernel(0, False, settling, 2)
    near_apply(jnp.int32(layers - 1), 1)
    acc[:, 256:512] += plain(mw[0:32, 0:256], whole, slice(256, 512), 0)
    for _ in settling:
        pass

    join_halves()

    def finish(z, carry):
        value = acc[:, span(z + 1)] + jnp.dot(
            locs[:, 0:192],
            jnp.concatenate([b3[:, span(z)], b3[0:64, span(z)]], 0),
            preferred_element_type=jnp.float32,
        )
        out[:, span(z)] = value * occupancy(z)
        return carry

    lax.fori_loop(0, layers, finish, 0, unroll=8)

    swap.wait_send()
    for pair in (point_edges, leaf_edges, box_edges):
        edges(pair, lambda pair: pair[0].wait_send(), lambda pair: pair[1].wait_send())

    everyone.wait_send()


def local(points, vectors, counts):
    cubes = counts.shape[0]
    nleaf, nsub = lax.axis_size("leaf"), lax.axis_size("sub")
    n = nleaf * nsub
    slab_count = cubes * n
    level_count = slab_count.bit_length() - 2
    cube_levels = cubes.bit_length() - 1
    lengths = term_lengths(slab_count)
    node_values = chebyshev(ORDER)
    leaf_up, leaf_down, box_up, box_down, far, leaf_far = [
        jnp.asarray(np_halves(t)) for t in make_tables(node_values, level_count, lengths)
    ]
    (c0, c1), pieces = smooth_split(lengths)
    moment_in, moment_out = [jnp.asarray(np_halves(t)) for t in moment_tables(node_values, c0, c1)]
    layers = 2 * cubes
    pairs = cubes // 2
    low_count = sum((pairs >> h) + 2 for h in range(cube_levels))
    top_count = sum((n // 2 >> h) + 2 for h in range(level_count - cube_levels))
    f32, bf16 = jnp.float32, jnp.bfloat16
    tables = (leaf_up, box_up, leaf_down, box_down, far, leaf_far, moment_in, moment_out)
    stay = pl.BlockSpec(memory_space=pltpu.HBM)
    return pl.pallas_call(
        functools.partial(kernel_body, (nleaf, nsub, cubes, level_count), lengths, pieces),
        out_shape=jax.ShapeDtypeStruct(vectors.shape, f32),
        in_specs=[stay, stay, pl.BlockSpec(memory_space=pltpu.SMEM)] + [stay] * len(tables),
        out_specs=pl.BlockSpec(memory_space=pltpu.VMEM),
        scratch_shapes=[
            pltpu.VMEM(points.shape, f32),
            pltpu.VMEM(vectors.shape, f32),
            pltpu.VMEM((64, (layers + 2) * 256), bf16),
            pltpu.VMEM((8, (layers + 2) * 256), f32),
            pltpu.VMEM((2, layers, 2, 128, 128), bf16),
            pltpu.VMEM((128, layers * 256), bf16),
            pltpu.VMEM((layers + 4, 32, 256), bf16),
            pltpu.VMEM((layers + 4, 32, 256), bf16),
            pltpu.VMEM((2, 256, 512), f32),
            pltpu.VMEM((2, 256, 512), bf16),
            pltpu.VMEM((32, (layers + 2) * 256), f32),
            pltpu.VMEM((2, 208, 128), f32),
            pltpu.VMEM((2, 208, 128), f32),
            pltpu.VMEM((2, 32 * cube_levels, 128), f32),
            pltpu.VMEM((2, 32 * cube_levels, 128), f32),
            pltpu.VMEM((2, 8, 128), f32),
            pltpu.VMEM((n, 8, 128), f32),
            pltpu.VMEM((2, 16, 128), f32),
            pltpu.VMEM((low_count, 32, 128), f32),
            pltpu.VMEM((top_count, 16, 128), f32),
            pltpu.VMEM((32, 256), bf16),
            pltpu.VMEM((layers, 32, 256), f32),
        ] + [pltpu.VMEM(t.shape, bf16) for t in tables] + [
            pltpu.SemaphoreType.DMA((6,)),
            pltpu.SemaphoreType.DMA((6,)),
            pltpu.SemaphoreType.DMA((1,)),
            pltpu.SemaphoreType.DMA((1,)),
            pltpu.SemaphoreType.DMA((2,)),
            pltpu.SemaphoreType.DMA((2 + len(tables),)),
        ],
        compiler_params=pltpu.CompilerParams(
            collective_id=0, has_side_effects=True, vmem_limit_bytes=VMEM_BYTES
        ),
    )(points, vectors, counts, *tables)


def solution(mesh):
    in_specs = (P(None, ("leaf", "sub")), P(None, ("leaf", "sub")), P(("leaf", "sub"), None))
    out_specs = P(None, ("leaf", "sub"))
    return jax.shard_map(local, mesh=mesh, in_specs=in_specs, out_specs=out_specs, check_vma=False)
```

```python
import functools
import math

import jax
import jax.numpy as jnp
import numpy as np
from jax import lax
from jax.experimental import pallas as pl
from jax.experimental.pallas import tpu as pltpu
from jax.sharding import PartitionSpec as P

ORDER = 4
FIRST_DEVICES = 2
SOONER_PLACE = 3
LATER_PLACE = 1
VMEM_BYTES = 60 * 1024 * 1024


TERM_SCALE = 1.0 / 32.0
ROOT_THREE = math.sqrt(3.0)
far_offsets = (-3, -2, 2, 3)
far_sources = ((0, (0, 4, 5)), (1, (0, 1, 5)))


def term_lengths(slab_count):
    term_count = (slab_count.bit_length() - 1) // 3 + 1
    return [slab_count / 4.0 / 8.0**term_index for term_index in range(term_count)]


def chebyshev(order):
    return np.cos((2.0 * np.arange(order) + 1.0) * np.pi / (2.0 * order))


def lagrange_table(values, node_values):
    columns = []
    for anchor in range(len(node_values)):
        product = values * 0.0 + 1.0
        for against in range(len(node_values)):
            if against != anchor:
                product = (
                    product
                    * (values - node_values[against])
                    / (node_values[anchor] - node_values[against])
                )
        columns.append(product)
    return np.stack(columns, -1)


def grid_nodes(node_values):
    number = len(node_values)
    along_z, along_y, along_x = np.meshgrid(
        np.arange(number), np.arange(number), np.arange(number), indexing="ij"
    )
    return np.stack(
        [node_values[along_x.ravel()], node_values[along_y.ravel()], node_values[along_z.ravel()]],
        -1,
    )


def kernel_table(targets, sources, lengths):
    offsets_xyz = targets[:, None, :] - sources[None, :, :]
    distance = np.sqrt(np.sum(offsets_xyz * offsets_xyz, -1))
    summed_terms = distance * 0.0
    for length in lengths:
        scaled = distance * (ROOT_THREE / length)
        summed_terms = summed_terms + TERM_SCALE / math.sqrt(length) * (1.0 + scaled) * np.exp(
            -scaled
        )
    return summed_terms


def child_tables(node_values):
    halves = [
        lagrange_table(side_offset + 0.5 * node_values, node_values) for side_offset in (-0.5, 0.5)
    ]
    identity = np.eye(len(node_values))
    octant_rows = []
    for depth_index in range(2):
        for row_index in range(2):
            for column_index in range(2):
                octant_rows.append(
                    np.kron(np.kron(halves[depth_index], halves[row_index]), halves[column_index])
                )
    octant_array = np.stack(octant_rows).reshape((2, 2, 2) + octant_rows[0].shape)
    half_array = np.stack(
        [np.kron(np.kron(halves[half_index], identity), identity) for half_index in range(2)]
    )
    return (octant_array, half_array)


def coarse_couplings(node_values, height, lengths):
    span = float(1 << height)
    targets = grid_nodes(node_values) * np.array([0.5, 0.5, 0.5 * span])
    return np.stack(
        [
            kernel_table(targets, targets + np.array([0.0, 0.0, offset * span]), lengths)
            for offset in far_offsets
        ]
    )


def halves_bf16(value):
    high = value.astype(jnp.bfloat16)
    low = (value - high.astype(jnp.float32)).astype(jnp.bfloat16)
    return high, low


def np_halves(table):
    table = np.asarray(table, np.float32)
    high = table.astype(jnp.bfloat16)
    low = (table - high.astype(np.float32)).astype(jnp.bfloat16)
    return np.stack([high, low])


def dot_split(first, second, high, low):
    return jnp.dot(
        jnp.concatenate([first, second, first], 1), jnp.concatenate([high, high, low], 0),
        preferred_element_type=jnp.float32,
    )


def dot3(value, high, low):
    return dot_split(*halves_bf16(value), high, low)


def smooth_split(lengths):
    r = np.linspace(0.0, math.sqrt(3.0) * 1.0005, 2001)
    s = r * r

    def term(length):
        a = r * (ROOT_THREE / length)
        return TERM_SCALE / math.sqrt(length) * (1.0 + a) * np.exp(-a)

    smooth = sum(term(length) for length in lengths[:-1])
    basis = np.stack([np.ones_like(r), s, s * r, s * s], 1)
    weight = np.ones_like(r)
    for _ in range(100):
        root = np.sqrt(weight)
        fitted = np.linalg.lstsq(basis * root[:, None], smooth * root, rcond=None)[0]
        error = np.abs(smooth - basis @ fitted)
        weight = weight * (error / error.max() + 1e-3)
        weight = weight / weight.mean()
    full = smooth + term(lengths[-1])
    low = basis[:, :2]
    c0, c1 = np.linalg.lstsq(low / full[:, None], np.ones_like(r), rcond=None)[0]
    return (float(c0), float(c1)), [float(v) for v in fitted - np.array([c0, c1, 0.0, 0.0])]


def layer_nodes(node_values):
    nodes = grid_nodes(node_values) * 0.25
    return np.concatenate(
        [nodes + np.array([0.5 * c - 0.25, 0.5 * r - 0.25, 0.0]) for r in range(2) for c in range(2)]
    )


def far_split(node_values, step, lengths):
    nodes = layer_nodes(node_values)
    offsets_xyz = nodes[:, None] - nodes[None] - np.array([0.0, 0.0, 0.5 * step])
    squared = np.sum(offsets_xyz * offsets_xyz, -1).ravel()
    table = kernel_table(nodes, nodes + np.array([0.0, 0.0, 0.5 * step]), lengths).ravel()
    basis = np.stack([np.ones_like(squared), squared], 1)
    c0, c1 = np.linalg.lstsq(basis, table, rcond=None)[0]
    return float(c0), float(c1), (table - basis @ np.array([c0, c1])).reshape(len(nodes), -1)


def moment_tables(node_values, near, lengths):
    x, y, d = layer_nodes(node_values).T
    norm = x * x + y * y + d * d
    one = np.ones_like(x)
    gather = np.zeros((len(x), 128))
    spread = np.zeros((128, len(x)))
    for group, step in enumerate(range(-3, 4)):
        c0, c1 = near if abs(step) < 2 else far_split(node_values, step, lengths)[:2]
        source = (
            c0 + c1 * (norm + step * step / 4.0 + step * d), -2.0 * c1 * x, -2.0 * c1 * y,
            -c1 * (2.0 * d + step), c1 * one,
        )
        for index, (column, row) in enumerate(zip(source, (one, x, y, d, norm))):
            gather[:, 8 * group + index] = column
            spread[8 * group + index] = row
    leaf_far = np.stack(
        [
            np.concatenate(
                [far_split(node_values, layer - 2 - depth, lengths)[2].T for layer in layers]
            )
            for depth, layers in far_sources
        ]
    )
    return gather, spread, leaf_far


def lagrange_coefficients(node_values):
    rows = []
    for anchor in range(len(node_values)):
        others = np.delete(node_values, anchor)
        rows.append(np.poly(others)[::-1] / np.prod(node_values[anchor] - others))
    return np.stack(rows)


def make_tables(node_values, level_count, lengths):
    octants, halves = child_tables(node_values)
    rank = ORDER**3
    eight = octants.reshape(8, rank, rank)
    leaf_up = np.zeros((2, 8, rank, 2, rank))
    for parity in range(2):
        leaf_up[parity, :, :, parity, :] = eight
    leaf_up = leaf_up.reshape(16 * rank, 2 * rank)
    leaf_down = leaf_up.T
    box_up = np.zeros((2, 2, rank, 2, rank))
    for parity in range(2):
        box_up[parity, :, :, parity, :] = halves
    box_up = box_up.reshape(2, 2 * rank, 2 * rank)
    box_down = np.swapaxes(box_up, 1, 2)
    far = np.zeros((level_count, 2, 2, rank, 2, rank))
    for height in range(level_count):
        m3, m2, p2, p3 = [c.T for c in coarse_couplings(node_values, height, lengths)]
        far[height, 0, 0, :, 0] = m2
        far[height, 0, 0, :, 1] = m3
        far[height, 0, 1, :, 1] = m2
        far[height, 1, 0, :, 0] = p2
        far[height, 1, 1, :, 0] = p3
        far[height, 1, 1, :, 1] = p2
    far = far.reshape(level_count, 2, 2 * rank, 2 * rank)
    return leaf_up, leaf_down, box_up, box_down, far


def kernel_body(
    dims, lengths, pieces, pts_hbm, vec_hbm, cnt, leaf_up_hbm, box_up_hbm, leaf_down_hbm,
    box_down_hbm, far_hbm, leaf_far_hbm, moment_in_hbm, moment_out_hbm,
    out, pts, vec, mw, pw, bd, b3, lh, ls, r2s, kn, acc, send, recv, send2, recv2, gsend, gath, crossed,
    low_pairs, ups, locs, ll, leaf_up, box_up, leaf_down, box_down, far, leaf_far, moment_in,
    moment_out, send_sems, recv_sems, gsend_sems, grecv_sems, swap_sems, table_sems,
):
    nleaf, nsub, cubes, levels = dims
    n = nleaf * nsub
    layers = 2 * cubes
    cube_levels = cubes.bit_length() - 1
    nodes = chebyshev(ORDER)
    me = lax.axis_index("leaf") * nsub + lax.axis_index("sub")
    mesh_id = pl.DeviceIdType.LOGICAL

    def place(d):
        return d

    copies = [
        pltpu.make_async_copy(source, target, table_sems.at[index])
        for index, (source, target) in enumerate((
            (pts_hbm, pts), (vec_hbm, vec), (leaf_up_hbm, leaf_up), (box_up_hbm, box_up),
            (moment_in_hbm, moment_in), (moment_out_hbm, moment_out), (leaf_far_hbm, leaf_far),
            (far_hbm, far), (box_down_hbm, box_down), (leaf_down_hbm, leaf_down),
        ))
    ]
    for copy in copies:
        copy.start()

    barrier = pltpu.get_barrier_semaphore()

    def greet(k, carry):
        pl.semaphore_signal(
            barrier, inc=1, device_id=place((me + k) & (n - 1)), device_id_type=mesh_id
        )
        return carry

    lax.fori_loop(1, n, greet, 0)

    first_slab = (me * cubes).astype(jnp.float32)
    lane = lax.broadcasted_iota(jnp.int32, (1, 256), 1)
    quarter = lane // 64
    slot = lane - quarter * 64
    centre_x = ((quarter % 2).astype(jnp.float32) + 0.5) * 0.5
    centre_y = ((quarter // 2).astype(jnp.float32) + 0.5) * 0.5
    row8 = lax.broadcasted_iota(jnp.int32, (8, 512), 0)

    def span(z, width=256):
        return pl.ds(pl.multiple_of(z * 256, 256), width)

    def occupancy(z):
        cube, base = z // 2, lax.rem(z, 2) * 4
        limit = jnp.where(
            quarter < 2,
            jnp.where(quarter == 0, cnt[cube, base], cnt[cube, base + 1]),
            jnp.where(quarter == 2, cnt[cube, base + 2], cnt[cube, base + 3]),
        )
        return jnp.where(slot < limit, 1.0, 0.0)

    table = lagrange_coefficients(nodes)
    row16 = lax.broadcasted_iota(jnp.int32, (16, 128), 0)

    def spread_rows(anchor):
        powers = []
        for power in range(ORDER):
            c = [float(v) for v in table[:, power]]
            one = jnp.where(
                anchor < 2, jnp.where(anchor == 0, c[0], c[1]), jnp.where(anchor == 2, c[2], c[3])
            )
            powers.append(jnp.concatenate([one, one], 1))
        return powers

    along_x = spread_rows(row16 % ORDER)
    along_y = spread_rows(row16 // ORDER)
    along_z = [c[0:8] for c in along_x]

    def poly_of(u, powers):
        p0, p1, p2, p3 = powers
        return ((p3 * u + p2) * u + p1) * u + p0

    def basis_of(ux, uy, uz):
        plane = poly_of(ux, along_x) * poly_of(uy, along_y)
        height = poly_of(uz, along_z)
        return halves_bf16(
            jnp.concatenate([plane * height[a : a + 1] for a in range(ORDER)], 0)
        )

    nt = (((1,), (1,)), ((), ()))
    left64 = lax.broadcasted_iota(jnp.int32, (64, 128), 1) < 64
    nothing = jnp.zeros((64, 128), jnp.bfloat16)

    def box_layer(z, carry):
        masked = vec[:, span(z)] * occupancy(z)
        mw[0:32, span(z + 1)], mw[32:64, span(z + 1)] = halves_bf16(masked)
        coords = pts[:, span(z)]
        pw[0:3, span(z + 1)] = coords
        b3[0:64, span(z)], b3[64:128, span(z)] = basis_of(
            coords[0:1] * 2.0 - 1.0, coords[1:2] * 2.0 - 1.0,
            (coords[2:3] - first_slab) * (2.0 / cubes) - 1.0,
        )
        return carry

    def leaf_layer(z, carry):
        coords = pts[:, span(z)]
        depth = (lax.rem(z, 2).astype(jnp.float32) + 0.5) * 0.5
        slab = first_slab + (z // 2).astype(jnp.float32)
        high, low = basis_of(
            (coords[0:1] - centre_x) * 4.0, (coords[1:2] - centre_y) * 4.0,
            ((coords[2:3] - slab) - depth) * 4.0,
        )
        for half in range(2):
            cols = slice(half * 128, half * 128 + 128)
            for which, part in ((0, high[:, cols]), (1, low[:, cols])):
                bd[which, z, half] = jnp.concatenate(
                    [jnp.where(left64, part, nothing), jnp.where(left64, nothing, part)], 0
                )
        return carry

    def couple():
        edge = [0, 1, layers - 2, layers - 1]
        for index, z in enumerate(edge + list(range(2, layers - 2))):
            for half in range(2):
                cols = slice(half * 128, half * 128 + 128)
                at = slice(256 * (z + 1) + half * 128, 256 * (z + 1) + half * 128 + 128)
                main = lax.dot_general(
                    mw[:, at], bd[0, z, half], nt, preferred_element_type=jnp.float32
                )
                rest = lax.dot_general(
                    mw[0:32, at], bd[1, z, half], nt, preferred_element_type=jnp.float32
                )
                coeffs = main[0:32] + main[32:64] + rest
                if z in edge:
                    side, i = (0, z) if z < 2 else (1, z - layers + 2)
                    start = (2 * i + half) * 32
                    send[side, start : start + 32] = coeffs
                lh[z + 2, :, cols], ls[z + 2, :, cols] = halves_bf16(coeffs)
            if index % 2:
                yield

    copies[0].wait()
    copies[1].wait()
    lax.fori_loop(0, layers, box_layer, 0, unroll=4)
    box = lax.dot_general(
        mw[:, 256 : 256 + layers * 256], b3[...], nt, preferred_element_type=jnp.float32
    )

    pairs = cubes // 2
    lane128 = lax.broadcasted_iota(jnp.int32, (16, 128), 1)
    offsets = []
    base = 128
    box = box[0:32] + box[32:64]
    box = box + pltpu.roll(box, 64, 1)
    core = lax.rem(me, 2)
    folded = [
        jnp.where(lane128[0:8] < 64, box[16 * k : 16 * k + 8], box[16 * k + 8 : 16 * k + 16])
        for k in range(2)
    ]
    gsend[0] = folded[0]
    gsend[1] = folded[1]
    gath[me] = jnp.where(core == 0, folded[0], folded[1])

    def rise():
        for copy in copies[2:4]:
            copy.wait()
        flat = []
        for part in (lh, ls):
            own = part[2 : 2 + layers].reshape(pairs, 4, 32, 256)
            flat.append(jnp.concatenate([own[:, i].reshape(pairs * 32, 256) for i in range(4)], 1))
        level = dot_split(*flat, leaf_up[0], leaf_up[1]).reshape(pairs, 32, 128)
        yield
        offset = 0
        for height in range(cube_levels):
            offsets.append(offset)
            count = pairs >> height
            low_pairs[offset + 1 : offset + 1 + count] = level
            send2[0, 32 * height : 32 * height + 32] = level[0]
            send2[1, 32 * height : 32 * height + 32] = level[count - 1]
            offset += count + 2
            if count > 1:
                two = level.reshape(count // 2, 2, 32, 128)
                level = dot3(
                    two[:, 0].reshape(count * 16, 128), box_up[0, 0], box_up[1, 0]
                ) + dot3(two[:, 1].reshape(count * 16, 128), box_up[0, 1], box_up[1, 1])
                level = level.reshape(count // 2, 32, 128)
                yield

    for side, edge in ((0, 0), (1, layers - 1)):
        masked = vec[:, edge * 256 : edge * 256 + 256] * occupancy(jnp.int32(edge))
        coords = pts[:, edge * 256 : edge * 256 + 256]
        for half in range(2):
            cols = slice(half * 128, half * 128 + 128)
            send[side, base + 32 * half : base + 32 + 32 * half] = masked[:, cols]
            send[side, base + 64 + 8 * half : base + 67 + 8 * half] = coords[:, cols]
    pad = jnp.zeros((5, 128), jnp.float32)
    for side in range(2):
        for half in range(2):
            send[side, base + 67 + 8 * half : base + 72 + 8 * half] = pad

    def near_squared(z, p, with_self=True):
        boundary = first_slab + (z + 1).astype(jnp.float32) * 0.5
        block = pw[:, span(z + 1, 512)]
        x = block[0:1] - 0.5
        y = block[1:2] - 0.5
        d = block[2:3] - boundary
        norm = x * x + y * y + d * d
        one = jnp.where(row8 == 4, 1.0, 0.0)
        right = jnp.where(row8 == 0, x, jnp.where(row8 == 1, y, jnp.where(row8 == 2, d,
            jnp.where(row8 == 3, norm, one))))
        swap = jnp.where(row8 == 3, 1.0, jnp.where(row8 == 4, norm, 0.0))
        left = jnp.where(row8 < 3, -2.0 * right, swap)[:, 0:256]

        def thirds(v):
            h = v.astype(jnp.bfloat16).astype(jnp.float32)
            m = (v - h).astype(jnp.bfloat16).astype(jnp.float32)
            return h, m, v - h - m

        rh, rm, rl = thirds(right)
        lh, lm, lo = thirds(left)
        if not with_self:
            rh, rm, rl = rh[:, 256:], rm[:, 256:], rl[:, 256:]
        rs = jnp.concatenate([rh, rm, rh, rl, rm, rh], 0).astype(jnp.bfloat16)
        ls = jnp.concatenate([lh, lh, lm, lh, lm, lo], 0).astype(jnp.bfloat16)
        r2s[p, :, (0 if with_self else 256) : 512] = lax.dot_general(
            ls, rs, (((0,), (0,)), ((), ())), preferred_element_type=jnp.float32
        )

    rate = ROOT_THREE / lengths[-1]
    weight = TERM_SCALE / math.sqrt(lengths[-1])
    d0, d1, q0, q1 = pieces

    def near_kernel(p, with_self=True, filler=None, every=4):
        for chunk in range(16):
            if filler is not None and chunk % every == 0:
                next(filler, None)
            rows = slice(chunk * 16, chunk * 16 + 16)
            c0 = (0 if chunk < 8 else 128) if with_self else 256
            sq = jnp.maximum(r2s[p, rows, c0:512], 1e-20)
            r = sq * lax.rsqrt(sq)
            decay = jnp.exp2(r * (-rate * math.log2(math.e)))
            rest = d0 + sq * (d1 + r * (q0 + r * q1))
            kn[p, rows, c0:512] = ((weight + (weight * rate) * r) * decay + rest).astype(jnp.bfloat16)

    first, second, whole = slice(0, 128), slice(128, 256), slice(0, 256)

    def plain(m, rows, cols, p):
        return jnp.dot(m, kn[p, rows, cols], preferred_element_type=jnp.float32)

    def turned(m, rows, cols, p):
        return lax.dot_general(m, kn[p, rows, cols], nt, preferred_element_type=jnp.float32)

    def near_apply(z, p):
        here = mw[0:32, span(z + 1)]
        there = mw[0:32, span(z + 2)]
        own = plain(here[:, first], first, whole, p)
        low = plain(here[:, second], second, second, p)
        high = turned(here[:, second], first, second, p)
        back = turned(there, whole, slice(256, 512), p)
        acc[:, span(z + 1)] += own + jnp.concatenate([high, low], 1) + back
        acc[:, span(z + 2)] = plain(here, whole, slice(256, 512), p)

    def near_step(z, p, filler=None, every=4):
        near_squared(z + 1, 1 - p)
        near_kernel(p, True, filler, every)
        near_apply(z - 1, 1 - p)

    def near_four(t, carry):
        for i in range(4):
            near_step(4 * t + (i + 1), (i + 1) % 2)
        return carry

    @pl.when(me == 0)
    def _():
        recv[0] = jnp.zeros(recv.shape[1:], jnp.float32)
        recv2[0] = jnp.zeros(recv2.shape[1:], jnp.float32)

    @pl.when(me == n - 1)
    def _():
        recv[1] = jnp.zeros(recv.shape[1:], jnp.float32)
        recv2[1] = jnp.zeros(recv2.shape[1:], jnp.float32)

    def sideways(source, target, rows, first_sem):
        to_left = pltpu.make_async_remote_copy(
            source.at[0, rows], target.at[1, rows],
            send_sems.at[first_sem], recv_sems.at[first_sem + 1],
            device_id=place((me + n - 1) & (n - 1)), device_id_type=mesh_id,
        )
        to_right = pltpu.make_async_remote_copy(
            source.at[1, rows], target.at[0, rows],
            send_sems.at[first_sem + 1], recv_sems.at[first_sem],
            device_id=place((me + 1) & (n - 1)), device_id_type=mesh_id,
        )
        return to_left, to_right

    point_edges = sideways(send, recv, pl.ds(base, 80), 0)
    leaf_edges = sideways(send, recv, pl.ds(0, base), 2)
    box_edges = sideways(send2, recv2, pl.ds(0, 32 * cube_levels), 4)

    def wait_edges(pair):
        edges(pair, lambda pair: pair[1].wait_recv(), lambda pair: pair[0].wait_recv())

    def edges(pair, left_action, right_action):
        @pl.when(me > 0)
        def _():
            left_action(pair)

        @pl.when(me < n - 1)
        def _():
            right_action(pair)

    def start_edges(pair):
        edges(pair, lambda pair: pair[0].start(), lambda pair: pair[1].start())

    def spread(k, target):
        return pltpu.make_async_remote_copy(
            gsend.at[target & 1], gath.at[me], gsend_sems.at[0], grecv_sems.at[0],
            device_id=place(target), device_id_type=mesh_id,
        )

    def spread_start(k, carry):
        spread(k, (me + k) & (n - 1)).start()
        return carry

    def first_sends():
        pl.semaphore_wait(barrier, n - 1)
        lax.fori_loop(1, n, spread_start, 0)
        start_edges(point_edges)

    sooner = me < FIRST_DEVICES

    def at_place(number):
        if LATER_PLACE == number:
            @pl.when(jnp.logical_not(sooner))
            def _():
                first_sends()
        if SOONER_PLACE == number:
            @pl.when(sooner)
            def _():
                first_sends()

    at_place(0)
    lax.fori_loop(0, layers, leaf_layer, 0, unroll=4)
    at_place(1)

    acc[:, 256:512] = jnp.zeros((32, 256), jnp.float32)
    late = layers // 4 - 1

    def climb():
        yield from couple()
        yield from rise()

    rising = climb()
    near_squared(jnp.int32(0), 0)
    near_squared(jnp.int32(1), 1)
    near_kernel(0, True, rising, 4)
    near_step(jnp.int32(1), 1, rising, 4)
    at_place(2)
    if SOONER_PLACE == 3:
        @pl.when(jnp.logical_not(sooner))
        def _():
            start_edges(leaf_edges)
    else:
        start_edges(leaf_edges)
    for z in range(2, 5):
        near_step(jnp.int32(z), z % 2, rising, 2)
    for _ in rising:
        pass
    if SOONER_PLACE == 3:
        @pl.when(sooner)
        def _():
            first_sends()
            start_edges(leaf_edges)
    start_edges(box_edges)
    lax.fori_loop(1, late, near_four, 0)

    def take_points():
        wait_edges(point_edges)
        for side, window in ((0, 0), (1, layers + 1)):
            for half in range(2):
                cols = slice(window * 256 + half * 128, window * 256 + half * 128 + 128)
                masked = recv[side, base + 32 * half : base + 32 + 32 * half]
                mw[0:32, cols] = masked.astype(jnp.bfloat16)
                pw[:, cols] = recv[side, base + 64 + 8 * half : base + 72 + 8 * half]

    def take_leaves():
        wait_edges(leaf_edges)
        for side in range(2):
            for i in range(2):
                at = i if side == 0 else layers + 2 + i
                for half in range(2):
                    start = (2 * i + half) * 32
                    lanes = slice(half * 128, half * 128 + 128)
                    lh[at, :, lanes], ls[at, :, lanes] = halves_bf16(recv[side, start : start + 32])

    def take_boxes():
        wait_edges(box_edges)
        for side in range(2):
            for height in range(cube_levels):
                at = offsets[height] + (0 if side == 0 else (pairs >> height) + 1)
                low_pairs[at] = recv2[side, 32 * height : 32 * height + 32]

    def leaves():
        rows = (layers + 4) * 32
        moments = dot_split(
            lh[...].reshape(rows, 256), ls[...].reshape(rows, 256), moment_in[0], moment_in[1]
        ).reshape(cubes + 2, 2, 32, 128)
        yield
        window = lh[...].reshape(cubes + 2, 2, 32, 256)
        group = lax.broadcasted_iota(jnp.int32, (cubes, 32, 128), 2) // 8
        for depth, sources in far_sources:
            joined = jnp.zeros((cubes, 32, 128), jnp.float32)
            for s in range(6):
                joined = jnp.where(
                    group == s + 1 - depth, moments[s // 2 : s // 2 + cubes, s % 2], joined
                )
            jh, jl = halves_bf16(joined.reshape(cubes * 32, 128))
            total = jnp.dot(
                jnp.concatenate(
                    [jh, jl, jh]
                    + [window[s // 2 : s // 2 + cubes, s % 2].reshape(cubes * 32, 256) for s in sources],
                    1,
                ),
                jnp.concatenate(
                    [moment_out[0], moment_out[0], moment_out[1], leaf_far[depth]], 0
                ),
                preferred_element_type=jnp.float32,
            )
            for j in range(cubes):
                ll[2 * j + depth] = total[32 * j : 32 * j + 32]
            yield

    def lower():
        expansion = None
        for height in reversed(range(cube_levels)):
            count = pairs >> height
            at = offsets[height]
            below = low_pairs[at : at + count].reshape(count * 32, 128)
            above = low_pairs[at + 2 : at + 2 + count].reshape(count * 32, 128)
            here = dot3(below, far[0, height, 0], far[1, height, 0]) + dot3(
                above, far[0, height, 1], far[1, height, 1]
            )
            if expansion is not None:
                below, above = [
                    dot3(expansion, box_down[0, side], box_down[1, side]).reshape(
                        count // 2, 1, 32, 128
                    )
                    for side in range(2)
                ]
                here = here + jnp.concatenate([below, above], 1).reshape(count * 32, 128)
            expansion = here
            yield
        inherited = dot3(expansion, leaf_down[0], leaf_down[1])
        yield
        for i in range(4):
            for j in range(pairs):
                ll[4 * j + i] += inherited[32 * j : 32 * j + 32, 256 * i : 256 * i + 256]
        yield

    partner = me + 1 - 2 * core
    swap = pltpu.make_async_remote_copy(
        crossed.at[core], crossed.at[core], swap_sems.at[0], swap_sems.at[1],
        device_id=place(partner), device_id_type=mesh_id,
    )

    def descend():
        count = n // 2
        blank = jnp.zeros((16, 128), jnp.float32)
        offset = 0
        tops = []
        for height in range(cube_levels, levels):
            tops.append(offset)
            ups[offset] = blank
            ups[offset + count + 1] = blank
            if height == cube_levels:

                folds = gath[...].reshape(count, 2, 8, 128)
                even, odd = folds[:, 0], folds[:, 1]
                near_half = lax.broadcasted_iota(jnp.int32, even.shape, 2) < 64
                ups[1 : 1 + count, 0:8] = jnp.where(near_half, even, pltpu.roll(odd, 64, 2))
                ups[1 : 1 + count, 8:16] = jnp.where(near_half, pltpu.roll(even, 64, 2), odd)
            else:
                two = ups[tops[-2] + 1 : tops[-2] + 1 + 2 * count].reshape(count, 2, 16, 128)
                level = dot3(
                    two[:, 0].reshape(count * 16, 128), box_up[0, 0], box_up[1, 0]
                ) + dot3(two[:, 1].reshape(count * 16, 128), box_up[0, 1], box_up[1, 1])
                ups[offset + 1 : offset + 1 + count] = level.reshape(count, 16, 128)
            offset += count + 2
            count //= 2
            yield

        expansion = None
        for height in range(levels - 1, cube_levels - 1, -1):
            j = me >> (height - cube_levels + 1)
            at = tops[height - cube_levels]
            below, above = ups[at + j], ups[at + j + 2]
            here = dot3(below, far[0, height, 0], far[1, height, 0]) + dot3(
                above, far[0, height, 1], far[1, height, 1]
            )
            if expansion is not None:
                parity = lax.rem(j, 2)
                here = here + dot3(expansion, box_down[0, parity], box_down[1, parity])
            expansion = here
            yield
        crossed[core] = expansion

    def join_halves():
        swap.wait_recv()
        both = jnp.concatenate([crossed[0], crossed[1]], 0)
        wide = lax.broadcasted_iota(jnp.int32, (32, 128), 1) < 64
        turned_round = pltpu.roll(both, 64, 1)
        own = jnp.where(wide == (core == 0), both, turned_round)
        high, low = halves_bf16(own)
        locs[...] = jnp.concatenate([high, low], 1)

    def settle():
        for z in range(layers):
            lhigh, llow = halves_bf16(ll[z])
            both = jnp.concatenate([lhigh, llow], 0)
            parts = []
            for half in range(2):
                cols = slice(half * 128, half * 128 + 128)
                main = jnp.dot(both[:, cols], bd[0, z, half], preferred_element_type=jnp.float32)
                rest = jnp.dot(lhigh[:, cols], bd[1, z, half], preferred_element_type=jnp.float32)
                parts.append(main[0:32] + main[32:64] + rest)
            acc[:, 256 * (z + 1) : 256 * (z + 2)] += jnp.concatenate(parts, 1)
            if z % 2:
                yield

    for copy in copies[4:]:
        copy.wait()
    take_leaves()
    spreading = leaves()
    near_step(jnp.int32(layers - 3), 1, spreading, 4)
    for _ in spreading:
        pass
    take_points()
    take_boxes()
    lowering = lower()
    near_step(jnp.int32(layers - 2), 0, lowering, 2)
    for _ in lowering:
        pass
    near_squared(jnp.int32(-1), 0, False)
    near_apply(jnp.int32(layers - 2), 0)

    everyone = pltpu.make_async_remote_copy(
        gath.at[pl.ds(0, n - 1)], gath.at[pl.ds(0, n - 1)], gsend_sems.at[0], grecv_sems.at[0],
        device_id=place(partner), device_id_type=mesh_id,
    )
    everyone.wait_recv()
    falling = descend()
    near_kernel(1, True, falling, 1)
    for _ in falling:
        pass
    swap.start()
    settling = settle()
    near_kernel(0, False, settling, 2)
    near_apply(jnp.int32(layers - 1), 1)
    acc[:, 256:512] += plain(mw[0:32, 0:256], whole, slice(256, 512), 0)
    for _ in settling:
        pass

    join_halves()

    def finish(z, carry):
        value = acc[:, span(z + 1)] + jnp.dot(
            locs[:, 0:192],
            jnp.concatenate([b3[:, span(z)], b3[0:64, span(z)]], 0),
            preferred_element_type=jnp.float32,
        )
        out[:, span(z)] = value * occupancy(z)
        return carry

    lax.fori_loop(0, layers, finish, 0, unroll=8)

    swap.wait_send()
    for pair in (point_edges, leaf_edges, box_edges):
        edges(pair, lambda pair: pair[0].wait_send(), lambda pair: pair[1].wait_send())

    everyone.wait_send()


def local(points, vectors, counts):
    cubes = counts.shape[0]
    nleaf, nsub = lax.axis_size("leaf"), lax.axis_size("sub")
    n = nleaf * nsub
    slab_count = cubes * n
    level_count = slab_count.bit_length() - 2
    cube_levels = cubes.bit_length() - 1
    lengths = term_lengths(slab_count)
    node_values = chebyshev(ORDER)
    leaf_up, leaf_down, box_up, box_down, far = [
        jnp.asarray(np_halves(t)) for t in make_tables(node_values, level_count, lengths)
    ]
    near, pieces = smooth_split(lengths)
    moment_in, moment_out, leaf_far = moment_tables(node_values, near, lengths)
    moment_in, moment_out = [jnp.asarray(np_halves(t)) for t in (moment_in, moment_out)]
    leaf_far = jnp.asarray(leaf_far.astype(np.float32).astype(jnp.bfloat16))
    layers = 2 * cubes
    pairs = cubes // 2
    low_count = sum((pairs >> h) + 2 for h in range(cube_levels))
    top_count = sum((n // 2 >> h) + 2 for h in range(level_count - cube_levels))
    f32, bf16 = jnp.float32, jnp.bfloat16
    tables = (leaf_up, box_up, leaf_down, box_down, far, leaf_far, moment_in, moment_out)
    stay = pl.BlockSpec(memory_space=pltpu.HBM)
    return pl.pallas_call(
        functools.partial(kernel_body, (nleaf, nsub, cubes, level_count), lengths, pieces),
        out_shape=jax.ShapeDtypeStruct(vectors.shape, f32),
        in_specs=[stay, stay, pl.BlockSpec(memory_space=pltpu.SMEM)] + [stay] * len(tables),
        out_specs=pl.BlockSpec(memory_space=pltpu.VMEM),
        scratch_shapes=[
            pltpu.VMEM(points.shape, f32),
            pltpu.VMEM(vectors.shape, f32),
            pltpu.VMEM((64, (layers + 2) * 256), bf16),
            pltpu.VMEM((8, (layers + 2) * 256), f32),
            pltpu.VMEM((2, layers, 2, 128, 128), bf16),
            pltpu.VMEM((128, layers * 256), bf16),
            pltpu.VMEM((layers + 4, 32, 256), bf16),
            pltpu.VMEM((layers + 4, 32, 256), bf16),
            pltpu.VMEM((2, 256, 512), f32),
            pltpu.VMEM((2, 256, 512), bf16),
            pltpu.VMEM((32, (layers + 2) * 256), f32),
            pltpu.VMEM((2, 208, 128), f32),
            pltpu.VMEM((2, 208, 128), f32),
            pltpu.VMEM((2, 32 * cube_levels, 128), f32),
            pltpu.VMEM((2, 32 * cube_levels, 128), f32),
            pltpu.VMEM((2, 8, 128), f32),
            pltpu.VMEM((n, 8, 128), f32),
            pltpu.VMEM((2, 16, 128), f32),
            pltpu.VMEM((low_count, 32, 128), f32),
            pltpu.VMEM((top_count, 16, 128), f32),
            pltpu.VMEM((32, 256), bf16),
            pltpu.VMEM((layers, 32, 256), f32),
        ] + [pltpu.VMEM(t.shape, bf16) for t in tables] + [
            pltpu.SemaphoreType.DMA((6,)),
            pltpu.SemaphoreType.DMA((6,)),
            pltpu.SemaphoreType.DMA((1,)),
            pltpu.SemaphoreType.DMA((1,)),
            pltpu.SemaphoreType.DMA((2,)),
            pltpu.SemaphoreType.DMA((2 + len(tables),)),
        ],
        compiler_params=pltpu.CompilerParams(
            collective_id=0, has_side_effects=True, vmem_limit_bytes=VMEM_BYTES
        ),
    )(points, vectors, counts, *tables)


def solution(mesh):
    in_specs = (P(None, ("leaf", "sub")), P(None, ("leaf", "sub")), P(("leaf", "sub"), None))
    out_specs = P(None, ("leaf", "sub"))
    return jax.shard_map(local, mesh=mesh, in_specs=in_specs, out_specs=out_specs, check_vma=False)
```

```python
import functools
import math

import jax
import jax.numpy as jnp
import numpy as np
from jax import lax
from jax.experimental import pallas as pl
from jax.experimental.pallas import tpu as pltpu
from jax.sharding import PartitionSpec as P

ORDER = 4
FIRST_DEVICES = 2
VMEM_BYTES = 60 * 1024 * 1024


TERM_SCALE = 1.0 / 32.0
ROOT_THREE = math.sqrt(3.0)
far_offsets = (-3, -2, 2, 3)
far_sources = ((0, (0, 4, 5)), (1, (0, 1, 5)))


def term_lengths(slab_count):
    term_count = (slab_count.bit_length() - 1) // 3 + 1
    return [slab_count / 4.0 / 8.0**term_index for term_index in range(term_count)]


def chebyshev(order):
    return np.cos((2.0 * np.arange(order) + 1.0) * np.pi / (2.0 * order))


def lagrange_table(values, node_values):
    columns = []
    for anchor in range(len(node_values)):
        product = values * 0.0 + 1.0
        for against in range(len(node_values)):
            if against != anchor:
                product = (
                    product
                    * (values - node_values[against])
                    / (node_values[anchor] - node_values[against])
                )
        columns.append(product)
    return np.stack(columns, -1)


def grid_nodes(node_values):
    number = len(node_values)
    along_z, along_y, along_x = np.meshgrid(
        np.arange(number), np.arange(number), np.arange(number), indexing="ij"
    )
    return np.stack(
        [node_values[along_x.ravel()], node_values[along_y.ravel()], node_values[along_z.ravel()]],
        -1,
    )


def kernel_table(targets, sources, lengths):
    offsets_xyz = targets[:, None, :] - sources[None, :, :]
    distance = np.sqrt(np.sum(offsets_xyz * offsets_xyz, -1))
    summed_terms = distance * 0.0
    for length in lengths:
        scaled = distance * (ROOT_THREE / length)
        summed_terms = summed_terms + TERM_SCALE / math.sqrt(length) * (1.0 + scaled) * np.exp(
            -scaled
        )
    return summed_terms


def child_tables(node_values):
    halves = [
        lagrange_table(side_offset + 0.5 * node_values, node_values) for side_offset in (-0.5, 0.5)
    ]
    identity = np.eye(len(node_values))
    octant_rows = []
    for depth_index in range(2):
        for row_index in range(2):
            for column_index in range(2):
                octant_rows.append(
                    np.kron(np.kron(halves[depth_index], halves[row_index]), halves[column_index])
                )
    octant_array = np.stack(octant_rows).reshape((2, 2, 2) + octant_rows[0].shape)
    half_array = np.stack(
        [np.kron(np.kron(halves[half_index], identity), identity) for half_index in range(2)]
    )
    return (octant_array, half_array)


def coarse_couplings(node_values, height, lengths):
    span = float(1 << height)
    targets = grid_nodes(node_values) * np.array([0.5, 0.5, 0.5 * span])
    return np.stack(
        [
            kernel_table(targets, targets + np.array([0.0, 0.0, offset * span]), lengths)
            for offset in far_offsets
        ]
    )


def halves_bf16(value):
    high = value.astype(jnp.bfloat16)
    low = (value - high.astype(jnp.float32)).astype(jnp.bfloat16)
    return high, low


def np_halves(table):
    table = np.asarray(table, np.float32)
    high = table.astype(jnp.bfloat16)
    low = (table - high.astype(np.float32)).astype(jnp.bfloat16)
    return np.stack([high, low])


def dot_split(first, second, high, low):
    return jnp.dot(
        jnp.concatenate([first, second, first], 1), jnp.concatenate([high, high, low], 0),
        preferred_element_type=jnp.float32,
    )


def dot3(value, high, low):
    return dot_split(*halves_bf16(value), high, low)


def smooth_split(lengths):
    r = np.linspace(0.0, math.sqrt(3.0) * 1.0005, 2001)
    s = r * r

    def term(length):
        a = r * (ROOT_THREE / length)
        return TERM_SCALE / math.sqrt(length) * (1.0 + a) * np.exp(-a)

    smooth = sum(term(length) for length in lengths[:-1])
    basis = np.stack([np.ones_like(r), s, s * r, s * s], 1)
    weight = np.ones_like(r)
    for _ in range(100):
        root = np.sqrt(weight)
        fitted = np.linalg.lstsq(basis * root[:, None], smooth * root, rcond=None)[0]
        error = np.abs(smooth - basis @ fitted)
        weight = weight * (error / error.max() + 1e-3)
        weight = weight / weight.mean()
    full = smooth + term(lengths[-1])
    low = basis[:, :2]
    c0, c1 = np.linalg.lstsq(low / full[:, None], np.ones_like(r), rcond=None)[0]
    return (float(c0), float(c1)), [float(v) for v in fitted - np.array([c0, c1, 0.0, 0.0])]


def layer_nodes(node_values):
    nodes = grid_nodes(node_values) * 0.25
    return np.concatenate(
        [nodes + np.array([0.5 * c - 0.25, 0.5 * r - 0.25, 0.0]) for r in range(2) for c in range(2)]
    )


def far_split(node_values, step, lengths):
    nodes = layer_nodes(node_values)
    offsets_xyz = nodes[:, None] - nodes[None] - np.array([0.0, 0.0, 0.5 * step])
    squared = np.sum(offsets_xyz * offsets_xyz, -1).ravel()
    table = kernel_table(nodes, nodes + np.array([0.0, 0.0, 0.5 * step]), lengths).ravel()
    basis = np.stack([np.ones_like(squared), squared], 1)
    c0, c1 = np.linalg.lstsq(basis, table, rcond=None)[0]
    return float(c0), float(c1), (table - basis @ np.array([c0, c1])).reshape(len(nodes), -1)


def moment_tables(node_values, near, lengths):
    x, y, d = layer_nodes(node_values).T
    norm = x * x + y * y + d * d
    one = np.ones_like(x)
    gather = np.zeros((len(x), 128))
    spread = np.zeros((128, len(x)))
    for group, step in enumerate(range(-3, 4)):
        c0, c1 = near if abs(step) < 2 else far_split(node_values, step, lengths)[:2]
        source = (
            c0 + c1 * (norm + step * step / 4.0 + step * d), -2.0 * c1 * x, -2.0 * c1 * y,
            -c1 * (2.0 * d + step), c1 * one,
        )
        for index, (column, row) in enumerate(zip(source, (one, x, y, d, norm))):
            gather[:, 8 * group + index] = column
            spread[8 * group + index] = row
    leaf_far = np.stack(
        [
            np.concatenate(
                [far_split(node_values, layer - 2 - depth, lengths)[2].T for layer in layers]
            )
            for depth, layers in far_sources
        ]
    )
    return gather, spread, leaf_far


def lagrange_coefficients(node_values):
    rows = []
    for anchor in range(len(node_values)):
        others = np.delete(node_values, anchor)
        rows.append(np.poly(others)[::-1] / np.prod(node_values[anchor] - others))
    return np.stack(rows)


def make_tables(node_values, level_count, lengths):
    octants, halves = child_tables(node_values)
    rank = ORDER**3
    eight = octants.reshape(8, rank, rank)
    leaf_up = np.zeros((2, 8, rank, 2, rank))
    for parity in range(2):
        leaf_up[parity, :, :, parity, :] = eight
    leaf_up = leaf_up.reshape(16 * rank, 2 * rank)
    leaf_down = leaf_up.T
    box_up = np.zeros((2, 2, rank, 2, rank))
    for parity in range(2):
        box_up[parity, :, :, parity, :] = halves
    box_up = box_up.reshape(2, 2 * rank, 2 * rank)
    box_down = np.swapaxes(box_up, 1, 2)
    far = np.zeros((level_count, 2, 2, rank, 2, rank))
    for height in range(level_count):
        m3, m2, p2, p3 = [c.T for c in coarse_couplings(node_values, height, lengths)]
        far[height, 0, 0, :, 0] = m2
        far[height, 0, 0, :, 1] = m3
        far[height, 0, 1, :, 1] = m2
        far[height, 1, 0, :, 0] = p2
        far[height, 1, 1, :, 0] = p3
        far[height, 1, 1, :, 1] = p2
    far = far.reshape(level_count, 2, 2 * rank, 2 * rank)
    return leaf_up, leaf_down, box_up, box_down, far


def kernel_body(
    dims, lengths, pieces, pts_hbm, vec_hbm, cnt, leaf_up_hbm, box_up_hbm, leaf_down_hbm,
    box_down_hbm, far_hbm, leaf_far_hbm, moment_in_hbm, moment_out_hbm,
    out, pts, vec, mw, pw, bd, b3, lh, ls, r2s, kn, acc, send, recv, send2, recv2, gsend, gath, crossed,
    low_pairs, ups, locs, ll, leaf_up, box_up, leaf_down, box_down, far, leaf_far, moment_in,
    moment_out, send_sems, recv_sems, gsend_sems, grecv_sems, swap_sems, table_sems, product,
    out_sems,
):
    nleaf, nsub, cubes, levels = dims
    n = nleaf * nsub
    layers = 2 * cubes
    cube_levels = cubes.bit_length() - 1
    nodes = chebyshev(ORDER)
    me = lax.axis_index("leaf") * nsub + lax.axis_index("sub")
    mesh_id = pl.DeviceIdType.LOGICAL

    def place(d):
        return d

    copies = [
        pltpu.make_async_copy(source, target, table_sems.at[index])
        for index, (source, target) in enumerate((
            (pts_hbm, pts), (vec_hbm, vec), (leaf_up_hbm, leaf_up), (box_up_hbm, box_up),
            (moment_in_hbm, moment_in), (moment_out_hbm, moment_out), (leaf_far_hbm, leaf_far),
            (far_hbm, far), (box_down_hbm, box_down), (leaf_down_hbm, leaf_down),
        ))
    ]
    for copy in copies:
        copy.start()

    barrier = pltpu.get_barrier_semaphore()

    def greet(k, carry):
        pl.semaphore_signal(
            barrier, inc=1, device_id=place((me + k) & (n - 1)), device_id_type=mesh_id
        )
        return carry

    lax.fori_loop(1, n, greet, 0)

    first_slab = (me * cubes).astype(jnp.float32)
    lane = lax.broadcasted_iota(jnp.int32, (1, 256), 1)
    quarter = lane // 64
    slot = lane - quarter * 64
    centre_x = ((quarter % 2).astype(jnp.float32) + 0.5) * 0.5
    centre_y = ((quarter // 2).astype(jnp.float32) + 0.5) * 0.5
    row8 = lax.broadcasted_iota(jnp.int32, (8, 512), 0)

    def span(z, width=256):
        return pl.ds(pl.multiple_of(z * 256, 256), width)

    def occupancy(z):
        cube, base = z // 2, lax.rem(z, 2) * 4
        limit = jnp.where(
            quarter < 2,
            jnp.where(quarter == 0, cnt[cube, base], cnt[cube, base + 1]),
            jnp.where(quarter == 2, cnt[cube, base + 2], cnt[cube, base + 3]),
        )
        return jnp.where(slot < limit, 1.0, 0.0)

    table = lagrange_coefficients(nodes)
    row16 = lax.broadcasted_iota(jnp.int32, (16, 128), 0)

    def spread_rows(anchor):
        powers = []
        for power in range(ORDER):
            c = [float(v) for v in table[:, power]]
            one = jnp.where(
                anchor < 2, jnp.where(anchor == 0, c[0], c[1]), jnp.where(anchor == 2, c[2], c[3])
            )
            powers.append(jnp.concatenate([one, one], 1))
        return powers

    along_x = spread_rows(row16 % ORDER)
    along_y = spread_rows(row16 // ORDER)
    along_z = [c[0:8] for c in along_x]

    def poly_of(u, powers):
        p0, p1, p2, p3 = powers
        return ((p3 * u + p2) * u + p1) * u + p0

    def basis_of(ux, uy, uz):
        plane = poly_of(ux, along_x) * poly_of(uy, along_y)
        height = poly_of(uz, along_z)
        return halves_bf16(
            jnp.concatenate([plane * height[a : a + 1] for a in range(ORDER)], 0)
        )

    nt = (((1,), (1,)), ((), ()))
    left64 = lax.broadcasted_iota(jnp.int32, (64, 128), 1) < 64
    nothing = jnp.zeros((64, 128), jnp.bfloat16)

    def box_layer(z, carry):
        masked = vec[:, span(z)] * occupancy(z)
        mw[0:32, span(z + 1)], mw[32:64, span(z + 1)] = halves_bf16(masked)
        coords = pts[:, span(z)]
        pw[0:3, span(z + 1)] = coords
        b3[0:64, span(z)], b3[64:128, span(z)] = basis_of(
            coords[0:1] * 2.0 - 1.0, coords[1:2] * 2.0 - 1.0,
            (coords[2:3] - first_slab) * (2.0 / cubes) - 1.0,
        )
        return carry

    def leaf_layer(z, carry):
        coords = pts[:, span(z)]
        depth = (lax.rem(z, 2).astype(jnp.float32) + 0.5) * 0.5
        slab = first_slab + (z // 2).astype(jnp.float32)
        high, low = basis_of(
            (coords[0:1] - centre_x) * 4.0, (coords[1:2] - centre_y) * 4.0,
            ((coords[2:3] - slab) - depth) * 4.0,
        )
        for half in range(2):
            cols = slice(half * 128, half * 128 + 128)
            for which, part in ((0, high[:, cols]), (1, low[:, cols])):
                bd[which, z, half] = jnp.concatenate(
                    [jnp.where(left64, part, nothing), jnp.where(left64, nothing, part)], 0
                )
        return carry

    def couple():
        edge = [0, 1, layers - 2, layers - 1]
        for index, z in enumerate(edge + list(range(2, layers - 2))):
            for half in range(2):
                cols = slice(half * 128, half * 128 + 128)
                at = slice(256 * (z + 1) + half * 128, 256 * (z + 1) + half * 128 + 128)
                main = lax.dot_general(
                    mw[:, at], bd[0, z, half], nt, preferred_element_type=jnp.float32
                )
                rest = lax.dot_general(
                    mw[0:32, at], bd[1, z, half], nt, preferred_element_type=jnp.float32
                )
                coeffs = main[0:32] + main[32:64] + rest
                if z in edge:
                    side, i = (0, z) if z < 2 else (1, z - layers + 2)
                    start = (2 * i + half) * 32
                    send[side, start : start + 32] = coeffs
                lh[z + 2, :, cols], ls[z + 2, :, cols] = halves_bf16(coeffs)
            if index % 2:
                yield

    copies[0].wait()
    copies[1].wait()
    lax.fori_loop(0, layers, box_layer, 0, unroll=4)
    box = lax.dot_general(
        mw[:, 256 : 256 + layers * 256], b3[...], nt, preferred_element_type=jnp.float32
    )

    pairs = cubes // 2
    lane128 = lax.broadcasted_iota(jnp.int32, (16, 128), 1)
    offsets = []
    base = 128
    box = box[0:32] + box[32:64]
    box = box + pltpu.roll(box, 64, 1)
    core = lax.rem(me, 2)
    folded = [
        jnp.where(lane128[0:8] < 64, box[16 * k : 16 * k + 8], box[16 * k + 8 : 16 * k + 16])
        for k in range(2)
    ]
    gsend[0] = folded[0]
    gsend[1] = folded[1]
    gath[me] = jnp.where(core == 0, folded[0], folded[1])

    def rise():
        for copy in copies[2:4]:
            copy.wait()
        flat = []
        for part in (lh, ls):
            own = part[2 : 2 + layers].reshape(pairs, 4, 32, 256)
            flat.append(jnp.concatenate([own[:, i].reshape(pairs * 32, 256) for i in range(4)], 1))
        level = dot_split(*flat, leaf_up[0], leaf_up[1]).reshape(pairs, 32, 128)
        yield
        offset = 0
        for height in range(cube_levels):
            offsets.append(offset)
            count = pairs >> height
            low_pairs[offset + 1 : offset + 1 + count] = level
            send2[0, 32 * height : 32 * height + 32] = level[0]
            send2[1, 32 * height : 32 * height + 32] = level[count - 1]
            offset += count + 2
            if count > 1:
                two = level.reshape(count // 2, 2, 32, 128)
                level = dot3(
                    two[:, 0].reshape(count * 16, 128), box_up[0, 0], box_up[1, 0]
                ) + dot3(two[:, 1].reshape(count * 16, 128), box_up[0, 1], box_up[1, 1])
                level = level.reshape(count // 2, 32, 128)
                yield

    for side, edge in ((0, 0), (1, layers - 1)):
        masked = vec[:, edge * 256 : edge * 256 + 256] * occupancy(jnp.int32(edge))
        coords = pts[:, edge * 256 : edge * 256 + 256]
        for half in range(2):
            cols = slice(half * 128, half * 128 + 128)
            send[side, base + 32 * half : base + 32 + 32 * half] = masked[:, cols]
            send[side, base + 64 + 8 * half : base + 67 + 8 * half] = coords[:, cols]
    pad = jnp.zeros((5, 128), jnp.float32)
    for side in range(2):
        for half in range(2):
            send[side, base + 67 + 8 * half : base + 72 + 8 * half] = pad

    def near_squared(z, p, with_self=True):
        boundary = first_slab + (z + 1).astype(jnp.float32) * 0.5
        block = pw[:, span(z + 1, 512)]
        x = block[0:1] - 0.5
        y = block[1:2] - 0.5
        d = block[2:3] - boundary
        norm = x * x + y * y + d * d
        one = jnp.where(row8 == 4, 1.0, 0.0)
        right = jnp.where(row8 == 0, x, jnp.where(row8 == 1, y, jnp.where(row8 == 2, d,
            jnp.where(row8 == 3, norm, one))))
        swap = jnp.where(row8 == 3, 1.0, jnp.where(row8 == 4, norm, 0.0))
        left = jnp.where(row8 < 3, -2.0 * right, swap)[:, 0:256]

        def thirds(v):
            h = v.astype(jnp.bfloat16).astype(jnp.float32)
            m = (v - h).astype(jnp.bfloat16).astype(jnp.float32)
            return h, m, v - h - m

        rh, rm, rl = thirds(right)
        lh, lm, lo = thirds(left)
        if not with_self:
            rh, rm, rl = rh[:, 256:], rm[:, 256:], rl[:, 256:]
        rs = jnp.concatenate([rh, rm, rh, rl, rm, rh], 0).astype(jnp.bfloat16)
        ls = jnp.concatenate([lh, lh, lm, lh, lm, lo], 0).astype(jnp.bfloat16)
        r2s[p, :, (0 if with_self else 256) : 512] = lax.dot_general(
            ls, rs, (((0,), (0,)), ((), ())), preferred_element_type=jnp.float32
        )

    rate = ROOT_THREE / lengths[-1]
    weight = TERM_SCALE / math.sqrt(lengths[-1])
    d0, d1, q0, q1 = pieces

    def near_kernel(p, with_self=True, filler=None, every=4):
        for chunk in range(16):
            if filler is not None and chunk % every == 0:
                next(filler, None)
            rows = slice(chunk * 16, chunk * 16 + 16)
            c0 = (0 if chunk < 8 else 128) if with_self else 256
            sq = jnp.maximum(r2s[p, rows, c0:512], 1e-20)
            r = sq * lax.rsqrt(sq)
            decay = jnp.exp2(r * (-rate * math.log2(math.e)))
            rest = d0 + sq * (d1 + r * (q0 + r * q1))
            kn[p, rows, c0:512] = ((weight + (weight * rate) * r) * decay + rest).astype(jnp.bfloat16)

    first, second, whole = slice(0, 128), slice(128, 256), slice(0, 256)

    def plain(m, rows, cols, p):
        return jnp.dot(m, kn[p, rows, cols], preferred_element_type=jnp.float32)

    def turned(m, rows, cols, p):
        return lax.dot_general(m, kn[p, rows, cols], nt, preferred_element_type=jnp.float32)

    def near_apply(z, p):
        here = mw[0:32, span(z + 1)]
        there = mw[0:32, span(z + 2)]
        own = plain(here[:, first], first, whole, p)
        low = plain(here[:, second], second, second, p)
        high = turned(here[:, second], first, second, p)
        back = turned(there, whole, slice(256, 512), p)
        acc[:, span(z + 1)] += own + jnp.concatenate([high, low], 1) + back
        acc[:, span(z + 2)] = plain(here, whole, slice(256, 512), p)

    def near_step(z, p, filler=None, every=4):
        near_squared(z + 1, 1 - p)
        near_kernel(p, True, filler, every)
        near_apply(z - 1, 1 - p)

    def near_four(t, carry):
        for i in range(4):
            near_step(4 * t + (i + 1), (i + 1) % 2)
        return carry

    @pl.when(me == 0)
    def _():
        recv[0] = jnp.zeros(recv.shape[1:], jnp.float32)
        recv2[0] = jnp.zeros(recv2.shape[1:], jnp.float32)

    @pl.when(me == n - 1)
    def _():
        recv[1] = jnp.zeros(recv.shape[1:], jnp.float32)
        recv2[1] = jnp.zeros(recv2.shape[1:], jnp.float32)

    def sideways(source, target, rows, first_sem):
        to_left = pltpu.make_async_remote_copy(
            source.at[0, rows], target.at[1, rows],
            send_sems.at[first_sem], recv_sems.at[first_sem + 1],
            device_id=place((me + n - 1) & (n - 1)), device_id_type=mesh_id,
        )
        to_right = pltpu.make_async_remote_copy(
            source.at[1, rows], target.at[0, rows],
            send_sems.at[first_sem + 1], recv_sems.at[first_sem],
            device_id=place((me + 1) & (n - 1)), device_id_type=mesh_id,
        )
        return to_left, to_right

    point_edges = sideways(send, recv, pl.ds(base, 80), 0)
    leaf_edges = sideways(send, recv, pl.ds(0, base), 2)
    box_edges = sideways(send2, recv2, pl.ds(0, 32 * cube_levels), 4)

    def wait_edges(pair):
        edges(pair, lambda pair: pair[1].wait_recv(), lambda pair: pair[0].wait_recv())

    def edges(pair, left_action, right_action):
        @pl.when(me > 0)
        def _():
            left_action(pair)

        @pl.when(me < n - 1)
        def _():
            right_action(pair)

    def start_edges(pair):
        edges(pair, lambda pair: pair[0].start(), lambda pair: pair[1].start())

    def spread(k, target):
        return pltpu.make_async_remote_copy(
            gsend.at[target & 1], gath.at[me], gsend_sems.at[0], grecv_sems.at[0],
            device_id=place(target), device_id_type=mesh_id,
        )

    def spread_start(k, carry):
        spread(k, (me + k) & (n - 1)).start()
        return carry

    def first_sends():
        pl.semaphore_wait(barrier, n - 1)
        lax.fori_loop(1, n, spread_start, 0)
        start_edges(point_edges)

    sooner = me < FIRST_DEVICES

    lax.fori_loop(0, layers, leaf_layer, 0, unroll=4)

    @pl.when(jnp.logical_not(sooner))
    def _():
        first_sends()


    acc[:, 256:512] = jnp.zeros((32, 256), jnp.float32)
    late = layers // 4 - 1

    def climb():
        yield from couple()
        yield from rise()

    rising = climb()
    near_squared(jnp.int32(0), 0)
    near_squared(jnp.int32(1), 1)
    next(rising)
    next(rising)

    @pl.when(jnp.logical_not(sooner))
    def _():
        start_edges(leaf_edges)

    near_kernel(0, True, rising, 1)
    for _ in rising:
        pass

    @pl.when(jnp.logical_not(sooner))
    def _():
        start_edges(box_edges)

    lax.fori_loop(0, 1, near_four, 0)

    @pl.when(sooner)
    def _():
        first_sends()
        start_edges(leaf_edges)
        start_edges(box_edges)

    lax.fori_loop(1, late, near_four, 0)

    def take_points():
        wait_edges(point_edges)
        for side, window in ((0, 0), (1, layers + 1)):
            for half in range(2):
                cols = slice(window * 256 + half * 128, window * 256 + half * 128 + 128)
                masked = recv[side, base + 32 * half : base + 32 + 32 * half]
                mw[0:32, cols] = masked.astype(jnp.bfloat16)
                pw[:, cols] = recv[side, base + 64 + 8 * half : base + 72 + 8 * half]

    def take_leaves():
        wait_edges(leaf_edges)
        for side in range(2):
            for i in range(2):
                at = i if side == 0 else layers + 2 + i
                for half in range(2):
                    start = (2 * i + half) * 32
                    lanes = slice(half * 128, half * 128 + 128)
                    lh[at, :, lanes], ls[at, :, lanes] = halves_bf16(recv[side, start : start + 32])

    def take_boxes():
        wait_edges(box_edges)
        for side in range(2):
            for height in range(cube_levels):
                at = offsets[height] + (0 if side == 0 else (pairs >> height) + 1)
                low_pairs[at] = recv2[side, 32 * height : 32 * height + 32]

    def leaves():
        rows = (layers + 4) * 32
        moments = dot_split(
            lh[...].reshape(rows, 256), ls[...].reshape(rows, 256), moment_in[0], moment_in[1]
        ).reshape(cubes + 2, 2, 32, 128)
        yield
        window = lh[...].reshape(cubes + 2, 2, 32, 256)
        group = lax.broadcasted_iota(jnp.int32, (cubes, 32, 128), 2) // 8
        for depth, sources in far_sources:
            joined = jnp.zeros((cubes, 32, 128), jnp.float32)
            for s in range(6):
                joined = jnp.where(
                    group == s + 1 - depth, moments[s // 2 : s // 2 + cubes, s % 2], joined
                )
            jh, jl = halves_bf16(joined.reshape(cubes * 32, 128))
            total = jnp.dot(
                jnp.concatenate(
                    [jh, jl, jh]
                    + [window[s // 2 : s // 2 + cubes, s % 2].reshape(cubes * 32, 256) for s in sources],
                    1,
                ),
                jnp.concatenate(
                    [moment_out[0], moment_out[0], moment_out[1], leaf_far[depth]], 0
                ),
                preferred_element_type=jnp.float32,
            )
            for j in range(cubes):
                ll[2 * j + depth] = total[32 * j : 32 * j + 32]
            yield

    def lower():
        expansion = None
        for height in reversed(range(cube_levels)):
            count = pairs >> height
            at = offsets[height]
            below = low_pairs[at : at + count].reshape(count * 32, 128)
            above = low_pairs[at + 2 : at + 2 + count].reshape(count * 32, 128)
            here = dot3(below, far[0, height, 0], far[1, height, 0]) + dot3(
                above, far[0, height, 1], far[1, height, 1]
            )
            if expansion is not None:
                below, above = [
                    dot3(expansion, box_down[0, side], box_down[1, side]).reshape(
                        count // 2, 1, 32, 128
                    )
                    for side in range(2)
                ]
                here = here + jnp.concatenate([below, above], 1).reshape(count * 32, 128)
            expansion = here
            yield
        inherited = dot3(expansion, leaf_down[0], leaf_down[1])
        yield
        for i in range(4):
            for j in range(pairs):
                ll[4 * j + i] += inherited[32 * j : 32 * j + 32, 256 * i : 256 * i + 256]
        yield

    partner = me + 1 - 2 * core
    swap = pltpu.make_async_remote_copy(
        crossed.at[core], crossed.at[core], swap_sems.at[0], swap_sems.at[1],
        device_id=place(partner), device_id_type=mesh_id,
    )

    def descend():
        count = n // 2
        blank = jnp.zeros((16, 128), jnp.float32)
        offset = 0
        tops = []
        for height in range(cube_levels, levels):
            tops.append(offset)
            ups[offset] = blank
            ups[offset + count + 1] = blank
            if height == cube_levels:

                folds = gath[...].reshape(count, 2, 8, 128)
                even, odd = folds[:, 0], folds[:, 1]
                near_half = lax.broadcasted_iota(jnp.int32, even.shape, 2) < 64
                ups[1 : 1 + count, 0:8] = jnp.where(near_half, even, pltpu.roll(odd, 64, 2))
                ups[1 : 1 + count, 8:16] = jnp.where(near_half, pltpu.roll(even, 64, 2), odd)
            else:
                two = ups[tops[-2] + 1 : tops[-2] + 1 + 2 * count].reshape(count, 2, 16, 128)
                level = dot3(
                    two[:, 0].reshape(count * 16, 128), box_up[0, 0], box_up[1, 0]
                ) + dot3(two[:, 1].reshape(count * 16, 128), box_up[0, 1], box_up[1, 1])
                ups[offset + 1 : offset + 1 + count] = level.reshape(count, 16, 128)
            offset += count + 2
            count //= 2
            yield

        expansion = None
        for height in range(levels - 1, cube_levels - 1, -1):
            j = me >> (height - cube_levels + 1)
            at = tops[height - cube_levels]
            below, above = ups[at + j], ups[at + j + 2]
            here = dot3(below, far[0, height, 0], far[1, height, 0]) + dot3(
                above, far[0, height, 1], far[1, height, 1]
            )
            if expansion is not None:
                parity = lax.rem(j, 2)
                here = here + dot3(expansion, box_down[0, parity], box_down[1, parity])
            expansion = here
            yield
        crossed[core] = expansion
        swap.start()

    def join_halves():
        swap.wait_recv()
        both = jnp.concatenate([crossed[0], crossed[1]], 0)
        wide = lax.broadcasted_iota(jnp.int32, (32, 128), 1) < 64
        turned_round = pltpu.roll(both, 64, 1)
        own = jnp.where(wide == (core == 0), both, turned_round)
        high, low = halves_bf16(own)
        locs[...] = jnp.concatenate([high, low], 1)

    def settle():
        for z in range(layers):
            lhigh, llow = halves_bf16(ll[z])
            both = jnp.concatenate([lhigh, llow], 0)
            parts = []
            for half in range(2):
                cols = slice(half * 128, half * 128 + 128)
                main = jnp.dot(both[:, cols], bd[0, z, half], preferred_element_type=jnp.float32)
                rest = jnp.dot(lhigh[:, cols], bd[1, z, half], preferred_element_type=jnp.float32)
                parts.append(main[0:32] + main[32:64] + rest)
            acc[:, 256 * (z + 1) : 256 * (z + 2)] += jnp.concatenate(parts, 1)
            if z % 2:
                yield

    for copy in copies[4:]:
        copy.wait()
    near_step(jnp.int32(layers - 3), 1)
    take_points()
    near_step(jnp.int32(layers - 2), 0)
    near_squared(jnp.int32(-1), 0, False)
    near_apply(jnp.int32(layers - 2), 0)
    near_kernel(1)
    near_kernel(0, False)
    near_apply(jnp.int32(layers - 1), 1)
    acc[:, 256:512] += plain(mw[0:32, 0:256], whole, slice(256, 512), 0)
    take_leaves()
    everyone = pltpu.make_async_remote_copy(
        gath.at[pl.ds(0, n - 1)], gath.at[pl.ds(0, n - 1)], gsend_sems.at[0], grecv_sems.at[0],
        device_id=place(partner), device_id_type=mesh_id,
    )
    everyone.wait_recv()
    take_boxes()
    parts = [descend(), leaves(), lower()]
    while parts:
        for part in list(parts):
            try:
                next(part)
            except StopIteration:
                parts.remove(part)
    for _ in settle():
        pass
    join_halves()

    def finish(z):
        value = acc[:, span(z + 1)] + jnp.dot(
            locs[:, 0:192],
            jnp.concatenate([b3[:, span(z)], b3[0:64, span(z)]], 0),
            preferred_element_type=jnp.float32,
        )
        product[:, span(z)] = value * occupancy(z)

    def leave(part):
        cols = span(part * 4, 1024)
        return pltpu.make_async_copy(product.at[:, cols], out.at[:, cols], out_sems.at[part])

    def finish_four(part, carry):
        for i in range(4):
            finish(part * 4 + i)
        leave(part).start()
        return carry

    lax.fori_loop(0, layers // 4, finish_four, 0)

    def leave_wait(part, carry):
        leave(part).wait()
        return carry

    lax.fori_loop(0, layers // 4, leave_wait, 0)
    swap.wait_send()
    for pair in (point_edges, leaf_edges, box_edges):
        edges(pair, lambda pair: pair[0].wait_send(), lambda pair: pair[1].wait_send())

    everyone.wait_send()


def local(points, vectors, counts):
    cubes = counts.shape[0]
    nleaf, nsub = lax.axis_size("leaf"), lax.axis_size("sub")
    n = nleaf * nsub
    slab_count = cubes * n
    level_count = slab_count.bit_length() - 2
    cube_levels = cubes.bit_length() - 1
    lengths = term_lengths(slab_count)
    node_values = chebyshev(ORDER)
    leaf_up, leaf_down, box_up, box_down, far = [
        jnp.asarray(np_halves(t)) for t in make_tables(node_values, level_count, lengths)
    ]
    near, pieces = smooth_split(lengths)
    moment_in, moment_out, leaf_far = moment_tables(node_values, near, lengths)
    moment_in, moment_out = [jnp.asarray(np_halves(t)) for t in (moment_in, moment_out)]
    leaf_far = jnp.asarray(leaf_far.astype(np.float32).astype(jnp.bfloat16))
    layers = 2 * cubes
    pairs = cubes // 2
    low_count = sum((pairs >> h) + 2 for h in range(cube_levels))
    top_count = sum((n // 2 >> h) + 2 for h in range(level_count - cube_levels))
    f32, bf16 = jnp.float32, jnp.bfloat16
    tables = (leaf_up, box_up, leaf_down, box_down, far, leaf_far, moment_in, moment_out)
    stay = pl.BlockSpec(memory_space=pltpu.HBM)
    return pl.pallas_call(
        functools.partial(kernel_body, (nleaf, nsub, cubes, level_count), lengths, pieces),
        out_shape=jax.ShapeDtypeStruct(vectors.shape, f32),
        in_specs=[stay, stay, pl.BlockSpec(memory_space=pltpu.SMEM)] + [stay] * len(tables),
        out_specs=stay,
        scratch_shapes=[
            pltpu.VMEM(points.shape, f32),
            pltpu.VMEM(vectors.shape, f32),
            pltpu.VMEM((64, (layers + 2) * 256), bf16),
            pltpu.VMEM((8, (layers + 2) * 256), f32),
            pltpu.VMEM((2, layers, 2, 128, 128), bf16),
            pltpu.VMEM((128, layers * 256), bf16),
            pltpu.VMEM((layers + 4, 32, 256), bf16),
            pltpu.VMEM((layers + 4, 32, 256), bf16),
            pltpu.VMEM((2, 256, 512), f32),
            pltpu.VMEM((2, 256, 512), bf16),
            pltpu.VMEM((32, (layers + 2) * 256), f32),
            pltpu.VMEM((2, 208, 128), f32),
            pltpu.VMEM((2, 208, 128), f32),
            pltpu.VMEM((2, 32 * cube_levels, 128), f32),
            pltpu.VMEM((2, 32 * cube_levels, 128), f32),
            pltpu.VMEM((2, 8, 128), f32),
            pltpu.VMEM((n, 8, 128), f32),
            pltpu.VMEM((2, 16, 128), f32),
            pltpu.VMEM((low_count, 32, 128), f32),
            pltpu.VMEM((top_count, 16, 128), f32),
            pltpu.VMEM((32, 256), bf16),
            pltpu.VMEM((layers, 32, 256), f32),
        ] + [pltpu.VMEM(t.shape, bf16) for t in tables] + [
            pltpu.SemaphoreType.DMA((6,)),
            pltpu.SemaphoreType.DMA((6,)),
            pltpu.SemaphoreType.DMA((1,)),
            pltpu.SemaphoreType.DMA((1,)),
            pltpu.SemaphoreType.DMA((2,)),
            pltpu.SemaphoreType.DMA((2 + len(tables),)),
            pltpu.VMEM(vectors.shape, f32),
            pltpu.SemaphoreType.DMA((layers // 4,)),
        ],
        compiler_params=pltpu.CompilerParams(
            collective_id=0, has_side_effects=True, vmem_limit_bytes=VMEM_BYTES
        ),
    )(points, vectors, counts, *tables)


def solution(mesh):
    in_specs = (P(None, ("leaf", "sub")), P(None, ("leaf", "sub")), P(("leaf", "sub"), None))
    out_specs = P(None, ("leaf", "sub"))
    return jax.shard_map(local, mesh=mesh, in_specs=in_specs, out_specs=out_specs, check_vma=False)
```

```python
import functools
import math

import jax
import jax.numpy as jnp
import numpy as np
from jax import lax
from jax.experimental import pallas as pl
from jax.experimental.pallas import tpu as pltpu
from jax.sharding import PartitionSpec as P

ORDER = 4
FIRST_DEVICES = 2
VMEM_BYTES = 40 * 1024 * 1024


TERM_SCALE = 1.0 / 32.0
ROOT_THREE = math.sqrt(3.0)
far_offsets = (-3, -2, 2, 3)
far_sources = ((0, (0, 4, 5)), (1, (0, 1, 5)))


def term_lengths(slab_count):
    term_count = (slab_count.bit_length() - 1) // 3 + 1
    return [slab_count / 4.0 / 8.0**term_index for term_index in range(term_count)]


def chebyshev(order):
    return np.cos((2.0 * np.arange(order) + 1.0) * np.pi / (2.0 * order))


def lagrange_table(values, node_values):
    columns = []
    for anchor in range(len(node_values)):
        product = values * 0.0 + 1.0
        for against in range(len(node_values)):
            if against != anchor:
                product = (
                    product
                    * (values - node_values[against])
                    / (node_values[anchor] - node_values[against])
                )
        columns.append(product)
    return np.stack(columns, -1)


def grid_nodes(node_values):
    number = len(node_values)
    along_z, along_y, along_x = np.meshgrid(
        np.arange(number), np.arange(number), np.arange(number), indexing="ij"
    )
    return np.stack(
        [node_values[along_x.ravel()], node_values[along_y.ravel()], node_values[along_z.ravel()]],
        -1,
    )


def kernel_table(targets, sources, lengths):
    offsets_xyz = targets[:, None, :] - sources[None, :, :]
    distance = np.sqrt(np.sum(offsets_xyz * offsets_xyz, -1))
    summed_terms = distance * 0.0
    for length in lengths:
        scaled = distance * (ROOT_THREE / length)
        summed_terms = summed_terms + TERM_SCALE / math.sqrt(length) * (1.0 + scaled) * np.exp(
            -scaled
        )
    return summed_terms


def child_tables(node_values):
    halves = [
        lagrange_table(side_offset + 0.5 * node_values, node_values) for side_offset in (-0.5, 0.5)
    ]
    identity = np.eye(len(node_values))
    octant_rows = []
    for depth_index in range(2):
        for row_index in range(2):
            for column_index in range(2):
                octant_rows.append(
                    np.kron(np.kron(halves[depth_index], halves[row_index]), halves[column_index])
                )
    octant_array = np.stack(octant_rows).reshape((2, 2, 2) + octant_rows[0].shape)
    half_array = np.stack(
        [np.kron(np.kron(halves[half_index], identity), identity) for half_index in range(2)]
    )
    return (octant_array, half_array)


def coarse_couplings(node_values, height, lengths):
    span = float(1 << height)
    targets = grid_nodes(node_values) * np.array([0.5, 0.5, 0.5 * span])
    return np.stack(
        [
            kernel_table(targets, targets + np.array([0.0, 0.0, offset * span]), lengths)
            for offset in far_offsets
        ]
    )


def halves_bf16(value):
    high = value.astype(jnp.bfloat16)
    low = (value - high.astype(jnp.float32)).astype(jnp.bfloat16)
    return high, low


def np_halves(table):
    table = np.asarray(table, np.float32)
    high = table.astype(jnp.bfloat16)
    low = (table - high.astype(np.float32)).astype(jnp.bfloat16)
    return np.stack([high, low])


def dot_split(first, second, high, low):
    return jnp.dot(
        jnp.concatenate([first, second, first], 1), jnp.concatenate([high, high, low], 0),
        preferred_element_type=jnp.float32,
    )


def dot3(value, high, low):
    return dot_split(*halves_bf16(value), high, low)


def smooth_split(lengths):
    r = np.linspace(0.0, math.sqrt(3.0) * 1.0005, 2001)
    s = r * r

    def term(length):
        a = r * (ROOT_THREE / length)
        return TERM_SCALE / math.sqrt(length) * (1.0 + a) * np.exp(-a)

    smooth = sum(term(length) for length in lengths[:-1])
    basis = np.stack([np.ones_like(r), s, s * r, s * s], 1)
    weight = np.ones_like(r)
    for _ in range(100):
        root = np.sqrt(weight)
        fitted = np.linalg.lstsq(basis * root[:, None], smooth * root, rcond=None)[0]
        error = np.abs(smooth - basis @ fitted)
        weight = weight * (error / error.max() + 1e-3)
        weight = weight / weight.mean()
    full = smooth + term(lengths[-1])
    low = basis[:, :2]
    c0, c1 = np.linalg.lstsq(low / full[:, None], np.ones_like(r), rcond=None)[0]
    return (float(c0), float(c1)), [float(v) for v in fitted - np.array([c0, c1, 0.0, 0.0])]


def layer_nodes(node_values):
    nodes = grid_nodes(node_values) * 0.25
    return np.concatenate(
        [nodes + np.array([0.5 * c - 0.25, 0.5 * r - 0.25, 0.0]) for r in range(2) for c in range(2)]
    )


def far_split(node_values, step, lengths):
    nodes = layer_nodes(node_values)
    offsets_xyz = nodes[:, None] - nodes[None] - np.array([0.0, 0.0, 0.5 * step])
    squared = np.sum(offsets_xyz * offsets_xyz, -1).ravel()
    table = kernel_table(nodes, nodes + np.array([0.0, 0.0, 0.5 * step]), lengths).ravel()
    basis = np.stack([np.ones_like(squared), squared], 1)
    c0, c1 = np.linalg.lstsq(basis, table, rcond=None)[0]
    return float(c0), float(c1), (table - basis @ np.array([c0, c1])).reshape(len(nodes), -1)


def moment_tables(node_values, near, lengths):
    x, y, d = layer_nodes(node_values).T
    norm = x * x + y * y + d * d
    one = np.ones_like(x)
    gather = np.zeros((len(x), 128))
    spread = np.zeros((128, len(x)))
    for group, step in enumerate(range(-3, 4)):
        c0, c1 = near if abs(step) < 2 else far_split(node_values, step, lengths)[:2]
        source = (
            c0 + c1 * (norm + step * step / 4.0 + step * d), -2.0 * c1 * x, -2.0 * c1 * y,
            -c1 * (2.0 * d + step), c1 * one,
        )
        for index, (column, row) in enumerate(zip(source, (one, x, y, d, norm))):
            gather[:, 8 * group + index] = column
            spread[8 * group + index] = row
    leaf_far = np.stack(
        [
            np.concatenate(
                [far_split(node_values, layer - 2 - depth, lengths)[2].T for layer in layers]
            )
            for depth, layers in far_sources
        ]
    )
    return gather, spread, leaf_far


def lagrange_coefficients(node_values):
    rows = []
    for anchor in range(len(node_values)):
        others = np.delete(node_values, anchor)
        rows.append(np.poly(others)[::-1] / np.prod(node_values[anchor] - others))
    return np.stack(rows)


def make_tables(node_values, level_count, lengths):
    octants, halves = child_tables(node_values)
    rank = ORDER**3
    eight = octants.reshape(8, rank, rank)
    leaf_up = np.zeros((2, 8, rank, 2, rank))
    for parity in range(2):
        leaf_up[parity, :, :, parity, :] = eight
    leaf_up = leaf_up.reshape(16 * rank, 2 * rank)
    leaf_down = leaf_up.T
    box_up = np.zeros((2, 2, rank, 2, rank))
    for parity in range(2):
        box_up[parity, :, :, parity, :] = halves
    box_up = box_up.reshape(2, 2 * rank, 2 * rank)
    box_down = np.swapaxes(box_up, 1, 2)
    far = np.zeros((level_count, 2, 2, rank, 2, rank))
    for height in range(level_count):
        m3, m2, p2, p3 = [c.T for c in coarse_couplings(node_values, height, lengths)]
        far[height, 0, 0, :, 0] = m2
        far[height, 0, 0, :, 1] = m3
        far[height, 0, 1, :, 1] = m2
        far[height, 1, 0, :, 0] = p2
        far[height, 1, 1, :, 0] = p3
        far[height, 1, 1, :, 1] = p2
    far = far.reshape(level_count, 2, 2 * rank, 2 * rank)
    return leaf_up, leaf_down, box_up, box_down, far


def kernel_body(
    dims, lengths, pieces, pts_hbm, vec_hbm, cnt_hbm, leaf_up_hbm, box_up_hbm, leaf_down_hbm,
    box_down_hbm, far_hbm, leaf_far_hbm, moment_in_hbm, moment_out_hbm,
    out, pts, vec, cnt, mw, pw, bd, b3, lh, ls, r2s, kn, acc, send, recv, send2, recv2, gsend, gath, crossed,
    low_pairs, ups, locs, ll, leaf_up, box_up, leaf_down, box_down, far, leaf_far, moment_in,
    moment_out, send_sems, recv_sems, gsend_sems, grecv_sems, swap_sems, table_sems,
):
    nleaf, nsub, cubes, levels = dims
    n = nleaf * nsub
    layers = 2 * cubes
    cube_levels = cubes.bit_length() - 1
    nodes = chebyshev(ORDER)
    me = lax.axis_index("leaf") * nsub + lax.axis_index("sub")
    mesh_id = pl.DeviceIdType.LOGICAL

    def place(d):
        return d

    copies = [
        pltpu.make_async_copy(source, target, table_sems.at[index])
        for index, (source, target) in enumerate((
            (cnt_hbm, cnt), (pts_hbm, pts), (vec_hbm, vec), (leaf_up_hbm, leaf_up), (box_up_hbm, box_up),
            (moment_in_hbm, moment_in), (moment_out_hbm, moment_out), (leaf_far_hbm, leaf_far),
            (far_hbm, far), (box_down_hbm, box_down), (leaf_down_hbm, leaf_down),
        ))
    ]
    for copy in copies:
        copy.start()

    barrier = pltpu.get_barrier_semaphore()

    def greet(k, carry):
        pl.semaphore_signal(
            barrier, inc=1, device_id=place((me + k) & (n - 1)), device_id_type=mesh_id
        )
        return carry

    lax.fori_loop(1, n, greet, 0)

    first_slab = (me * cubes).astype(jnp.float32)
    lane = lax.broadcasted_iota(jnp.int32, (1, 256), 1)
    quarter = lane // 64
    slot = lane - quarter * 64
    centre_x = ((quarter % 2).astype(jnp.float32) + 0.5) * 0.5
    centre_y = ((quarter // 2).astype(jnp.float32) + 0.5) * 0.5
    row8 = lax.broadcasted_iota(jnp.int32, (8, 512), 0)

    def span(z, width=256):
        return pl.ds(pl.multiple_of(z * 256, 256), width)

    def occupancy(z):
        cube, base = z // 2, lax.rem(z, 2) * 4
        limit = jnp.where(
            quarter < 2,
            jnp.where(quarter == 0, cnt[cube, base], cnt[cube, base + 1]),
            jnp.where(quarter == 2, cnt[cube, base + 2], cnt[cube, base + 3]),
        )
        return jnp.where(slot < limit, 1.0, 0.0)

    table = lagrange_coefficients(nodes)
    row16 = lax.broadcasted_iota(jnp.int32, (16, 128), 0)

    def spread_rows(anchor):
        powers = []
        for power in range(ORDER):
            c = [float(v) for v in table[:, power]]
            one = jnp.where(
                anchor < 2, jnp.where(anchor == 0, c[0], c[1]), jnp.where(anchor == 2, c[2], c[3])
            )
            powers.append(jnp.concatenate([one, one], 1))
        return powers

    along_x = spread_rows(row16 % ORDER)
    along_y = spread_rows(row16 // ORDER)
    along_z = [c[0:8] for c in along_x]

    def poly_of(u, powers):
        p0, p1, p2, p3 = powers
        return ((p3 * u + p2) * u + p1) * u + p0

    def basis_of(ux, uy, uz):
        plane = poly_of(ux, along_x) * poly_of(uy, along_y)
        height = poly_of(uz, along_z)
        return halves_bf16(
            jnp.concatenate([plane * height[a : a + 1] for a in range(ORDER)], 0)
        )

    nt = (((1,), (1,)), ((), ()))
    left64 = lax.broadcasted_iota(jnp.int32, (64, 128), 1) < 64
    nothing = jnp.zeros((64, 128), jnp.bfloat16)

    def box_layer(z, carry):
        masked = vec[:, span(z)] * occupancy(z)
        mw[0:32, span(z + 1)], mw[32:64, span(z + 1)] = halves_bf16(masked)
        coords = pts[:, span(z)]
        pw[0:3, span(z + 1)] = coords
        b3[0:64, span(z)], b3[64:128, span(z)] = basis_of(
            coords[0:1] * 2.0 - 1.0, coords[1:2] * 2.0 - 1.0,
            (coords[2:3] - first_slab) * (2.0 / cubes) - 1.0,
        )
        return carry

    def leaf_layer(z, carry):
        coords = pts[:, span(z)]
        depth = (lax.rem(z, 2).astype(jnp.float32) + 0.5) * 0.5
        slab = first_slab + (z // 2).astype(jnp.float32)
        high, low = basis_of(
            (coords[0:1] - centre_x) * 4.0, (coords[1:2] - centre_y) * 4.0,
            ((coords[2:3] - slab) - depth) * 4.0,
        )
        for half in range(2):
            cols = slice(half * 128, half * 128 + 128)
            for which, part in ((0, high[:, cols]), (1, low[:, cols])):
                bd[which, z, half] = jnp.concatenate(
                    [jnp.where(left64, part, nothing), jnp.where(left64, nothing, part)], 0
                )
        return carry

    def couple():
        edge = [0, 1, layers - 2, layers - 1]
        for index, z in enumerate(edge + list(range(2, layers - 2))):
            for half in range(2):
                cols = slice(half * 128, half * 128 + 128)
                at = slice(256 * (z + 1) + half * 128, 256 * (z + 1) + half * 128 + 128)
                main = lax.dot_general(
                    mw[:, at], bd[0, z, half], nt, preferred_element_type=jnp.float32
                )
                rest = lax.dot_general(
                    mw[0:32, at], bd[1, z, half], nt, preferred_element_type=jnp.float32
                )
                coeffs = main[0:32] + main[32:64] + rest
                if z in edge:
                    side, i = (0, z) if z < 2 else (1, z - layers + 2)
                    start = (2 * i + half) * 32
                    send[side, start : start + 32] = coeffs
                lh[z + 2, :, cols], ls[z + 2, :, cols] = halves_bf16(coeffs)
            if index % 2:
                yield

    for copy in copies[0:3]:
        copy.wait()
    lax.fori_loop(0, layers, box_layer, 0, unroll=4)
    box = lax.dot_general(
        mw[:, 256 : 256 + layers * 256], b3[...], nt, preferred_element_type=jnp.float32
    )

    pairs = cubes // 2
    lane128 = lax.broadcasted_iota(jnp.int32, (16, 128), 1)
    offsets = []
    base = 128
    box = box[0:32] + box[32:64]
    box = box + pltpu.roll(box, 64, 1)
    core = lax.rem(me, 2)
    folded = [
        jnp.where(lane128[0:8] < 64, box[16 * k : 16 * k + 8], box[16 * k + 8 : 16 * k + 16])
        for k in range(2)
    ]
    gsend[0] = folded[0]
    gsend[1] = folded[1]
    gath[me] = jnp.where(core == 0, folded[0], folded[1])

    def rise():
        for copy in copies[3:5]:
            copy.wait()
        flat = []
        for part in (lh, ls):
            own = part[2 : 2 + layers].reshape(pairs, 4, 32, 256)
            flat.append(jnp.concatenate([own[:, i].reshape(pairs * 32, 256) for i in range(4)], 1))
        level = dot_split(*flat, leaf_up[0], leaf_up[1]).reshape(pairs, 32, 128)
        yield
        offset = 0
        for height in range(cube_levels):
            offsets.append(offset)
            count = pairs >> height
            low_pairs[offset + 1 : offset + 1 + count] = level
            send2[0, 32 * height : 32 * height + 32] = level[0]
            send2[1, 32 * height : 32 * height + 32] = level[count - 1]
            offset += count + 2
            if count > 1:
                two = level.reshape(count // 2, 2, 32, 128)
                level = dot3(
                    two[:, 0].reshape(count * 16, 128), box_up[0, 0], box_up[1, 0]
                ) + dot3(two[:, 1].reshape(count * 16, 128), box_up[0, 1], box_up[1, 1])
                level = level.reshape(count // 2, 32, 128)
                yield

    for side, edge in ((0, 0), (1, layers - 1)):
        masked = vec[:, edge * 256 : edge * 256 + 256] * occupancy(jnp.int32(edge))
        coords = pts[:, edge * 256 : edge * 256 + 256]
        for half in range(2):
            cols = slice(half * 128, half * 128 + 128)
            send[side, base + 32 * half : base + 32 + 32 * half] = masked[:, cols]
            send[side, base + 64 + 8 * half : base + 67 + 8 * half] = coords[:, cols]
    pad = jnp.zeros((5, 128), jnp.float32)
    for side in range(2):
        for half in range(2):
            send[side, base + 67 + 8 * half : base + 72 + 8 * half] = pad

    def near_squared(z, p, with_self=True):
        boundary = first_slab + (z + 1).astype(jnp.float32) * 0.5
        block = pw[:, span(z + 1, 512)]
        x = block[0:1] - 0.5
        y = block[1:2] - 0.5
        d = block[2:3] - boundary
        norm = x * x + y * y + d * d
        one = jnp.where(row8 == 4, 1.0, 0.0)
        right = jnp.where(row8 == 0, x, jnp.where(row8 == 1, y, jnp.where(row8 == 2, d,
            jnp.where(row8 == 3, norm, one))))
        swap = jnp.where(row8 == 3, 1.0, jnp.where(row8 == 4, norm, 0.0))
        left = jnp.where(row8 < 3, -2.0 * right, swap)[:, 0:256]

        def thirds(v):
            h = v.astype(jnp.bfloat16).astype(jnp.float32)
            m = (v - h).astype(jnp.bfloat16).astype(jnp.float32)
            return h, m, v - h - m

        rh, rm, rl = thirds(right)
        lh, lm, lo = thirds(left)
        if not with_self:
            rh, rm, rl = rh[:, 256:], rm[:, 256:], rl[:, 256:]
        rs = jnp.concatenate([rh, rm, rh, rl, rm, rh], 0).astype(jnp.bfloat16)
        ls = jnp.concatenate([lh, lh, lm, lh, lm, lo], 0).astype(jnp.bfloat16)
        r2s[p, :, (0 if with_self else 256) : 512] = lax.dot_general(
            ls, rs, (((0,), (0,)), ((), ())), preferred_element_type=jnp.float32
        )

    rate = ROOT_THREE / lengths[-1]
    weight = TERM_SCALE / math.sqrt(lengths[-1])
    d0, d1, q0, q1 = pieces

    def near_kernel(p, with_self=True, filler=None, every=4):
        for chunk in range(16):
            if filler is not None and chunk % every == 0:
                next(filler, None)
            rows = slice(chunk * 16, chunk * 16 + 16)
            c0 = (0 if chunk < 8 else 128) if with_self else 256
            sq = jnp.maximum(r2s[p, rows, c0:512], 1e-20)
            r = sq * lax.rsqrt(sq)
            decay = jnp.exp2(r * (-rate * math.log2(math.e)))
            rest = d0 + sq * (d1 + r * (q0 + r * q1))
            kn[p, rows, c0:512] = ((weight + (weight * rate) * r) * decay + rest).astype(jnp.bfloat16)

    first, second, whole = slice(0, 128), slice(128, 256), slice(0, 256)

    def plain(m, rows, cols, p):
        return jnp.dot(m, kn[p, rows, cols], preferred_element_type=jnp.float32)

    def turned(m, rows, cols, p):
        return lax.dot_general(m, kn[p, rows, cols], nt, preferred_element_type=jnp.float32)

    def near_apply(z, p):
        here = mw[0:32, span(z + 1)]
        there = mw[0:32, span(z + 2)]
        own = plain(here[:, first], first, whole, p)
        low = plain(here[:, second], second, second, p)
        high = turned(here[:, second], first, second, p)
        back = turned(there, whole, slice(256, 512), p)
        acc[:, span(z + 1)] += own + jnp.concatenate([high, low], 1) + back
        acc[:, span(z + 2)] = plain(here, whole, slice(256, 512), p)

    def near_step(z, p, filler=None, every=4):
        near_squared(z + 1, 1 - p)
        near_kernel(p, True, filler, every)
        near_apply(z - 1, 1 - p)

    def near_four(t, carry):
        for i in range(4):
            near_step(4 * t + (i + 1), (i + 1) % 2)
        return carry

    @pl.when(me == 0)
    def _():
        recv[0] = jnp.zeros(recv.shape[1:], jnp.float32)
        recv2[0] = jnp.zeros(recv2.shape[1:], jnp.float32)

    @pl.when(me == n - 1)
    def _():
        recv[1] = jnp.zeros(recv.shape[1:], jnp.float32)
        recv2[1] = jnp.zeros(recv2.shape[1:], jnp.float32)

    def sideways(source, target, rows, first_sem):
        to_left = pltpu.make_async_remote_copy(
            source.at[0, rows], target.at[1, rows],
            send_sems.at[first_sem], recv_sems.at[first_sem + 1],
            device_id=place((me + n - 1) & (n - 1)), device_id_type=mesh_id,
        )
        to_right = pltpu.make_async_remote_copy(
            source.at[1, rows], target.at[0, rows],
            send_sems.at[first_sem + 1], recv_sems.at[first_sem],
            device_id=place((me + 1) & (n - 1)), device_id_type=mesh_id,
        )
        return to_left, to_right

    point_edges = sideways(send, recv, pl.ds(base, 80), 0)
    leaf_edges = sideways(send, recv, pl.ds(0, base), 2)
    box_edges = sideways(send2, recv2, pl.ds(0, 32 * cube_levels), 4)

    def wait_edges(pair):
        edges(pair, lambda pair: pair[1].wait_recv(), lambda pair: pair[0].wait_recv())

    def edges(pair, left_action, right_action):
        @pl.when(me > 0)
        def _():
            left_action(pair)

        @pl.when(me < n - 1)
        def _():
            right_action(pair)

    def start_edges(pair):
        edges(pair, lambda pair: pair[0].start(), lambda pair: pair[1].start())

    def spread(k, target):
        return pltpu.make_async_remote_copy(
            gsend.at[target & 1], gath.at[me], gsend_sems.at[0], grecv_sems.at[0],
            device_id=place(target), device_id_type=mesh_id,
        )

    def spread_start(k, carry):
        spread(k, (me + k) & (n - 1)).start()
        return carry

    def first_sends():
        pl.semaphore_wait(barrier, n - 1)
        lax.fori_loop(1, n, spread_start, 0)
        start_edges(point_edges)

    sooner = me < FIRST_DEVICES

    lax.fori_loop(0, layers, leaf_layer, 0, unroll=4)

    @pl.when(jnp.logical_not(sooner))
    def _():
        first_sends()


    acc[:, 256:512] = jnp.zeros((32, 256), jnp.float32)
    late = layers // 4 - 1

    def climb():
        yield from couple()
        yield from rise()

    rising = climb()
    near_squared(jnp.int32(0), 0)
    near_squared(jnp.int32(1), 1)
    next(rising)
    next(rising)

    @pl.when(jnp.logical_not(sooner))
    def _():
        start_edges(leaf_edges)

    near_kernel(0, True, rising, 1)
    for _ in rising:
        pass

    @pl.when(jnp.logical_not(sooner))
    def _():
        start_edges(box_edges)

    lax.fori_loop(0, 1, near_four, 0)

    @pl.when(sooner)
    def _():
        first_sends()
        start_edges(leaf_edges)
        start_edges(box_edges)

    lax.fori_loop(1, late, near_four, 0)

    def take_points():
        wait_edges(point_edges)
        for side, window in ((0, 0), (1, layers + 1)):
            for half in range(2):
                cols = slice(window * 256 + half * 128, window * 256 + half * 128 + 128)
                masked = recv[side, base + 32 * half : base + 32 + 32 * half]
                mw[0:32, cols] = masked.astype(jnp.bfloat16)
                pw[:, cols] = recv[side, base + 64 + 8 * half : base + 72 + 8 * half]

    def take_leaves():
        wait_edges(leaf_edges)
        for side in range(2):
            for i in range(2):
                at = i if side == 0 else layers + 2 + i
                for half in range(2):
                    start = (2 * i + half) * 32
                    lanes = slice(half * 128, half * 128 + 128)
                    lh[at, :, lanes], ls[at, :, lanes] = halves_bf16(recv[side, start : start + 32])

    def take_boxes():
        wait_edges(box_edges)
        for side in range(2):
            for height in range(cube_levels):
                at = offsets[height] + (0 if side == 0 else (pairs >> height) + 1)
                low_pairs[at] = recv2[side, 32 * height : 32 * height + 32]

    def leaves():
        rows = (layers + 4) * 32
        moments = dot_split(
            lh[...].reshape(rows, 256), ls[...].reshape(rows, 256), moment_in[0], moment_in[1]
        ).reshape(cubes + 2, 2, 32, 128)
        yield
        window = lh[...].reshape(cubes + 2, 2, 32, 256)
        group = lax.broadcasted_iota(jnp.int32, (cubes, 32, 128), 2) // 8
        for depth, sources in far_sources:
            joined = jnp.zeros((cubes, 32, 128), jnp.float32)
            for s in range(6):
                joined = jnp.where(
                    group == s + 1 - depth, moments[s // 2 : s // 2 + cubes, s % 2], joined
                )
            jh, jl = halves_bf16(joined.reshape(cubes * 32, 128))
            total = jnp.dot(
                jnp.concatenate(
                    [jh, jl, jh]
                    + [window[s // 2 : s // 2 + cubes, s % 2].reshape(cubes * 32, 256) for s in sources],
                    1,
                ),
                jnp.concatenate(
                    [moment_out[0], moment_out[0], moment_out[1], leaf_far[depth]], 0
                ),
                preferred_element_type=jnp.float32,
            )
            for j in range(cubes):
                ll[2 * j + depth] = total[32 * j : 32 * j + 32]
            yield

    def lower():
        expansion = None
        for height in reversed(range(cube_levels)):
            count = pairs >> height
            at = offsets[height]
            below = low_pairs[at : at + count].reshape(count * 32, 128)
            above = low_pairs[at + 2 : at + 2 + count].reshape(count * 32, 128)
            here = dot3(below, far[0, height, 0], far[1, height, 0]) + dot3(
                above, far[0, height, 1], far[1, height, 1]
            )
            if expansion is not None:
                below, above = [
                    dot3(expansion, box_down[0, side], box_down[1, side]).reshape(
                        count // 2, 1, 32, 128
                    )
                    for side in range(2)
                ]
                here = here + jnp.concatenate([below, above], 1).reshape(count * 32, 128)
            expansion = here
            yield
        inherited = dot3(expansion, leaf_down[0], leaf_down[1])
        yield
        for i in range(4):
            for j in range(pairs):
                ll[4 * j + i] += inherited[32 * j : 32 * j + 32, 256 * i : 256 * i + 256]
        yield

    partner = me + 1 - 2 * core
    swap = pltpu.make_async_remote_copy(
        crossed.at[core], crossed.at[core], swap_sems.at[0], swap_sems.at[1],
        device_id=place(partner), device_id_type=mesh_id,
    )

    def descend():
        count = n // 2
        blank = jnp.zeros((16, 128), jnp.float32)
        offset = 0
        tops = []
        for height in range(cube_levels, levels):
            tops.append(offset)
            ups[offset] = blank
            ups[offset + count + 1] = blank
            if height == cube_levels:

                folds = gath[...].reshape(count, 2, 8, 128)
                even, odd = folds[:, 0], folds[:, 1]
                near_half = lax.broadcasted_iota(jnp.int32, even.shape, 2) < 64
                ups[1 : 1 + count, 0:8] = jnp.where(near_half, even, pltpu.roll(odd, 64, 2))
                ups[1 : 1 + count, 8:16] = jnp.where(near_half, pltpu.roll(even, 64, 2), odd)
            else:
                two = ups[tops[-2] + 1 : tops[-2] + 1 + 2 * count].reshape(count, 2, 16, 128)
                level = dot3(
                    two[:, 0].reshape(count * 16, 128), box_up[0, 0], box_up[1, 0]
                ) + dot3(two[:, 1].reshape(count * 16, 128), box_up[0, 1], box_up[1, 1])
                ups[offset + 1 : offset + 1 + count] = level.reshape(count, 16, 128)
            offset += count + 2
            count //= 2
            yield

        expansion = None
        for height in range(levels - 1, cube_levels - 1, -1):
            j = me >> (height - cube_levels + 1)
            at = tops[height - cube_levels]
            below, above = ups[at + j], ups[at + j + 2]
            here = dot3(below, far[0, height, 0], far[1, height, 0]) + dot3(
                above, far[0, height, 1], far[1, height, 1]
            )
            if expansion is not None:
                parity = lax.rem(j, 2)
                here = here + dot3(expansion, box_down[0, parity], box_down[1, parity])
            expansion = here
            yield
        crossed[core] = expansion
        swap.start()

    def join_halves():
        swap.wait_recv()
        both = jnp.concatenate([crossed[0], crossed[1]], 0)
        wide = lax.broadcasted_iota(jnp.int32, (32, 128), 1) < 64
        turned_round = pltpu.roll(both, 64, 1)
        own = jnp.where(wide == (core == 0), both, turned_round)
        high, low = halves_bf16(own)
        locs[...] = jnp.concatenate([high, low], 1)

    def settle():
        for z in range(layers):
            lhigh, llow = halves_bf16(ll[z])
            both = jnp.concatenate([lhigh, llow], 0)
            parts = []
            for half in range(2):
                cols = slice(half * 128, half * 128 + 128)
                main = jnp.dot(both[:, cols], bd[0, z, half], preferred_element_type=jnp.float32)
                rest = jnp.dot(lhigh[:, cols], bd[1, z, half], preferred_element_type=jnp.float32)
                parts.append(main[0:32] + main[32:64] + rest)
            acc[:, 256 * (z + 1) : 256 * (z + 2)] += jnp.concatenate(parts, 1)
            if z % 2:
                yield

    for copy in copies[5:]:
        copy.wait()
    near_step(jnp.int32(layers - 3), 1)
    take_points()
    near_step(jnp.int32(layers - 2), 0)
    near_squared(jnp.int32(-1), 0, False)
    near_apply(jnp.int32(layers - 2), 0)
    near_kernel(1)
    near_kernel(0, False)
    near_apply(jnp.int32(layers - 1), 1)
    acc[:, 256:512] += plain(mw[0:32, 0:256], whole, slice(256, 512), 0)
    take_leaves()
    everyone = pltpu.make_async_remote_copy(
        gath.at[pl.ds(0, n - 1)], gath.at[pl.ds(0, n - 1)], gsend_sems.at[0], grecv_sems.at[0],
        device_id=place(partner), device_id_type=mesh_id,
    )
    everyone.wait_recv()
    take_boxes()
    parts = [descend(), leaves(), lower()]
    while parts:
        for part in list(parts):
            try:
                next(part)
            except StopIteration:
                parts.remove(part)
    for _ in settle():
        pass
    join_halves()

    def finish(z):
        value = acc[:, span(z + 1)] + jnp.dot(
            locs[:, 0:192],
            jnp.concatenate([b3[:, span(z)], b3[0:64, span(z)]], 0),
            preferred_element_type=jnp.float32,
        )
        out[:, span(z)] = value * occupancy(z)

    def finish_four(part, carry):
        for i in range(4):
            finish(part * 4 + i)
        return carry

    lax.fori_loop(0, layers // 4, finish_four, 0)
    swap.wait_send()
    for pair in (point_edges, leaf_edges, box_edges):
        edges(pair, lambda pair: pair[0].wait_send(), lambda pair: pair[1].wait_send())

    everyone.wait_send()


def local(points, vectors, counts):
    cubes = counts.shape[0]
    nleaf, nsub = lax.axis_size("leaf"), lax.axis_size("sub")
    n = nleaf * nsub
    slab_count = cubes * n
    level_count = slab_count.bit_length() - 2
    cube_levels = cubes.bit_length() - 1
    lengths = term_lengths(slab_count)
    node_values = chebyshev(ORDER)
    leaf_up, leaf_down, box_up, box_down, far = [
        jnp.asarray(np_halves(t)) for t in make_tables(node_values, level_count, lengths)
    ]
    near, pieces = smooth_split(lengths)
    moment_in, moment_out, leaf_far = moment_tables(node_values, near, lengths)
    moment_in, moment_out = [jnp.asarray(np_halves(t)) for t in (moment_in, moment_out)]
    leaf_far = jnp.asarray(leaf_far.astype(np.float32).astype(jnp.bfloat16))
    layers = 2 * cubes
    pairs = cubes // 2
    low_count = sum((pairs >> h) + 2 for h in range(cube_levels))
    top_count = sum((n // 2 >> h) + 2 for h in range(level_count - cube_levels))
    f32, bf16 = jnp.float32, jnp.bfloat16
    tables = (leaf_up, box_up, leaf_down, box_down, far, leaf_far, moment_in, moment_out)
    stay = pl.BlockSpec(memory_space=pltpu.HBM)

    def hold(array):
        return pltpu.with_memory_space_constraint(array, pltpu.HBM)

    return pl.pallas_call(
        functools.partial(kernel_body, (nleaf, nsub, cubes, level_count), lengths, pieces),
        out_shape=jax.ShapeDtypeStruct(vectors.shape, f32),
        in_specs=[stay] * (3 + len(tables)),
        out_specs=pl.BlockSpec(memory_space=pltpu.VMEM),
        scratch_shapes=[
            pltpu.VMEM(points.shape, f32),
            pltpu.VMEM(vectors.shape, f32),
            pltpu.SMEM(counts.shape, jnp.int32),
            pltpu.VMEM((64, (layers + 2) * 256), bf16),
            pltpu.VMEM((8, (layers + 2) * 256), f32),
            pltpu.VMEM((2, layers, 2, 128, 128), bf16),
            pltpu.VMEM((128, layers * 256), bf16),
            pltpu.VMEM((layers + 4, 32, 256), bf16),
            pltpu.VMEM((layers + 4, 32, 256), bf16),
            pltpu.VMEM((2, 256, 512), f32),
            pltpu.VMEM((2, 256, 512), bf16),
            pltpu.VMEM((32, (layers + 2) * 256), f32),
            pltpu.VMEM((2, 208, 128), f32),
            pltpu.VMEM((2, 208, 128), f32),
            pltpu.VMEM((2, 32 * cube_levels, 128), f32),
            pltpu.VMEM((2, 32 * cube_levels, 128), f32),
            pltpu.VMEM((2, 8, 128), f32),
            pltpu.VMEM((n, 8, 128), f32),
            pltpu.VMEM((2, 16, 128), f32),
            pltpu.VMEM((low_count, 32, 128), f32),
            pltpu.VMEM((top_count, 16, 128), f32),
            pltpu.VMEM((32, 256), bf16),
            pltpu.VMEM((layers, 32, 256), f32),
        ] + [pltpu.VMEM(t.shape, bf16) for t in tables] + [
            pltpu.SemaphoreType.DMA((6,)),
            pltpu.SemaphoreType.DMA((6,)),
            pltpu.SemaphoreType.DMA((1,)),
            pltpu.SemaphoreType.DMA((1,)),
            pltpu.SemaphoreType.DMA((2,)),
            pltpu.SemaphoreType.DMA((3 + len(tables),)),

        ],
        compiler_params=pltpu.CompilerParams(
            collective_id=0, has_side_effects=True, vmem_limit_bytes=VMEM_BYTES
        ),
    )(hold(points), hold(vectors), hold(counts), *[hold(t) for t in tables])


def solution(mesh):
    in_specs = (P(None, ("leaf", "sub")), P(None, ("leaf", "sub")), P(("leaf", "sub"), None))
    out_specs = P(None, ("leaf", "sub"))
    return jax.shard_map(local, mesh=mesh, in_specs=in_specs, out_specs=out_specs, check_vma=False)
```

```python
import functools
import math

import jax
import jax.numpy as jnp
import numpy as np
from jax import lax
from jax.experimental import pallas as pl
from jax.experimental.pallas import tpu as pltpu
from jax.sharding import PartitionSpec as P

ORDER = 4
FIRST_DEVICES = 2
VMEM_BYTES = 40 * 1024 * 1024


TERM_SCALE = 1.0 / 32.0
ROOT_THREE = math.sqrt(3.0)
far_offsets = (-3, -2, 2, 3)
far_sources = ((0, (0, 4, 5)), (1, (0, 1, 5)))


def term_lengths(slab_count):
    term_count = (slab_count.bit_length() - 1) // 3 + 1
    return [slab_count / 4.0 / 8.0**term_index for term_index in range(term_count)]


def chebyshev(order):
    return np.cos((2.0 * np.arange(order) + 1.0) * np.pi / (2.0 * order))


def lagrange_table(values, node_values):
    columns = []
    for anchor in range(len(node_values)):
        product = values * 0.0 + 1.0
        for against in range(len(node_values)):
            if against != anchor:
                product = (
                    product
                    * (values - node_values[against])
                    / (node_values[anchor] - node_values[against])
                )
        columns.append(product)
    return np.stack(columns, -1)


def grid_nodes(node_values):
    number = len(node_values)
    along_z, along_y, along_x = np.meshgrid(
        np.arange(number), np.arange(number), np.arange(number), indexing="ij"
    )
    return np.stack(
        [node_values[along_x.ravel()], node_values[along_y.ravel()], node_values[along_z.ravel()]],
        -1,
    )


def kernel_table(targets, sources, lengths):
    offsets_xyz = targets[:, None, :] - sources[None, :, :]
    distance = np.sqrt(np.sum(offsets_xyz * offsets_xyz, -1))
    summed_terms = distance * 0.0
    for length in lengths:
        scaled = distance * (ROOT_THREE / length)
        summed_terms = summed_terms + TERM_SCALE / math.sqrt(length) * (1.0 + scaled) * np.exp(
            -scaled
        )
    return summed_terms


def child_tables(node_values):
    halves = [
        lagrange_table(side_offset + 0.5 * node_values, node_values) for side_offset in (-0.5, 0.5)
    ]
    identity = np.eye(len(node_values))
    octant_rows = []
    for depth_index in range(2):
        for row_index in range(2):
            for column_index in range(2):
                octant_rows.append(
                    np.kron(np.kron(halves[depth_index], halves[row_index]), halves[column_index])
                )
    octant_array = np.stack(octant_rows).reshape((2, 2, 2) + octant_rows[0].shape)
    half_array = np.stack(
        [np.kron(np.kron(halves[half_index], identity), identity) for half_index in range(2)]
    )
    return (octant_array, half_array)


def coarse_couplings(node_values, height, lengths):
    span = float(1 << height)
    targets = grid_nodes(node_values) * np.array([0.5, 0.5, 0.5 * span])
    return np.stack(
        [
            kernel_table(targets, targets + np.array([0.0, 0.0, offset * span]), lengths)
            for offset in far_offsets
        ]
    )


def halves_bf16(value):
    high = value.astype(jnp.bfloat16)
    low = (value - high.astype(jnp.float32)).astype(jnp.bfloat16)
    return high, low


def np_halves(table):
    table = np.asarray(table, np.float32)
    high = table.astype(jnp.bfloat16)
    low = (table - high.astype(np.float32)).astype(jnp.bfloat16)
    return np.stack([high, low])


def dot_split(first, second, high, low):
    return jnp.dot(
        jnp.concatenate([first, second, first], 1), jnp.concatenate([high, high, low], 0),
        preferred_element_type=jnp.float32,
    )


def dot3(value, high, low):
    return dot_split(*halves_bf16(value), high, low)


def smooth_split(lengths):
    r = np.linspace(0.0, math.sqrt(3.0) * 1.0005, 2001)
    s = r * r

    def term(length):
        a = r * (ROOT_THREE / length)
        return TERM_SCALE / math.sqrt(length) * (1.0 + a) * np.exp(-a)

    smooth = sum(term(length) for length in lengths[:-1])
    basis = np.stack([np.ones_like(r), s, s * r, s * s], 1)
    weight = np.ones_like(r)
    for _ in range(100):
        root = np.sqrt(weight)
        fitted = np.linalg.lstsq(basis * root[:, None], smooth * root, rcond=None)[0]
        error = np.abs(smooth - basis @ fitted)
        weight = weight * (error / error.max() + 1e-3)
        weight = weight / weight.mean()
    full = smooth + term(lengths[-1])
    low = basis[:, :2]
    c0, c1 = np.linalg.lstsq(low / full[:, None], np.ones_like(r), rcond=None)[0]
    return (float(c0), float(c1)), [float(v) for v in fitted - np.array([c0, c1, 0.0, 0.0])]


def layer_nodes(node_values):
    nodes = grid_nodes(node_values) * 0.25
    return np.concatenate(
        [nodes + np.array([0.5 * c - 0.25, 0.5 * r - 0.25, 0.0]) for r in range(2) for c in range(2)]
    )


def far_split(node_values, step, lengths):
    nodes = layer_nodes(node_values)
    offsets_xyz = nodes[:, None] - nodes[None] - np.array([0.0, 0.0, 0.5 * step])
    squared = np.sum(offsets_xyz * offsets_xyz, -1).ravel()
    table = kernel_table(nodes, nodes + np.array([0.0, 0.0, 0.5 * step]), lengths).ravel()
    basis = np.stack([np.ones_like(squared), squared], 1)
    c0, c1 = np.linalg.lstsq(basis, table, rcond=None)[0]
    return float(c0), float(c1), (table - basis @ np.array([c0, c1])).reshape(len(nodes), -1)


def moment_tables(node_values, near, lengths):
    x, y, d = layer_nodes(node_values).T
    norm = x * x + y * y + d * d
    one = np.ones_like(x)
    gather = np.zeros((len(x), 128))
    spread = np.zeros((128, len(x)))
    for group, step in enumerate(range(-3, 4)):
        c0, c1 = near if abs(step) < 2 else far_split(node_values, step, lengths)[:2]
        source = (
            c0 + c1 * (norm + step * step / 4.0 + step * d), -2.0 * c1 * x, -2.0 * c1 * y,
            -c1 * (2.0 * d + step), c1 * one,
        )
        for index, (column, row) in enumerate(zip(source, (one, x, y, d, norm))):
            gather[:, 8 * group + index] = column
            spread[8 * group + index] = row
    leaf_far = np.stack(
        [
            np.concatenate(
                [far_split(node_values, layer - 2 - depth, lengths)[2].T for layer in layers]
            )
            for depth, layers in far_sources
        ]
    )
    return gather, spread, leaf_far


def lagrange_coefficients(node_values):
    rows = []
    for anchor in range(len(node_values)):
        others = np.delete(node_values, anchor)
        rows.append(np.poly(others)[::-1] / np.prod(node_values[anchor] - others))
    return np.stack(rows)


def make_tables(node_values, level_count, lengths):
    octants, halves = child_tables(node_values)
    rank = ORDER**3
    eight = octants.reshape(8, rank, rank)
    leaf_up = np.zeros((2, 8, rank, 2, rank))
    for parity in range(2):
        leaf_up[parity, :, :, parity, :] = eight
    leaf_up = leaf_up.reshape(16 * rank, 2 * rank)
    leaf_down = leaf_up.T
    box_up = np.zeros((2, 2, rank, 2, rank))
    for parity in range(2):
        box_up[parity, :, :, parity, :] = halves
    box_up = box_up.reshape(2, 2 * rank, 2 * rank)
    box_down = np.swapaxes(box_up, 1, 2)
    far = np.zeros((level_count, 2, 2, rank, 2, rank))
    for height in range(level_count):
        m3, m2, p2, p3 = [c.T for c in coarse_couplings(node_values, height, lengths)]
        far[height, 0, 0, :, 0] = m2
        far[height, 0, 0, :, 1] = m3
        far[height, 0, 1, :, 1] = m2
        far[height, 1, 0, :, 0] = p2
        far[height, 1, 1, :, 0] = p3
        far[height, 1, 1, :, 1] = p2
    far = far.reshape(level_count, 2, 2 * rank, 2 * rank)
    return leaf_up, leaf_down, box_up, box_down, far


def kernel_body(
    dims, lengths, pieces, pts_hbm, vec_hbm, cnt_hbm, leaf_up_hbm, box_up_hbm, leaf_down_hbm,
    box_down_hbm, far_hbm, leaf_far_hbm, moment_in_hbm, moment_out_hbm,
    out, pts, vec, cnt, mw, pw, bd, b3, lh, ls, r2s, kn, acc, send, recv, send2, recv2, gsend, gath, crossed,
    low_pairs, ups, locs, ll, leaf_up, box_up, leaf_down, box_down, far, leaf_far, moment_in,
    moment_out, send_sems, recv_sems, gsend_sems, grecv_sems, swap_sems, table_sems,
):
    nleaf, nsub, cubes, levels = dims
    n = nleaf * nsub
    layers = 2 * cubes
    cube_levels = cubes.bit_length() - 1
    nodes = chebyshev(ORDER)
    me = lax.axis_index("leaf") * nsub + lax.axis_index("sub")
    mesh_id = pl.DeviceIdType.LOGICAL

    def place(d):
        return d

    copies = [
        pltpu.make_async_copy(source, target, table_sems.at[index])
        for index, (source, target) in enumerate((
            (cnt_hbm, cnt), (pts_hbm, pts), (vec_hbm, vec), (leaf_up_hbm, leaf_up), (box_up_hbm, box_up),
            (moment_in_hbm, moment_in), (moment_out_hbm, moment_out), (leaf_far_hbm, leaf_far),
            (far_hbm, far), (box_down_hbm, box_down), (leaf_down_hbm, leaf_down),
        ))
    ]
    for copy in copies:
        copy.start()

    barrier = pltpu.get_barrier_semaphore()

    def greet(k, carry):
        pl.semaphore_signal(
            barrier, inc=1, device_id=place((me + k) & (n - 1)), device_id_type=mesh_id
        )
        return carry

    lax.fori_loop(1, n, greet, 0)

    first_slab = (me * cubes).astype(jnp.float32)
    lane = lax.broadcasted_iota(jnp.int32, (1, 256), 1)
    quarter = lane // 64
    slot = lane - quarter * 64
    centre_x = ((quarter % 2).astype(jnp.float32) + 0.5) * 0.5
    centre_y = ((quarter // 2).astype(jnp.float32) + 0.5) * 0.5
    row8 = lax.broadcasted_iota(jnp.int32, (8, 512), 0)

    def span(z, width=256):
        return pl.ds(pl.multiple_of(z * 256, 256), width)

    def occupancy(z):
        cube, base = z // 2, lax.rem(z, 2) * 4
        limit = jnp.where(
            quarter < 2,
            jnp.where(quarter == 0, cnt[cube, base], cnt[cube, base + 1]),
            jnp.where(quarter == 2, cnt[cube, base + 2], cnt[cube, base + 3]),
        )
        return jnp.where(slot < limit, 1.0, 0.0)

    table = lagrange_coefficients(nodes)
    row16 = lax.broadcasted_iota(jnp.int32, (16, 128), 0)

    def spread_rows(anchor):
        powers = []
        for power in range(ORDER):
            c = [float(v) for v in table[:, power]]
            one = jnp.where(
                anchor < 2, jnp.where(anchor == 0, c[0], c[1]), jnp.where(anchor == 2, c[2], c[3])
            )
            powers.append(jnp.concatenate([one, one], 1))
        return powers

    along_x = spread_rows(row16 % ORDER)
    along_y = spread_rows(row16 // ORDER)
    along_z = [c[0:8] for c in along_x]

    def poly_of(u, powers):
        p0, p1, p2, p3 = powers
        return ((p3 * u + p2) * u + p1) * u + p0

    def basis_of(ux, uy, uz):
        plane = poly_of(ux, along_x) * poly_of(uy, along_y)
        height = poly_of(uz, along_z)
        return halves_bf16(
            jnp.concatenate([plane * height[a : a + 1] for a in range(ORDER)], 0)
        )

    nt = (((1,), (1,)), ((), ()))
    left64 = lax.broadcasted_iota(jnp.int32, (64, 128), 1) < 64
    nothing = jnp.zeros((64, 128), jnp.bfloat16)

    def box_layer(z, carry):
        masked = vec[:, span(z)] * occupancy(z)
        mw[0:32, span(z + 1)], mw[32:64, span(z + 1)] = halves_bf16(masked)
        coords = pts[:, span(z)]
        pw[0:3, span(z + 1)] = coords
        b3[0:64, span(z)], b3[64:128, span(z)] = basis_of(
            coords[0:1] * 2.0 - 1.0, coords[1:2] * 2.0 - 1.0,
            (coords[2:3] - first_slab) * (2.0 / cubes) - 1.0,
        )
        return carry

    def leaf_layer(z, carry):
        coords = pts[:, span(z)]
        depth = (lax.rem(z, 2).astype(jnp.float32) + 0.5) * 0.5
        slab = first_slab + (z // 2).astype(jnp.float32)
        high, low = basis_of(
            (coords[0:1] - centre_x) * 4.0, (coords[1:2] - centre_y) * 4.0,
            ((coords[2:3] - slab) - depth) * 4.0,
        )
        for half in range(2):
            cols = slice(half * 128, half * 128 + 128)
            for which, part in ((0, high[:, cols]), (1, low[:, cols])):
                bd[which, z, half] = jnp.concatenate(
                    [jnp.where(left64, part, nothing), jnp.where(left64, nothing, part)], 0
                )
        return carry

    def couple():
        edge = [0, 1, layers - 2, layers - 1]
        for index, z in enumerate(edge + list(range(2, layers - 2))):
            for half in range(2):
                cols = slice(half * 128, half * 128 + 128)
                at = slice(256 * (z + 1) + half * 128, 256 * (z + 1) + half * 128 + 128)
                main = lax.dot_general(
                    mw[:, at], bd[0, z, half], nt, preferred_element_type=jnp.float32
                )
                rest = lax.dot_general(
                    mw[0:32, at], bd[1, z, half], nt, preferred_element_type=jnp.float32
                )
                coeffs = main[0:32] + main[32:64] + rest
                if z in edge:
                    side, i = (0, z) if z < 2 else (1, z - layers + 2)
                    start = (2 * i + half) * 32
                    send[side, start : start + 32] = coeffs
                lh[z + 2, :, cols], ls[z + 2, :, cols] = halves_bf16(coeffs)
            if index % 2:
                yield

    for copy in copies[0:3]:
        copy.wait()
    lax.fori_loop(0, layers, box_layer, 0, unroll=4)
    middle = layers * 128
    box = lax.dot_general(
        mw[:, 256 : 256 + middle], b3[:, 0:middle], nt, preferred_element_type=jnp.float32
    ) + lax.dot_general(
        mw[:, 256 + middle : 256 + 2 * middle], b3[:, middle : 2 * middle], nt,
        preferred_element_type=jnp.float32,
    )

    pairs = cubes // 2
    lane128 = lax.broadcasted_iota(jnp.int32, (16, 128), 1)
    offsets = []
    base = 128
    box = box[0:32] + box[32:64]
    box = box + pltpu.roll(box, 64, 1)
    core = lax.rem(me, 2)
    folded = [
        jnp.where(lane128[0:8] < 64, box[16 * k : 16 * k + 8], box[16 * k + 8 : 16 * k + 16])
        for k in range(2)
    ]
    gsend[0] = folded[0]
    gsend[1] = folded[1]
    gath[me] = jnp.where(core == 0, folded[0], folded[1])

    def rise():
        for copy in copies[3:5]:
            copy.wait()
        flat = []
        for part in (lh, ls):
            own = part[2 : 2 + layers].reshape(pairs, 4, 32, 256)
            flat.append(jnp.concatenate([own[:, i].reshape(pairs * 32, 256) for i in range(4)], 1))
        level = dot_split(*flat, leaf_up[0], leaf_up[1]).reshape(pairs, 32, 128)
        yield
        offset = 0
        for height in range(cube_levels):
            offsets.append(offset)
            count = pairs >> height
            low_pairs[offset + 1 : offset + 1 + count] = level
            send2[0, 32 * height : 32 * height + 32] = level[0]
            send2[1, 32 * height : 32 * height + 32] = level[count - 1]
            offset += count + 2
            if count > 1:
                two = level.reshape(count // 2, 2, 32, 128)
                level = dot3(
                    two[:, 0].reshape(count * 16, 128), box_up[0, 0], box_up[1, 0]
                ) + dot3(two[:, 1].reshape(count * 16, 128), box_up[0, 1], box_up[1, 1])
                level = level.reshape(count // 2, 32, 128)
                yield

    for side, edge in ((0, 0), (1, layers - 1)):
        masked = vec[:, edge * 256 : edge * 256 + 256] * occupancy(jnp.int32(edge))
        coords = pts[:, edge * 256 : edge * 256 + 256]
        for half in range(2):
            cols = slice(half * 128, half * 128 + 128)
            send[side, base + 32 * half : base + 32 + 32 * half] = masked[:, cols]
            send[side, base + 64 + 8 * half : base + 67 + 8 * half] = coords[:, cols]
    pad = jnp.zeros((5, 128), jnp.float32)
    for side in range(2):
        for half in range(2):
            send[side, base + 67 + 8 * half : base + 72 + 8 * half] = pad

    def near_squared(z, p, with_self=True):
        boundary = first_slab + (z + 1).astype(jnp.float32) * 0.5
        block = pw[:, span(z + 1, 512)]
        x = block[0:1] - 0.5
        y = block[1:2] - 0.5
        d = block[2:3] - boundary
        norm = x * x + y * y + d * d
        one = jnp.where(row8 == 4, 1.0, 0.0)
        right = jnp.where(row8 == 0, x, jnp.where(row8 == 1, y, jnp.where(row8 == 2, d,
            jnp.where(row8 == 3, norm, one))))
        swap = jnp.where(row8 == 3, 1.0, jnp.where(row8 == 4, norm, 0.0))
        left = jnp.where(row8 < 3, -2.0 * right, swap)[:, 0:256]

        def thirds(v):
            h = v.astype(jnp.bfloat16).astype(jnp.float32)
            m = (v - h).astype(jnp.bfloat16).astype(jnp.float32)
            return h, m, v - h - m

        rh, rm, rl = thirds(right)
        lh, lm, lo = thirds(left)
        if not with_self:
            rh, rm, rl = rh[:, 256:], rm[:, 256:], rl[:, 256:]
        rs = jnp.concatenate([rh, rm, rh, rl, rm, rh], 0).astype(jnp.bfloat16)
        ls = jnp.concatenate([lh, lh, lm, lh, lm, lo], 0).astype(jnp.bfloat16)
        r2s[p, :, (0 if with_self else 256) : 512] = lax.dot_general(
            ls, rs, (((0,), (0,)), ((), ())), preferred_element_type=jnp.float32
        )

    rate = ROOT_THREE / lengths[-1]
    weight = TERM_SCALE / math.sqrt(lengths[-1])
    d0, d1, q0, q1 = pieces

    def near_kernel(p, with_self=True, filler=None, every=4):
        for chunk in range(16):
            if filler is not None and chunk % every == 0:
                next(filler, None)
            rows = slice(chunk * 16, chunk * 16 + 16)
            c0 = (0 if chunk < 8 else 128) if with_self else 256
            sq = jnp.maximum(r2s[p, rows, c0:512], 1e-20)
            r = sq * lax.rsqrt(sq)
            decay = jnp.exp2(r * (-rate * math.log2(math.e)))
            rest = d0 + sq * (d1 + r * (q0 + r * q1))
            kn[p, rows, c0:512] = ((weight + (weight * rate) * r) * decay + rest).astype(jnp.bfloat16)

    first, second, whole = slice(0, 128), slice(128, 256), slice(0, 256)

    def plain(m, rows, cols, p):
        return jnp.dot(m, kn[p, rows, cols], preferred_element_type=jnp.float32)

    def turned(m, rows, cols, p):
        return lax.dot_general(m, kn[p, rows, cols], nt, preferred_element_type=jnp.float32)

    def near_apply(z, p):
        here = mw[0:32, span(z + 1)]
        there = mw[0:32, span(z + 2)]
        own = plain(here[:, first], first, whole, p)
        low = plain(here[:, second], second, second, p)
        high = turned(here[:, second], first, second, p)
        back = turned(there, whole, slice(256, 512), p)
        acc[:, span(z + 1)] += own + jnp.concatenate([high, low], 1) + back
        acc[:, span(z + 2)] = plain(here, whole, slice(256, 512), p)

    def near_step(z, p, filler=None, every=4):
        near_squared(z + 1, 1 - p)
        near_kernel(p, True, filler, every)
        near_apply(z - 1, 1 - p)

    def near_four(t, carry):
        for i in range(4):
            near_step(4 * t + (i + 1), (i + 1) % 2)
        return carry

    @pl.when(me == 0)
    def _():
        recv[0] = jnp.zeros(recv.shape[1:], jnp.float32)
        recv2[0] = jnp.zeros(recv2.shape[1:], jnp.float32)

    @pl.when(me == n - 1)
    def _():
        recv[1] = jnp.zeros(recv.shape[1:], jnp.float32)
        recv2[1] = jnp.zeros(recv2.shape[1:], jnp.float32)

    def sideways(source, target, rows, first_sem):
        to_left = pltpu.make_async_remote_copy(
            source.at[0, rows], target.at[1, rows],
            send_sems.at[first_sem], recv_sems.at[first_sem + 1],
            device_id=place((me + n - 1) & (n - 1)), device_id_type=mesh_id,
        )
        to_right = pltpu.make_async_remote_copy(
            source.at[1, rows], target.at[0, rows],
            send_sems.at[first_sem + 1], recv_sems.at[first_sem],
            device_id=place((me + 1) & (n - 1)), device_id_type=mesh_id,
        )
        return to_left, to_right

    point_edges = sideways(send, recv, pl.ds(base, 80), 0)
    leaf_edges = sideways(send, recv, pl.ds(0, base), 2)
    box_edges = sideways(send2, recv2, pl.ds(0, 32 * cube_levels), 4)

    def wait_edges(pair):
        edges(pair, lambda pair: pair[1].wait_recv(), lambda pair: pair[0].wait_recv())

    def edges(pair, left_action, right_action):
        @pl.when(me > 0)
        def _():
            left_action(pair)

        @pl.when(me < n - 1)
        def _():
            right_action(pair)

    def start_edges(pair):
        edges(pair, lambda pair: pair[0].start(), lambda pair: pair[1].start())

    def spread(k, target):
        return pltpu.make_async_remote_copy(
            gsend.at[target & 1], gath.at[me], gsend_sems.at[0], grecv_sems.at[0],
            device_id=place(target), device_id_type=mesh_id,
        )

    def spread_start(k, carry):
        spread(k, (me + k) & (n - 1)).start()
        return carry

    def first_sends():
        pl.semaphore_wait(barrier, n - 1)
        lax.fori_loop(1, n, spread_start, 0)
        start_edges(point_edges)

    sooner = me < FIRST_DEVICES

    lax.fori_loop(0, layers, leaf_layer, 0, unroll=4)

    @pl.when(jnp.logical_not(sooner))
    def _():
        first_sends()


    acc[:, 256:512] = jnp.zeros((32, 256), jnp.float32)
    late = layers // 4 - 1

    def climb():
        coupling = couple()
        for _ in range(2):
            next(coupling)
            yield

        @pl.when(jnp.logical_not(sooner))
        def _():
            start_edges(leaf_edges)

        yield from coupling
        yield from rise()

    rising = climb()
    near_squared(jnp.int32(0), 0)
    near_squared(jnp.int32(1), 1)
    near_kernel(0, True, rising, 1)
    for _ in rising:
        pass

    @pl.when(jnp.logical_not(sooner))
    def _():
        start_edges(box_edges)

    lax.fori_loop(0, 1, near_four, 0)

    @pl.when(sooner)
    def _():
        first_sends()
        start_edges(leaf_edges)
        start_edges(box_edges)

    lax.fori_loop(1, late, near_four, 0)

    def take_points():
        wait_edges(point_edges)
        for side, window in ((0, 0), (1, layers + 1)):
            for half in range(2):
                cols = slice(window * 256 + half * 128, window * 256 + half * 128 + 128)
                masked = recv[side, base + 32 * half : base + 32 + 32 * half]
                mw[0:32, cols] = masked.astype(jnp.bfloat16)
                pw[:, cols] = recv[side, base + 64 + 8 * half : base + 72 + 8 * half]

    def take_leaves():
        wait_edges(leaf_edges)
        for side in range(2):
            for i in range(2):
                at = i if side == 0 else layers + 2 + i
                for half in range(2):
                    start = (2 * i + half) * 32
                    lanes = slice(half * 128, half * 128 + 128)
                    lh[at, :, lanes], ls[at, :, lanes] = halves_bf16(recv[side, start : start + 32])

    def take_boxes():
        wait_edges(box_edges)
        for side in range(2):
            for height in range(cube_levels):
                at = offsets[height] + (0 if side == 0 else (pairs >> height) + 1)
                low_pairs[at] = recv2[side, 32 * height : 32 * height + 32]

    def leaves():
        rows = (layers + 4) * 32
        moments = dot_split(
            lh[...].reshape(rows, 256), ls[...].reshape(rows, 256), moment_in[0], moment_in[1]
        ).reshape(cubes + 2, 2, 32, 128)
        yield
        window = lh[...].reshape(cubes + 2, 2, 32, 256)
        group = lax.broadcasted_iota(jnp.int32, (cubes, 32, 128), 2) // 8
        for depth, sources in far_sources:
            joined = jnp.zeros((cubes, 32, 128), jnp.float32)
            for s in range(6):
                joined = jnp.where(
                    group == s + 1 - depth, moments[s // 2 : s // 2 + cubes, s % 2], joined
                )
            jh, jl = halves_bf16(joined.reshape(cubes * 32, 128))
            total = jnp.dot(
                jnp.concatenate(
                    [jh, jl, jh]
                    + [window[s // 2 : s // 2 + cubes, s % 2].reshape(cubes * 32, 256) for s in sources],
                    1,
                ),
                jnp.concatenate(
                    [moment_out[0], moment_out[0], moment_out[1], leaf_far[depth]], 0
                ),
                preferred_element_type=jnp.float32,
            )
            for j in range(cubes):
                ll[2 * j + depth] = total[32 * j : 32 * j + 32]
            yield

    def lower():
        expansion = None
        for height in reversed(range(cube_levels)):
            count = pairs >> height
            at = offsets[height]
            below = low_pairs[at : at + count].reshape(count * 32, 128)
            above = low_pairs[at + 2 : at + 2 + count].reshape(count * 32, 128)
            here = dot3(below, far[0, height, 0], far[1, height, 0]) + dot3(
                above, far[0, height, 1], far[1, height, 1]
            )
            if expansion is not None:
                below, above = [
                    dot3(expansion, box_down[0, side], box_down[1, side]).reshape(
                        count // 2, 1, 32, 128
                    )
                    for side in range(2)
                ]
                here = here + jnp.concatenate([below, above], 1).reshape(count * 32, 128)
            expansion = here
            yield
        inherited = dot3(expansion, leaf_down[0], leaf_down[1])
        yield
        for i in range(4):
            for j in range(pairs):
                ll[4 * j + i] += inherited[32 * j : 32 * j + 32, 256 * i : 256 * i + 256]
        yield

    partner = me + 1 - 2 * core
    swap = pltpu.make_async_remote_copy(
        crossed.at[core], crossed.at[core], swap_sems.at[0], swap_sems.at[1],
        device_id=place(partner), device_id_type=mesh_id,
    )

    def descend():
        count = n // 2
        blank = jnp.zeros((16, 128), jnp.float32)
        offset = 0
        tops = []
        for height in range(cube_levels, levels):
            tops.append(offset)
            ups[offset] = blank
            ups[offset + count + 1] = blank
            if height == cube_levels:

                folds = gath[...].reshape(count, 2, 8, 128)
                even, odd = folds[:, 0], folds[:, 1]
                near_half = lax.broadcasted_iota(jnp.int32, even.shape, 2) < 64
                ups[1 : 1 + count, 0:8] = jnp.where(near_half, even, pltpu.roll(odd, 64, 2))
                ups[1 : 1 + count, 8:16] = jnp.where(near_half, pltpu.roll(even, 64, 2), odd)
            else:
                two = ups[tops[-2] + 1 : tops[-2] + 1 + 2 * count].reshape(count, 2, 16, 128)
                level = dot3(
                    two[:, 0].reshape(count * 16, 128), box_up[0, 0], box_up[1, 0]
                ) + dot3(two[:, 1].reshape(count * 16, 128), box_up[0, 1], box_up[1, 1])
                ups[offset + 1 : offset + 1 + count] = level.reshape(count, 16, 128)
            offset += count + 2
            count //= 2
            yield

        expansion = None
        for height in range(levels - 1, cube_levels - 1, -1):
            j = me >> (height - cube_levels + 1)
            at = tops[height - cube_levels]
            below, above = ups[at + j], ups[at + j + 2]
            here = dot3(below, far[0, height, 0], far[1, height, 0]) + dot3(
                above, far[0, height, 1], far[1, height, 1]
            )
            if expansion is not None:
                parity = lax.rem(j, 2)
                here = here + dot3(expansion, box_down[0, parity], box_down[1, parity])
            expansion = here
            yield
        crossed[core] = expansion
        swap.start()

    def join_halves():
        swap.wait_recv()
        both = jnp.concatenate([crossed[0], crossed[1]], 0)
        wide = lax.broadcasted_iota(jnp.int32, (32, 128), 1) < 64
        turned_round = pltpu.roll(both, 64, 1)
        own = jnp.where(wide == (core == 0), both, turned_round)
        high, low = halves_bf16(own)
        locs[...] = jnp.concatenate([high, low], 1)

    def settle():
        for z in range(layers):
            lhigh, llow = halves_bf16(ll[z])
            both = jnp.concatenate([lhigh, llow], 0)
            parts = []
            for half in range(2):
                cols = slice(half * 128, half * 128 + 128)
                main = jnp.dot(both[:, cols], bd[0, z, half], preferred_element_type=jnp.float32)
                rest = jnp.dot(lhigh[:, cols], bd[1, z, half], preferred_element_type=jnp.float32)
                parts.append(main[0:32] + main[32:64] + rest)
            acc[:, 256 * (z + 1) : 256 * (z + 2)] += jnp.concatenate(parts, 1)
            if z % 2:
                yield

    for copy in copies[5:]:
        copy.wait()
    near_step(jnp.int32(layers - 3), 1)
    take_points()
    near_step(jnp.int32(layers - 2), 0)
    near_squared(jnp.int32(-1), 0, False)
    near_apply(jnp.int32(layers - 2), 0)
    near_kernel(1)
    near_kernel(0, False)
    near_apply(jnp.int32(layers - 1), 1)
    acc[:, 256:512] += plain(mw[0:32, 0:256], whole, slice(256, 512), 0)
    take_leaves()
    everyone = pltpu.make_async_remote_copy(
        gath.at[pl.ds(0, n - 1)], gath.at[pl.ds(0, n - 1)], gsend_sems.at[0], grecv_sems.at[0],
        device_id=place(partner), device_id_type=mesh_id,
    )
    everyone.wait_recv()
    take_boxes()
    parts = [descend(), leaves(), lower()]
    while parts:
        for part in list(parts):
            try:
                next(part)
            except StopIteration:
                parts.remove(part)
    for _ in settle():
        pass
    join_halves()

    def finish(z):
        value = acc[:, span(z + 1)] + jnp.dot(
            locs[:, 0:192],
            jnp.concatenate([b3[:, span(z)], b3[0:64, span(z)]], 0),
            preferred_element_type=jnp.float32,
        )
        out[:, span(z)] = value * occupancy(z)

    for z in range(layers):
        finish(z)

    swap.wait_send()
    for pair in (point_edges, leaf_edges, box_edges):
        edges(pair, lambda pair: pair[0].wait_send(), lambda pair: pair[1].wait_send())

    everyone.wait_send()


def local(points, vectors, counts):
    cubes = counts.shape[0]
    nleaf, nsub = lax.axis_size("leaf"), lax.axis_size("sub")
    n = nleaf * nsub
    slab_count = cubes * n
    level_count = slab_count.bit_length() - 2
    cube_levels = cubes.bit_length() - 1
    lengths = term_lengths(slab_count)
    node_values = chebyshev(ORDER)
    leaf_up, leaf_down, box_up, box_down, far = [
        jnp.asarray(np_halves(t)) for t in make_tables(node_values, level_count, lengths)
    ]
    near, pieces = smooth_split(lengths)
    moment_in, moment_out, leaf_far = moment_tables(node_values, near, lengths)
    moment_in, moment_out = [jnp.asarray(np_halves(t)) for t in (moment_in, moment_out)]
    leaf_far = jnp.asarray(leaf_far.astype(np.float32).astype(jnp.bfloat16))
    layers = 2 * cubes
    pairs = cubes // 2
    low_count = sum((pairs >> h) + 2 for h in range(cube_levels))
    top_count = sum((n // 2 >> h) + 2 for h in range(level_count - cube_levels))
    f32, bf16 = jnp.float32, jnp.bfloat16
    tables = (leaf_up, box_up, leaf_down, box_down, far, leaf_far, moment_in, moment_out)
    stay = pl.BlockSpec(memory_space=pltpu.HBM)

    def hold(array):
        return pltpu.with_memory_space_constraint(array, pltpu.HBM)

    return pl.pallas_call(
        functools.partial(kernel_body, (nleaf, nsub, cubes, level_count), lengths, pieces),
        out_shape=jax.ShapeDtypeStruct(vectors.shape, f32),
        in_specs=[stay] * (3 + len(tables)),
        out_specs=pl.BlockSpec(memory_space=pltpu.VMEM),
        scratch_shapes=[
            pltpu.VMEM(points.shape, f32),
            pltpu.VMEM(vectors.shape, f32),
            pltpu.SMEM(counts.shape, jnp.int32),
            pltpu.VMEM((64, (layers + 2) * 256), bf16),
            pltpu.VMEM((8, (layers + 2) * 256), f32),
            pltpu.VMEM((2, layers, 2, 128, 128), bf16),
            pltpu.VMEM((128, layers * 256), bf16),
            pltpu.VMEM((layers + 4, 32, 256), bf16),
            pltpu.VMEM((layers + 4, 32, 256), bf16),
            pltpu.VMEM((2, 256, 512), f32),
            pltpu.VMEM((2, 256, 512), bf16),
            pltpu.VMEM((32, (layers + 2) * 256), f32),
            pltpu.VMEM((2, 208, 128), f32),
            pltpu.VMEM((2, 208, 128), f32),
            pltpu.VMEM((2, 32 * cube_levels, 128), f32),
            pltpu.VMEM((2, 32 * cube_levels, 128), f32),
            pltpu.VMEM((2, 8, 128), f32),
            pltpu.VMEM((n, 8, 128), f32),
            pltpu.VMEM((2, 16, 128), f32),
            pltpu.VMEM((low_count, 32, 128), f32),
            pltpu.VMEM((top_count, 16, 128), f32),
            pltpu.VMEM((32, 256), bf16),
            pltpu.VMEM((layers, 32, 256), f32),
        ] + [pltpu.VMEM(t.shape, bf16) for t in tables] + [
            pltpu.SemaphoreType.DMA((6,)),
            pltpu.SemaphoreType.DMA((6,)),
            pltpu.SemaphoreType.DMA((1,)),
            pltpu.SemaphoreType.DMA((1,)),
            pltpu.SemaphoreType.DMA((2,)),
            pltpu.SemaphoreType.DMA((3 + len(tables),)),

        ],
        compiler_params=pltpu.CompilerParams(
            collective_id=0, has_side_effects=True, vmem_limit_bytes=VMEM_BYTES
        ),
    )(hold(points), hold(vectors), hold(counts), *[hold(t) for t in tables])


def solution(mesh):
    in_specs = (P(None, ("leaf", "sub")), P(None, ("leaf", "sub")), P(("leaf", "sub"), None))
    out_specs = P(None, ("leaf", "sub"))
    return jax.shard_map(local, mesh=mesh, in_specs=in_specs, out_specs=out_specs, check_vma=False)
```
